32 devices in a mesh: dp: 16 (over z, y, x), tensor: 2 (over core).
Axes of the slice: x: 2, y: 2, z: 4, core: 2. Of those that a mesh axis runs over, the one named last changes fastest.
Arguments:
- tokens: bfloat16 [16384, 1024], P('dp', 'tensor'), may hold values from -15 to 15
- cotangent: bfloat16 [16384, 1024], P('dp', 'tensor'), may hold values from -6 to 6
- ln_weight: float32 [1024], replicated, may hold values from 0.25 to 1.75
- up_inner: bfloat16 [1024, 2048], P(None, 'tensor'), may hold values from -0.1875 to 0.1875
- up_gate: bfloat16 [1024, 2048], P(None, 'tensor'), may hold values from -0.1875 to 0.1875
- conv_weight: float32 [4, 2048], P(None, 'tensor'), may hold values from -3 to 3
- conv_bias: float32 [2048], P('tensor'), may hold values from -2 to 2
- query_weight: float32 [512, 4, 4], P('tensor'), may hold values from -3 to 3
- key_weight: float32 [512, 4, 4], P('tensor'), may hold values from -3 to 3
- value_weight: float32 [512, 4, 4], P('tensor'), may hold values from -3 to 3
- gate_weight: bfloat16 [3, 2048, 8], P(None, 'tensor'), may hold values from -0.078125 to 0.078125
- gate_bias: float32 [8], replicated, may hold values from -1 to 9
- group_weight: float32 [2048], P('tensor'), may hold values from 0.25 to 1.75
- skip_weight: float32 [2048], P('tensor'), may hold values from 0.5 to 1.5
- down_weight: bfloat16 [2048, 1024], P('tensor'), may hold values from -0.125 to 0.125
Outputs:
- out: bfloat16 [16384, 1024], P('dp', 'tensor')
- grad_tokens: float32 [16384, 1024], P('dp', 'tensor')
- grad_ln_weight: float32 [1024], P('tensor')
- grad_up_inner: float32 [1024, 2048], P(None, 'tensor')
- grad_up_gate: float32 [1024, 2048], P(None, 'tensor')
- grad_conv_weight: float32 [4, 2048], P(None, 'tensor')
- grad_conv_bias: float32 [2048], P('tensor')
- grad_query_weight: float32 [512, 4, 4], P('tensor')
- grad_key_weight: float32 [512, 4, 4], P('tensor')
- grad_value_weight: float32 [512, 4, 4], P('tensor')
- grad_gate_weight: float32 [3, 2048, 8], P(None, 'tensor')
- grad_gate_bias: float32 [8], replicated
- grad_group_weight: float32 [2048], P('tensor')
- grad_skip_weight: float32 [2048], P('tensor')
- grad_down_weight: float32 [2048, 1024], P('tensor')
- rms: float32 [1], replicated
The draws below stay inside these ranges and needn't reach their ends.
All inputs are finite; a program needn't handle non-finite values.
Results may differ from the reference program's by a relative error of at most 0.023.
The reference program's roundings to bfloat16 on the way count: a program that leaves them out, or rounds other values in their place, can miss the bound.
Values may be sent and summed in bfloat16 or wider, within the bound.
No kernel may reach another device: no remote copies, remote signals or barrier semaphores. Data moves between devices by JAX's collectives and lax.ppermute only.
A program may use at most 448 MiB of HBM per device.

```python
import jax
import jax.numpy as jnp
from jax import lax

D = 1024
INNER = 2048
NH = 4
DH = 512
QB = 4
CONV = 4
BLOCK = 64
SEQ_LEN = 8192
TOK_DEV = 1024
TOKENS = 16384


def draw_tokens(key, part):
    rising = 1.0 + 2.0 * jnp.arange(TOKENS, dtype=jnp.float32) / TOKENS
    base_draw = jnp.clip(jax.random.normal(key, (TOKENS, D), jnp.float32), -5.0, 5.0)
    return (base_draw * rising[:, None]).astype(jnp.bfloat16)


def draw_gate_bias(key, part):
    in_key, forget_key = jax.random.split(jax.random.fold_in(key, 7))
    in_part = jax.random.uniform(in_key, (NH,), jnp.float32, -1.0, 1.0)
    forget_part = jax.random.uniform(forget_key, (NH,), jnp.float32, 2.0, 9.0)
    return jnp.concatenate([in_part, forget_part])


def shard_levels(stream_key, dims, pieces, low, largest):
    factor_of, own = 1.0, jax.random.fold_in(stream_key, 6)
    for dim, shards_of in pieces:
        steps = jnp.exp(jax.random.uniform(jax.random.fold_in(own, dim), (shards_of,), jnp.float32, low / len(pieces), largest / len(pieces)))
        factor_of = factor_of * jnp.repeat(steps, dims[dim] // shards_of).reshape([-1 if axis == dim else 1 for axis in range(len(dims))])
    return factor_of


def noise(key, extent, width, most, shards=(), kind=jnp.bfloat16):
    values = jax.random.normal(key, extent, jnp.float32) * width
    if len(shards) > 0:
        values = shard_levels(key, extent, shards, -0.22, 0.18) * values
    return jnp.clip(values, min=-most, max=most).astype(kind)


def setup_inputs(seed: int = 0) -> dict:
    key_of = jax.random.split(jax.random.key(seed), 16)
    tokens = draw_tokens(jax.random.fold_in(key_of[15], 71), 0)
    cotangent = noise(key_of[1], (TOKENS, D), 1.0, 6.0, ((0, 16), (1, 2)))
    ln_weight = jnp.clip(1.0 + 0.15 * jax.random.normal(key_of[2], (D,), jnp.float32), 0.25, 1.75)
    up_inner = noise(key_of[3], (D, INNER), D ** -0.5, 0.1875, ((1, 2),))
    up_gate = noise(key_of[4], (D, INNER), D ** -0.5, 0.1875, ((1, 2),))
    conv_weight = noise(key_of[5], (CONV, INNER), 0.5, 3.0, ((1, 2),), jnp.float32)
    conv_bias = noise(key_of[6], (INNER,), 0.3, 2.0, ((0, 2),), jnp.float32)
    query_weight = noise(key_of[7], (INNER // QB, QB, QB), QB ** -0.5, 3.0, ((0, 2),), jnp.float32)
    key_weight = noise(key_of[8], (INNER // QB, QB, QB), QB ** -0.5, 3.0, ((0, 2),), jnp.float32)
    value_weight = noise(key_of[9], (INNER // QB, QB, QB), QB ** -0.5, 3.0, ((0, 2),), jnp.float32)
    gate_weight = noise(key_of[10], (3, INNER, 2 * NH), (3 * INNER) ** -0.5, 0.078125, ((1, 2),))
    gate_bias = draw_gate_bias(jax.random.fold_in(key_of[15], 71), 0)
    group_weight = jnp.clip(1.0 + 0.15 * jax.random.normal(key_of[12], (INNER,), jnp.float32), 0.25, 1.75)
    skip_weight = jnp.clip(0.5 + 1.0 * jax.random.uniform(key_of[13], (INNER,), jnp.float32) ** shard_levels(key_of[13], (INNER,), ((0, 2),), -0.2, 0.2), 0.5, 1.5)
    down_weight = noise(key_of[14], (INNER, D), INNER ** -0.5, 0.125, ((0, 2),))
    return dict(tokens=tokens, cotangent=cotangent, ln_weight=ln_weight, up_inner=up_inner, up_gate=up_gate, conv_weight=conv_weight, conv_bias=conv_bias, query_weight=query_weight, key_weight=key_weight, value_weight=value_weight, gate_weight=gate_weight, gate_bias=gate_bias, group_weight=group_weight, skip_weight=skip_weight, down_weight=down_weight)


highest = lax.Precision.HIGHEST
norm_eps = 1e-05
far_below = -1e+30

@jax.custom_vjp
def low(v):
    return lax.optimization_barrier(v.astype(jnp.bfloat16)).astype(jnp.float32)

@jax.custom_vjp
def low_back(v):
    return v

def low_keep(v):
    return (low(v), None)

def low_pass(kept, grad):
    return (grad,)

def back_keep(v):
    return (v, None)

def back_low(kept, grad):
    return (low(grad),)
low.defvjp(low_keep, low_pass)
low_back.defvjp(back_keep, back_low)

def matmul(left, right):
    return jnp.dot(left, right, precision=highest, preferred_element_type=jnp.float32)

def plain_norm(values):
    centered = values - lax.optimization_barrier(jnp.mean(values, axis=-1, keepdims=True))
    return centered * lax.rsqrt(lax.optimization_barrier(jnp.mean(centered * centered, axis=-1, keepdims=True)) + norm_eps)

def headwise(values, weight):
    grouped = values.reshape(values.shape[0], weight.shape[0], weight.shape[1])
    mapped = jnp.einsum('tbi,boi->tbo', grouped, weight, precision=highest)
    return mapped.reshape(values.shape[0], values.shape[1])

def block_step(carried_state, block_data):
    queries, key_vecs, value_vecs, in_pre, forget_pre = block_data
    head_dim = queries.shape[-1]
    key_scale = head_dim ** (-0.5)
    length = queries.shape[0]
    cumulative = jnp.cumsum(jax.nn.log_sigmoid(forget_pre), axis=0)
    last_cum = cumulative[-1]
    causal = lax.broadcasted_iota(jnp.int32, (length, length), 0) >= lax.broadcasted_iota(jnp.int32, (length, length), 1)
    cum_heads = cumulative.T
    exponent = cum_heads[:, :, None] - cum_heads[:, None, :] + in_pre.T[:, None, :]
    damping = jnp.exp(jnp.where(causal[None], exponent, far_below))
    scores = low_back(jnp.einsum('thd,shd->hts', queries, key_vecs, precision=highest))
    weights = scores * damping * key_scale
    inside = low_back(jnp.einsum('hts,shd->thd', low(weights), value_vecs, precision=highest))
    cross_term = low_back(jnp.einsum('thd,hde->the', queries, low(carried_state[:, :head_dim]), precision=highest))
    growth = jnp.exp(cumulative)
    numerator = inside + growth[:, :, None] * cross_term
    normal = lax.optimization_barrier(jnp.sum(weights, axis=2)).T + growth * jnp.einsum('thd,hd->th', queries, carried_state[:, head_dim], precision=highest)
    denominator = jnp.maximum(jnp.abs(normal), 1.0)
    keep_weight = jnp.exp(last_cum[None, :] - cumulative + in_pre) * key_scale
    weighted = low(key_vecs * keep_weight[:, :, None])
    update = low_back(jnp.einsum('shd,she->hde', weighted, value_vecs, precision=highest))
    norm_part = jnp.einsum('sh,shd->hd', keep_weight, key_vecs, precision=highest)
    increment = jnp.concatenate([update, norm_part[:, None, :]], axis=1)
    new_state = jnp.exp(last_cum)[:, None, None] * carried_state + increment
    return (new_state, numerator / denominator[:, :, None])

def forward(seq_tokens, ln_weight, up_inner, up_gate, conv_weight, conv_bias, query_weight, key_weight, value_weight, gate_weight, gate_bias, group_weight, skip_weight, down_weight):
    normed = low(plain_norm(seq_tokens) * ln_weight)
    inner_act = low_back(matmul(normed, up_inner))
    gate_in = low_back(matmul(normed, up_gate))
    padded = jnp.concatenate([jnp.zeros((CONV - 1, INNER), jnp.float32), inner_act], axis=0)
    conv_out = conv_bias
    for tap_pos in range(CONV):
        conv_out = conv_out + conv_weight[tap_pos] * padded[CONV - 1 - tap_pos:CONV - 1 - tap_pos + SEQ_LEN]
    active = jax.nn.silu(conv_out)
    queries = low(headwise(active, query_weight))
    key_vecs = low(headwise(active, key_weight))
    value_vecs = low(headwise(inner_act, value_weight))
    gate_pre = low_back(matmul(queries, gate_weight[0]) + matmul(key_vecs, gate_weight[1]) + matmul(value_vecs, gate_weight[2]) + gate_bias)
    block_count = SEQ_LEN // BLOCK

    def split_heads(array_in):
        return array_in.reshape(block_count, BLOCK, NH, DH)
    in_pre = gate_pre[:, :NH].reshape(block_count, BLOCK, NH)
    forget_pre = gate_pre[:, NH:].reshape(block_count, BLOCK, NH)
    start_state = jnp.zeros((NH, DH + 1, DH), jnp.float32)
    _, mixed = lax.scan(jax.checkpoint(block_step), start_state, (split_heads(queries), split_heads(key_vecs), split_heads(value_vecs), in_pre, forget_pre))
    group_hat = plain_norm(mixed.reshape(SEQ_LEN, NH, DH)).reshape(SEQ_LEN, INNER)
    gated_state = group_hat * group_weight + skip_weight * active
    gated = low(gated_state * jax.nn.silu(gate_in))
    branch = matmul(gated, down_weight)
    return (seq_tokens + branch, branch)

def reference(tokens, cotangent, ln_weight, up_inner, up_gate, conv_weight, conv_bias, query_weight, key_weight, value_weight, gate_weight, gate_bias, group_weight, skip_weight, down_weight):
    params = tuple((array_in.astype(jnp.float32) for array_in in (ln_weight, up_inner, up_gate, conv_weight, conv_bias, query_weight, key_weight, value_weight, gate_weight, gate_bias, group_weight, skip_weight, down_weight)))
    seq_count = TOKENS // SEQ_LEN
    seq_span = SEQ_LEN // TOK_DEV

    def to_seqs(array_in):
        return array_in.reshape(seq_span, seq_count, TOK_DEV, D).transpose(1, 0, 2, 3).reshape(seq_count, SEQ_LEN, D)

    def from_seqs(array_in):
        return array_in.reshape(seq_count, seq_span, TOK_DEV, D).transpose(1, 0, 2, 3).reshape(TOKENS, D)
    token_seqs = to_seqs(tokens.astype(jnp.float32))
    cot_seqs = to_seqs(cotangent.astype(jnp.float32))

    def one_sequence(totals, seq_item):
        seq_tokens, seq_cot = seq_item
        result, pullback, branch = jax.vjp(forward, seq_tokens, *params, has_aux=True)
        gradients = pullback(seq_cot)
        totals = tuple((running + new_grad for running, new_grad in zip(totals, gradients[1:])))
        return (totals, (result, gradients[0], jnp.sum(result * result)))
    start_totals = tuple((jnp.zeros_like(array_in) for array_in in params))
    totals, (results, token_grads, result_squares) = lax.scan(one_sequence, start_totals, (token_seqs, cot_seqs))
    rms_single = jnp.sqrt(jnp.sum(result_squares) / (TOKENS * D))[None]
    return (from_seqs(results).astype(jnp.bfloat16), from_seqs(token_grads)) + totals + (rms_single,)
```

```python
import jax
import jax.numpy as jnp
from jax import lax
from jax.experimental import pallas as pl
from jax.experimental.pallas import tpu as pltpu
from jax.sharding import PartitionSpec as P

DH = 512
BLOCK = 64
QB = 4
SEQ_LEN = 8192
TILE = 256
GROUP = 256
HALO = 16
LANES = 128
NORM_EPS = 1e-05
PACK = DH + 16
WIDE = DH + 8
SMALL = 56

f32 = jnp.float32
bf16 = jnp.bfloat16
highest = lax.Precision.HIGHEST


def mm(left, right):
    return lax.dot_general(left, right, (((1,), (0,)), ((), ())), preferred_element_type=f32)


def mm_tn(left, right):
    return lax.dot_general(left, right, (((0,), (0,)), ((), ())), preferred_element_type=f32)


def mm_nt(left, right):
    return lax.dot_general(left, right, (((1,), (1,)), ((), ())), preferred_element_type=f32)


def split2(value):
    high = value.astype(bf16)
    return high, (value - high.astype(f32)).astype(bf16)


def split3(value):
    high = value.astype(bf16)
    rest = value - high.astype(f32)
    mid = rest.astype(bf16)
    return high, mid, (rest - mid.astype(f32)).astype(bf16)


def sigmoid(value):
    return 1.0 / (1.0 + jnp.exp(-value))


def params(vmem_mib):
    return pltpu.CompilerParams(
        dimension_semantics=("arbitrary",), vmem_limit_bytes=vmem_mib * 1024 * 1024
    )


def cost(flops, moved):
    return pl.CostEstimate(flops=flops, bytes_accessed=moved, transcendentals=0)


def rows(width, tile=TILE, flip=0):
    if flip:
        return pl.BlockSpec((tile, width), lambda i: (flip - 1 - i, 0))
    return pl.BlockSpec((tile, width), lambda i: (i, 0))


def whole(*shape):
    return pl.BlockSpec(shape, lambda i: (0,) * len(shape))


smem = pl.BlockSpec(memory_space=pltpu.MemorySpace.SMEM)


def shape_of(*dims, dtype=f32):
    return jax.ShapeDtypeStruct(dims, dtype)


def normed_rows(x, ln):
    centered = x - jnp.mean(x, axis=1, keepdims=True)
    inverse = lax.rsqrt(jnp.mean(centered * centered, axis=1, keepdims=True) + NORM_EPS)
    return (centered * inverse * ln).astype(bf16)


def band_sum(value, coefs, reach):
    sums = [coef[reach : reach + 1] * value for coef in coefs]
    for offset in range(-reach, reach + 1):
        if offset != 0:
            moved = pltpu.roll(value, -offset % value.shape[1], 1)
            sums = [
                total + coef[reach + offset : reach + offset + 1] * moved for total, coef in zip(sums, coefs)
            ]
    return sums


def first_kernel(
    flag, x_ref, halo_ref, ln_ref, up_ref, cw_ref, cb_ref, coef_ref, gw_ref,
    normed_ref, inner_ref, conv_ref, active_ref, q_ref, k_ref, v_ref, pre_ref, pad_ref,
):
    step = pl.program_id(0)
    tile = x_ref.shape[0]

    @pl.when(step == 0)
    def _():
        before = mm(normed_rows(halo_ref[...].astype(f32), ln_ref[...]), up_ref[...])
        pad_ref[0:8, :] = jnp.where(flag[0] == 1, 0.0, before[HALO - 8 :, :])

    normed = normed_rows(x_ref[...].astype(f32), ln_ref[...])
    normed_ref[...] = normed
    inner = mm(normed, up_ref[...])
    inner_ref[...] = inner
    pad_ref[8:, :] = inner
    conv = cb_ref[...] + cw_ref[0:1, :] * inner
    for j in range(1, cw_ref.shape[0]):
        conv = conv + cw_ref[j : j + 1, :] * pad_ref[8 - j : 8 - j + tile, :]
    conv_ref[...] = conv
    pad_ref[0:8, :] = pad_ref[tile : tile + 8, :]
    active_ref[...] = conv * sigmoid(conv)
    reach = QB - 1
    for g in range(inner.shape[1] // LANES):
        part = slice(g * LANES, (g + 1) * LANES)
        query, key = band_sum(active_ref[:, part], (coef_ref[0, :, part], coef_ref[1, :, part]), reach)
        q_ref[:, part] = query.astype(bf16)
        k_ref[:, part] = key.astype(bf16)
        v_ref[:, part] = band_sum(inner_ref[:, part], (coef_ref[2, :, part],), reach)[0].astype(bf16)
    pre = mm(q_ref[...], gw_ref[0]) + mm(k_ref[...], gw_ref[1]) + mm(v_ref[...], gw_ref[2])
    pre_ref[...] = jnp.transpose(pre)[0:8, :]


def first_stage(flag, full, halo, ln, up, cw, cb, coefs, gw):
    count, width = full.shape
    chan = up.shape[1]
    wide = (count, chan)
    return pl.pallas_call(
        first_kernel,
        grid=(count // TILE,),
        in_specs=[
            smem, rows(width), whole(*halo.shape), whole(*ln.shape), whole(*up.shape), whole(*cw.shape),
            whole(*cb.shape), whole(*coefs.shape), whole(*gw.shape),
        ],
        out_specs=[rows(width), rows(chan), rows(chan), rows(chan), rows(chan), rows(chan), rows(chan),
                   pl.BlockSpec((8, TILE), lambda i: (0, i))],
        out_shape=[shape_of(count, width, dtype=bf16), shape_of(*wide), shape_of(*wide), shape_of(*wide),
                   shape_of(*wide, dtype=bf16), shape_of(*wide, dtype=bf16), shape_of(*wide, dtype=bf16),
                   shape_of(8, count)],
        scratch_shapes=[pltpu.VMEM((TILE + 8, chan), f32)],
        compiler_params=params(48),
        cost_estimate=cost(2 * count * width * chan * 4, count * chan * 20),
        name="first",
    )(flag, full, halo, ln, up, cw, cb, coefs, gw)


def gates_kernel(place, own_ref, other_ref, bias_ref, row_ref, col_ref, total_ref):
    count = own_ref.shape[1]
    pre = own_ref[...] + other_ref[...] + bias_ref[...]
    low_half = place[0] == 0
    in_pre = jnp.where(low_half, pre[0:2], pre[2:4])
    forget = jnp.where(low_half, pre[4:6], pre[6:8])
    both = jnp.concatenate([in_pre, forget, in_pre, forget], axis=0)
    in8 = jnp.concatenate([in_pre] * 4, axis=0)
    f8 = jnp.concatenate([forget] * 4, axis=0)
    log_keep = jnp.minimum(f8, 0.0) - jnp.log1p(jnp.exp(-jnp.abs(f8)))
    lane = lax.broadcasted_iota(jnp.int32, f8.shape, 1)
    place_in = lane % BLOCK
    cum = log_keep
    dist = 1
    while dist < BLOCK:
        cum = cum + jnp.where(place_in >= dist, pltpu.roll(cum, dist, 1), 0.0)
        dist *= 2
    last = jnp.where(place_in == BLOCK - 1, cum, 0.0)
    dist = 1
    while dist < BLOCK:
        last = last + jnp.where(place_in < BLOCK - dist, pltpu.roll(last, count - dist, 1), 0.0)
        dist *= 2
    before = jnp.where(lane >= BLOCK, pltpu.roll(last, BLOCK, 1), 0.0)
    after = jnp.where(lane < count - BLOCK, pltpu.roll(last, count - BLOCK, 1), 0.0)
    dist = BLOCK
    while dist < count:
        before = before + jnp.where(lane >= dist, pltpu.roll(before, dist, 1), 0.0)
        after = after + jnp.where(lane < count - dist, pltpu.roll(after, count - dist, 1), 0.0)
        dist *= 2
    scale = DH ** (-0.5)
    keep = jnp.exp(last - cum + in8) * scale
    table = jnp.concatenate(
        [
            cum[0:2], jnp.exp(cum[0:2]), keep[0:2], jnp.exp(after[0:2]),
            jnp.exp(before[0:2]), jnp.exp(last[0:2]), in8[0:2], 1.0 / (1.0 + jnp.exp(f8[0:2])),
        ],
        axis=0,
    )
    tall = jnp.concatenate([table, jnp.zeros((LANES - 16, count), f32)], axis=0)
    col_ref[...] = jnp.transpose(tall)
    small = jnp.concatenate([cum[0:2], in8[0:2], cum[0:2], in8[0:2]], axis=0)
    for b in range(count // BLOCK):
        row_ref[b] = small[:, b * BLOCK : (b + 1) * BLOCK]
    total = (before + last)[:, count - 1 : count]
    total_ref[...] = jnp.broadcast_to(total, total_ref.shape)


def gates_stage(place, own, other, bias):
    count = own.shape[1]
    return pl.pallas_call(
        gates_kernel,
        grid=(1,),
        in_specs=[smem, whole(8, count), whole(8, count), whole(8, 1)],
        out_specs=[whole(count // BLOCK, 8, BLOCK), whole(count, LANES), whole(8, DH)],
        out_shape=[shape_of(count // BLOCK, 8, BLOCK), shape_of(count, LANES), shape_of(8, DH)],
        compiler_params=params(24),
        cost_estimate=cost(count * 1000, count * 600),
        name="gates",
    )(place, own, other, bias)


def write_pack(ref, state, vector, log_decay):
    ref[0:DH, :] = state.astype(bf16)
    terms = split3(vector) + split3(log_decay)
    tail = jnp.concatenate(
        [t.astype(f32) for t in terms] + [jnp.zeros((PACK - DH - 6, DH), f32)], axis=0
    )
    ref[DH:PACK, :] = tail.astype(bf16)


def write_wide(ref, state, vector, log_decay):
    ref[0:DH, :] = state
    ref[DH:WIDE, :] = jnp.concatenate([vector, log_decay, jnp.zeros((WIDE - DH - 2, DH), f32)], axis=0)


def read_pack(ref):
    tail = ref[DH:PACK, :].astype(f32)
    return (
        ref[0:DH, :].astype(f32), (tail[0:1] + tail[1:2]) + tail[2:3], (tail[3:4] + tail[4:5]) + tail[5:6]
    )


def read_wide(ref):
    return ref[0:DH, :], ref[DH : DH + 1, :], ref[DH + 1 : DH + 2, :]


def joined(first, second):
    decay = jnp.exp(second[2])
    return decay * first[0] + second[0], decay * first[1] + second[1], first[2] + second[2]


def chosen(which, yes, no):
    return tuple(jnp.where(which, a, b) for a, b in zip(yes, no))


def pair_kernel(flag, own_ref, got_ref, send_ref, total_ref, lead_ref):
    own, got = read_wide(own_ref), read_pack(got_ref)
    is_lead = flag[0] == 1
    lead = chosen(is_lead, own, got)
    total = joined(lead, chosen(is_lead, got, own))
    write_wide(lead_ref, *lead)
    write_wide(total_ref, *total)
    write_pack(send_ref, *total)


def step_kernel(flag, total_ref, got_ref, before_ref, send_ref, new_total_ref, new_before_ref):
    total, got, before = read_wide(total_ref), read_pack(got_ref), read_wide(before_ref)
    upper = flag[0] == 1
    both = joined(chosen(upper, got, total), chosen(upper, total, got))
    write_wide(new_total_ref, *both)
    write_pack(send_ref, *both)
    write_wide(new_before_ref, *chosen(upper, joined(got, before), before))


def last_kernel(flag, got_ref, before_ref, lead_ref, send_ref, mine_ref):
    before, got = read_wide(before_ref), read_pack(got_ref)
    upper = flag[0] == 1
    is_lead = flag[1] == 1
    found = chosen(upper, joined(got, before), before)
    after = joined(found, read_wide(lead_ref))
    write_pack(send_ref, *chosen(is_lead, after, found))
    write_wide(mine_ref, *chosen(is_lead, found, after))


def pack_spec(wide):
    return whole(WIDE if wide else PACK, DH)


def pack_shape(wide):
    return shape_of(WIDE if wide else PACK, DH, dtype=f32 if wide else bf16)


def small_call(kernel, name, ins, outs, flag, *packs):
    return pl.pallas_call(
        kernel,
        grid=(1,),
        in_specs=[smem] + [pack_spec(w) for w in ins],
        out_specs=[pack_spec(w) for w in outs],
        out_shape=[pack_shape(w) for w in outs],
        compiler_params=params(24),
        cost_estimate=cost(PACK * DH * 8, PACK * DH * 3 * (len(ins) + len(outs))),
        name=name,
    )(flag, *packs)


def pass_states(own, send, place, span, stride):
    devices = lax.axis_size("dp")

    def swap(value, bit):
        route = [((i // stride ^ bit) * stride + i % stride, i) for i in range(devices)]
        return lax.ppermute(value, "dp", route)

    def as_flag(*values):
        return jnp.stack([jnp.asarray(v).astype(jnp.int32) for v in values])

    is_lead = place % 2 == 0
    got = swap(send, 1)
    out, total, lead = small_call(pair_kernel, "pair", (1, 0), (0, 1, 1), as_flag(is_lead), own, got)
    before = jnp.zeros_like(own)
    bit = 2
    while bit < span:
        got = swap(out, bit)
        upper = (place // bit) % 2 == 1
        if bit * 2 < span:
            out, total, before = small_call(
                step_kernel, "step", (1, 0, 1), (0, 1, 1), as_flag(upper), total, got, before
            )
        bit *= 2
    out, mine = small_call(last_kernel, "last", (0, 1, 1), (0, 1), as_flag(upper, is_lead), got, before, lead)
    return mine, swap(out, 1)


def put_states(flag, mine_ref, came_ref, state_ref, vec_ref):
    mine, came = read_wide(mine_ref), read_pack(came_ref)
    for h in range(2):
        found = chosen((flag[0] == 1) == (h == 0), mine, came)
        state_ref[h] = found[0]
        vec_ref[h : h + 1, :] = found[1]


def ends_kernel(flag, k_ref, v_ref, col_ref, total_ref, own_ref, send_ref, state_ref, vec_ref):
    step = pl.program_id(0)

    @pl.when(step == 0)
    def _():
        state_ref[...] = jnp.zeros_like(state_ref)
        vec_ref[...] = jnp.zeros_like(vec_ref)

    col = col_ref[...]
    for h in range(2):
        part = slice(h * DH, (h + 1) * DH)
        wide = k_ref[:, part].astype(f32)
        keep = col[:, 4 + h : 5 + h]
        later = col[:, 6 + h : 7 + h]
        kept = wide * keep
        high, low = split2(kept.astype(bf16).astype(f32) * later)
        value = v_ref[:, part]
        state_ref[h] += mm_tn(high, value) + mm_tn(low, value)
        vec_ref[h : h + 1, :] += jnp.sum(kept * later, axis=0, keepdims=True)

    @pl.when(step == pl.num_programs(0) - 1)
    def _():
        write_two(flag, state_ref, vec_ref, total_ref, own_ref, send_ref)


def write_two(flag, state_ref, vec_ref, total_ref, own_ref, send_ref):
    for h in range(2):
        found = (state_ref[h], vec_ref[h : h + 1, :], total_ref[h : h + 1, :])

        @pl.when(flag[0] == 1 - h)
        def _():
            write_wide(own_ref, *found)

        @pl.when(flag[0] == h)
        def _():
            write_pack(send_ref, *found)


def ends_stage(flag, k, v, col, total):
    count, chan = k.shape
    return pl.pallas_call(
        ends_kernel,
        grid=(count // TILE,),
        in_specs=[smem, rows(chan), rows(chan), rows(LANES), whole(8, DH)],
        out_specs=[pack_spec(1), pack_spec(0)],
        out_shape=[pack_shape(1), pack_shape(0)],
        scratch_shapes=[pltpu.VMEM((2, DH, DH), f32), pltpu.VMEM((8, DH), f32)],
        compiler_params=params(32),
        cost_estimate=cost(4 * count * chan * DH, count * chan * 4),
        name="ends",
    )(flag, k, v, col, total)


def damping_of(col, row, h):
    t = lax.broadcasted_iota(jnp.int32, (BLOCK, BLOCK), 0)
    s = lax.broadcasted_iota(jnp.int32, (BLOCK, BLOCK), 1)
    expo = col[:, h : h + 1] - row[h : h + 1, :] + row[2 + h : 3 + h, :]
    return jnp.exp(jnp.where(t >= s, expo, -1e30))


def lanes_of(*columns):
    lane = lax.broadcasted_iota(jnp.int32, (columns[0].shape[0], LANES), 1)
    out = jnp.zeros(lane.shape, f32)
    for i, column in enumerate(columns):
        out = jnp.where(lane == i, column, out)
    return out


def inside_kernel(q_ref, k_ref, v_ref, col_ref, row_ref, inside_ref, norm_ref):
    scale = DH ** (-0.5)

    def body(b, carry):
        r0 = pl.multiple_of(b * BLOCK, BLOCK)
        here = pl.ds(r0, BLOCK)
        col = col_ref[here, :]
        row = row_ref[b]
        sums = []
        for h in range(2):
            part = slice(h * DH, (h + 1) * DH)
            scores = mm_nt(q_ref[here, part], k_ref[here, part])
            weights = scores * damping_of(col, row, h) * scale
            inside_ref[here, part] = mm(weights.astype(bf16), v_ref[here, part])
            sums.append(jnp.sum(weights, axis=1, keepdims=True))
        norm_ref[here, :] = lanes_of(*sums)
        return carry

    lax.fori_loop(0, q_ref.shape[0] // BLOCK, body, 0)


def inside_stage(q, k, v, col, row):
    count, chan = q.shape
    return pl.pallas_call(
        inside_kernel,
        grid=(count // TILE,),
        in_specs=[rows(chan), rows(chan), rows(chan), rows(LANES),
                  pl.BlockSpec((TILE // BLOCK, 8, BLOCK), lambda i: (i, 0, 0))],
        out_specs=[rows(chan), rows(LANES)],
        out_shape=[shape_of(count, chan), shape_of(count, LANES)],
        compiler_params=params(32),
        cost_estimate=cost(4 * count * chan * BLOCK, count * chan * 10),
        name="inside",
    )(q, k, v, col, row)


def middle_kernel(
    flag, mine_ref, came_ref, q_ref, k_ref, v_ref, inside_ref, norm_ref, col_ref, gate_ref, dgated_ref,
    active_ref, group_ref, skip_ref, total_ref,
    gated_ref, gig_ref, sgrad_ref, nlow_ref, clow_ref, start_ref, nvec_ref, stat_ref, ggroup_ref, gskip_ref,
    own_ref, send_ref,
    state_ref, vec_ref, back_ref, bvec_ref,
):
    step = pl.program_id(0)

    @pl.when(step == 0)
    def _():
        put_states(flag, mine_ref, came_ref, state_ref, vec_ref)
        back_ref[...] = jnp.zeros_like(back_ref)
        bvec_ref[...] = jnp.zeros_like(bvec_ref)
        ggroup_ref[...] = jnp.zeros_like(ggroup_ref)
        gskip_ref[...] = jnp.zeros_like(gskip_ref)

    def body(b, carry):
        r0 = pl.multiple_of(b * BLOCK, BLOCK)
        here = pl.ds(r0, BLOCK)
        col = col_ref[here, :]
        norms = norm_ref[here, :]
        nvec_ref[b] = vec_ref[...]
        stats = []
        for h in range(2):
            part = slice(h * DH, (h + 1) * DH)
            query = q_ref[here, part]
            state = state_ref[h]
            state_low = state.astype(bf16)
            start_ref[h, b] = state_low
            growth = col[:, 2 + h : 3 + h]
            carried = growth * mm(query, state_low)
            vec = vec_ref[h : h + 1, :]
            norm_cross = growth * jnp.sum(query.astype(f32) * vec, axis=1, keepdims=True)
            numer = inside_ref[here, part] + carried
            normal = norms[:, h : h + 1] + norm_cross
            over = 1.0 / jnp.maximum(jnp.abs(normal), 1.0)
            mixed = numer * over
            centered = mixed - jnp.mean(mixed, axis=1, keepdims=True)
            inverse = lax.rsqrt(jnp.mean(centered * centered, axis=1, keepdims=True) + NORM_EPS)
            ghat = centered * inverse
            active = active_ref[here, part]
            gate = gate_ref[here, part]
            sig = sigmoid(gate)
            gact = gate * sig
            gweight = group_ref[0:1, part]
            gstate = ghat * gweight + skip_ref[0:1, part] * active
            gated_ref[here, part] = (gstate * gact).astype(bf16)
            dgated = dgated_ref[here, part]
            sgrad = dgated * gact
            sgrad_ref[here, part] = sgrad
            gig_ref[here, part] = (dgated * gstate * sig * (1.0 + gate * (1.0 - sig))).astype(bf16)
            gskip_ref[0:1, part] += jnp.sum(sgrad * active, axis=0, keepdims=True)
            ggroup_ref[0:1, part] += jnp.sum(sgrad * ghat, axis=0, keepdims=True)
            g = sgrad * gweight
            mgrad = inverse * (
                g - jnp.mean(g, axis=1, keepdims=True) - ghat * jnp.mean(g * ghat, axis=1, keepdims=True)
            )
            ngrad = mgrad * over
            down = -jnp.sum(mgrad * mixed, axis=1, keepdims=True) * over
            normal_grad = jnp.where(normal > 1.0, down, jnp.where(normal < -1.0, -down, 0.0))
            nlow_ref[here, part] = ngrad.astype(bf16)
            clow_ref[here, part] = (growth * ngrad).astype(bf16)
            moved = jnp.sum(ngrad * carried, axis=1, keepdims=True) + normal_grad * norm_cross
            stats.append((normal_grad, moved))
            wide = k_ref[here, part].astype(f32)
            kept = wide * col[:, 4 + h : 5 + h]
            decay = col[0:1, 10 + h : 11 + h]
            state_ref[h] = decay * state + mm_tn(kept.astype(bf16), v_ref[here, part])
            vec_ref[h : h + 1, :] = decay * vec + jnp.sum(kept, axis=0, keepdims=True)
            scaled = col[:, 8 + h : 9 + h] * growth * normal_grad
            bvec_ref[h : h + 1, :] += jnp.sum(scaled * query.astype(f32), axis=0, keepdims=True)
        stat_ref[here, :] = lanes_of(stats[0][0], stats[1][0], stats[0][1], stats[1][1])
        return carry

    lax.fori_loop(0, q_ref.shape[0] // BLOCK, body, 0)
    for h in range(2):
        part = slice(h * DH, (h + 1) * DH)
        high, low = split2(clow_ref[:, part].astype(f32) * col_ref[:, 8 + h : 9 + h])
        query = q_ref[:, part]
        back_ref[h] += mm_tn(query, high) + mm_tn(query, low)

    @pl.when(step == pl.num_programs(0) - 1)
    def _():
        write_two(flag, back_ref, bvec_ref, total_ref, own_ref, send_ref)


def middle_stage(flag, mine, came, q, k, v, inside, norms, col, gate, dgated, active, group, skip, total):
    count, chan = q.shape
    blocks = count // BLOCK
    per = TILE // BLOCK
    return pl.pallas_call(
        middle_kernel,
        grid=(count // TILE,),
        in_specs=[smem, pack_spec(1), pack_spec(0), rows(chan), rows(chan), rows(chan), rows(chan), rows(LANES), rows(LANES),
                  rows(chan), rows(chan), rows(chan), whole(1, chan), whole(1, chan), whole(8, DH)],
        out_specs=[rows(chan), rows(chan), rows(chan), rows(chan), rows(chan),
                   pl.BlockSpec((2, per, DH, DH), lambda i: (0, i, 0, 0)),
                   pl.BlockSpec((per, 8, DH), lambda i: (i, 0, 0)),
                   rows(LANES), whole(8, chan), whole(8, chan), pack_spec(1), pack_spec(0)],
        out_shape=[shape_of(count, chan, dtype=bf16), shape_of(count, chan, dtype=bf16), shape_of(count, chan),
                   shape_of(count, chan, dtype=bf16), shape_of(count, chan, dtype=bf16),
                   shape_of(2, blocks, DH, DH, dtype=bf16), shape_of(blocks, 8, DH), shape_of(count, LANES),
                   shape_of(8, chan), shape_of(8, chan),
                   pack_shape(1), pack_shape(0)],
        scratch_shapes=[pltpu.VMEM((2, DH, DH), f32), pltpu.VMEM((8, DH), f32),
                        pltpu.VMEM((2, DH, DH), f32), pltpu.VMEM((8, DH), f32)],
        compiler_params=params(56),
        cost_estimate=cost(10 * count * chan * DH, count * chan * 40),
        name="middle",
    )(flag, mine, came, q, k, v, inside, norms, col, gate, dgated, active, group, skip, total)


def back_kernel(
    flag, mine_ref, came_ref, q_ref, k_ref, v_ref, nlow_ref, clow_ref, start_ref, nvec_ref, col_ref, row_ref,
    stat_ref,
    qg_ref, kg_ref, vg_ref, pre_ref,
    state_ref, vec_ref,
):
    scale = DH ** (-0.5)

    @pl.when(pl.program_id(0) == 0)
    def _():
        put_states(flag, mine_ref, came_ref, state_ref, vec_ref)

    u = lax.broadcasted_iota(jnp.int32, (BLOCK, BLOCK), 0)
    t = lax.broadcasted_iota(jnp.int32, (BLOCK, BLOCK), 1)
    from_here = jnp.where(t >= u, 1.0, 0.0)
    at_end = lax.broadcasted_iota(jnp.int32, (BLOCK, 1), 0) == BLOCK - 1
    per = q_ref.shape[0] // BLOCK

    def body(i, carry):
        b = per - 1 - i
        r0 = pl.multiple_of(b * BLOCK, BLOCK)
        here = pl.ds(r0, BLOCK)
        col = col_ref[here, :]
        row = row_ref[b]
        stat = stat_ref[here, :]
        starts = nvec_ref[b]
        in_cols, cum_cols = [], []
        for h in range(2):
            part = slice(h * DH, (h + 1) * DH)
            query, key, value = q_ref[here, part], k_ref[here, part], v_ref[here, part]
            numer_low, cross_low = nlow_ref[here, part], clow_ref[here, part]
            growth = col[:, 2 + h : 3 + h]
            keep = col[:, 4 + h : 5 + h]
            decay = col[0:1, 10 + h : 11 + h]
            normal_grad = stat[:, h : h + 1]
            moved = stat[:, 2 + h : 3 + h]
            end = state_ref[h]
            end_low = end.astype(bf16)
            end_vec = vec_ref[h : h + 1, :]
            start_low = start_ref[h, b]
            start_vec = starts[h : h + 1, :]
            damping = damping_of(col, row, h)
            scores = mm_nt(query, key)
            weights_low = (scores * damping * scale).astype(bf16)
            weights_grad = mm_nt(numer_low, value) + normal_grad
            damped = weights_grad * scale * damping
            scores_low = damped.astype(bf16)
            expo = damped * scores
            pull = growth * normal_grad
            qg_ref[here, part] = mm(scores_low, key) + mm_nt(cross_low, start_low) + pull * start_vec
            wide = key.astype(f32)
            kept_low = (wide * keep).astype(bf16)
            key_total = mm_nt(value, end_low) + end_vec
            kg_ref[here, part] = mm_tn(scores_low, query) + keep * key_total
            vg_ref[here, part] = mm_tn(weights_low, numer_low) + mm(kept_low, end_low)
            keep_grad = keep * jnp.sum(wide * key_total, axis=1, keepdims=True)
            held = jnp.sum(end * start_low.astype(f32), axis=0, keepdims=True) + end_vec * start_vec
            last_grad = decay * jnp.sum(held, axis=1, keepdims=True) + jnp.sum(keep_grad, axis=0, keepdims=True)
            over_t = jnp.sum(jnp.transpose(expo), axis=1, keepdims=True)
            cum_grad = jnp.sum(expo, axis=1, keepdims=True) - over_t + moved - keep_grad
            cum_cols.append(cum_grad + jnp.where(at_end, last_grad, 0.0))
            in_cols.append(over_t + keep_grad)
            state_ref[h] = decay * end + mm_tn(query, cross_low)
            vec_ref[h : h + 1, :] = decay * end_vec + jnp.sum(pull * query.astype(f32), axis=0, keepdims=True)
        sums = lax.dot_general(
            from_here, lanes_of(*cum_cols), (((1,), (0,)), ((), ())), precision=highest, preferred_element_type=f32
        )
        forget = [sums[:, h : h + 1] * col[:, 14 + h : 15 + h] for h in range(2)]
        pre_ref[here, :] = lanes_of(*in_cols, *forget).astype(bf16)
        return carry

    lax.fori_loop(0, per, body, 0)


def back_stage(flag, mine, came, q, k, v, nlow, clow, start, nvec, col, row, stat):
    count, chan = q.shape
    tiles = count // TILE
    per = TILE // BLOCK
    flip = rows(chan, flip=tiles)
    thin = rows(LANES, flip=tiles)
    return pl.pallas_call(
        back_kernel,
        grid=(tiles,),
        in_specs=[smem, pack_spec(1), pack_spec(0), flip, flip, flip, flip, flip,
                  pl.BlockSpec((2, per, DH, DH), lambda i: (0, tiles - 1 - i, 0, 0)),
                  pl.BlockSpec((per, 8, DH), lambda i: (tiles - 1 - i, 0, 0)), thin,
                  pl.BlockSpec((per, 8, BLOCK), lambda i: (tiles - 1 - i, 0, 0)), thin],
        out_specs=[flip, flip, flip, thin],
        out_shape=[shape_of(count, chan)] * 3 + [shape_of(count, LANES, dtype=bf16)],
        scratch_shapes=[pltpu.VMEM((2, DH, DH), f32), pltpu.VMEM((8, DH), f32)],
        compiler_params=params(56),
        cost_estimate=cost(14 * count * chan * DH, count * chan * 30),
        name="back",
    )(flag, mine, came, q, k, v, nlow, clow, start, nvec, col, row, stat)


def band_back(value, map_hi, map_lo):
    high, low = value
    found = []
    for g in range(high.shape[1] // GROUP):
        part = slice(g * GROUP, (g + 1) * GROUP)
        found.append(
            mm_nt(high[:, part], map_hi[g])
            + (mm_nt(low[:, part], map_hi[g]) + mm_nt(high[:, part], map_lo[g]))
        )
    return jnp.concatenate(found, axis=1)


def conv_grad_of(active_grad, conv):
    sig = sigmoid(conv)
    return active_grad * sig * (1.0 + conv * (1.0 - sig))


def edge_kernel(qg_ref, kg_ref, pre_ref, sgrad_ref, conv_ref, skip_ref, coef_ref, gwt_ref, out_ref):
    pre = pre_ref[...]
    query_all = qg_ref[...] + mm(pre, gwt_ref[0])
    key_all = kg_ref[...] + mm(pre, gwt_ref[1])
    reach = QB - 1
    for g in range(query_all.shape[1] // LANES):
        part = slice(g * LANES, (g + 1) * LANES)
        total = sgrad_ref[:, part] * skip_ref[:, part]
        for m, value in enumerate((query_all[:, part], key_all[:, part])):
            for offset in range(-reach, reach + 1):
                total = total + pltpu.roll(
                    coef_ref[m, reach - offset : reach - offset + 1, part] * value, -offset % LANES, 1
                )
        out_ref[:, part] = conv_grad_of(total, conv_ref[:, part])[0:8, :]


def edge_stage(qg, kg, pre8, sgrad, conv, skip, coefs, gwt):
    chan = qg.shape[1]
    top = rows(chan, HALO)
    return pl.pallas_call(
        edge_kernel,
        grid=(1,),
        in_specs=[top, top, rows(LANES, HALO), top, top, whole(*skip.shape), whole(*coefs.shape),
                  whole(*gwt.shape)],
        out_specs=whole(8, chan),
        out_shape=shape_of(8, chan),
        compiler_params=params(16),
        cost_estimate=cost(10**7, 10**6),
        name="edge",
    )(qg, kg, pre8, sgrad, conv, skip, coefs, gwt)


def maps_kernel(
    flag, qg_ref, kg_ref, vg_ref, pre_ref, sgrad_ref, conv_ref, inner_ref, q_ref, k_ref, v_ref, edge_ref,
    skip_ref, cw_ref, coef_ref, gwt_ref,
    low_ref, small_ref,
    pad_ref, hi_ref, lo_ref, gmap_ref,
):
    tile, chan = qg_ref.shape
    groups = chan // GROUP
    reach = QB - 1

    @pl.when(pl.program_id(0) == 0)
    def _():
        pad_ref[tile : tile + 8, :] = jnp.where(flag[0] == 1, 0.0, edge_ref[...])
        gmap_ref[...] = jnp.zeros_like(gmap_ref)
        small_ref[...] = jnp.zeros_like(small_ref)
        apart = lax.broadcasted_iota(jnp.int32, (GROUP, GROUP), 0) - lax.broadcasted_iota(
            jnp.int32, (GROUP, GROUP), 1
        )
        for m in range(3):
            for g in range(groups):
                dense = jnp.zeros((GROUP, GROUP), f32)
                for offset in range(-reach, reach + 1):
                    coef = coef_ref[m, reach + offset : reach + offset + 1, g * GROUP : (g + 1) * GROUP]
                    dense = jnp.where(apart == offset, coef, dense)
                hi_ref[m, g], lo_ref[m, g] = split2(dense)

    pre = pre_ref[...]
    conv = conv_ref[...]
    inner = inner_ref[...]
    query_all = split2(qg_ref[...] + mm(pre, gwt_ref[0]))
    key_all = split2(kg_ref[...] + mm(pre, gwt_ref[1]))
    value_all = split2(vg_ref[...] + mm(pre, gwt_ref[2]))
    active = split2(conv * sigmoid(conv))
    inner2 = split2(inner)
    for m, (grads, acts) in enumerate(((query_all, active), (key_all, active), (value_all, inner2))):
        for g in range(groups):
            part = slice(g * GROUP, (g + 1) * GROUP)
            gmap_ref[m, g] += mm_tn(grads[0][:, part], acts[0][:, part]) + (
                mm_tn(grads[1][:, part], acts[0][:, part]) + mm_tn(grads[0][:, part], acts[1][:, part])
            )
    active_grad = (
        sgrad_ref[...] * skip_ref[...]
        + band_back(query_all, hi_ref[0], lo_ref[0])
        + band_back(key_all, hi_ref[1], lo_ref[1])
    )
    grad = conv_grad_of(active_grad, conv)
    pad_ref[0:tile, :] = grad
    taps = cw_ref.shape[0]
    small_ref[taps : taps + 1, :] += jnp.sum(grad, axis=0, keepdims=True)
    inner_grad = band_back(value_all, hi_ref[2], lo_ref[2])
    for j in range(cw_ref.shape[0]):
        moved = pad_ref[j : j + tile, :]
        inner_grad = inner_grad + cw_ref[j : j + 1, :] * moved
        small_ref[j : j + 1, :] += jnp.sum(moved * inner, axis=0, keepdims=True)
    low_ref[...] = inner_grad.astype(bf16)
    pad_ref[tile : tile + 8, :] = pad_ref[0:8, :]
    for m, ref in enumerate((q_ref, k_ref, v_ref)):
        small_ref[8 * (m + 1) : 8 * (m + 2), :] += mm_tn(pre, ref[...])[0:8, :]
    small_ref[taps + 1 : taps + 2, 0:LANES] += jnp.sum(pre.astype(f32), axis=0, keepdims=True)

    @pl.when(pl.program_id(0) == pl.num_programs(0) - 1)
    def _():
        r = lax.broadcasted_iota(jnp.int32, (GROUP, GROUP), 0)
        c = lax.broadcasted_iota(jnp.int32, (GROUP, GROUP), 1)
        pick = jnp.where(
            lax.broadcasted_iota(jnp.int32, (8, GROUP), 1) % QB == lax.broadcasted_iota(jnp.int32, (8, GROUP), 0),
            1.0, 0.0,
        )
        for m in range(3):
            for g in range(groups):
                held = jnp.where(r // QB == c // QB, gmap_ref[m, g], 0.0)
                small_ref[8 * (m + 4) : 8 * (m + 5), g * GROUP : (g + 1) * GROUP] = lax.dot_general(
                    pick, held, (((1,), (1,)), ((), ())), precision=highest, preferred_element_type=f32
                )


def maps_stage(flag, qg, kg, vg, pre8, sgrad, conv, inner, q, k, v, edge, skip, cw, coefs, gwt):
    count, chan = qg.shape
    tiles = count // TILE
    flip = rows(chan, flip=tiles)
    groups = chan // GROUP
    return pl.pallas_call(
        maps_kernel,
        grid=(tiles,),
        in_specs=[smem, flip, flip, flip, rows(LANES, flip=tiles), flip, flip, flip, flip, flip, flip,
                  whole(8, chan), whole(*skip.shape), whole(*cw.shape), whole(*coefs.shape), whole(*gwt.shape)],
        out_specs=[flip, whole(SMALL, chan)],
        out_shape=[shape_of(count, chan, dtype=bf16), shape_of(SMALL, chan)],
        scratch_shapes=[pltpu.VMEM((TILE + 8, chan), f32), pltpu.VMEM((3, groups, GROUP, GROUP), bf16),
                        pltpu.VMEM((3, groups, GROUP, GROUP), bf16), pltpu.VMEM((3, groups, GROUP, GROUP), f32)],
        compiler_params=params(60),
        cost_estimate=cost(20 * count * chan * GROUP, count * chan * 32),
        name="maps",
    )(flag, qg, kg, vg, pre8, sgrad, conv, inner, q, k, v, edge, skip, cw, coefs, gwt)


def exchanged(value, bit):
    route = [(i ^ bit, i) for i in range(lax.axis_size("dp"))]
    return lax.ppermute(value, "dp", route)


def summed(value, bits):
    place = lax.axis_index("dp")
    width = value.shape[1]
    for bit in bits:
        mine = (place // bit) % 2
        size = value.shape[0] // 2
        send = lax.dynamic_slice(value, ((1 - mine) * size, 0), (size, width)).astype(bf16)
        keep = lax.dynamic_slice(value, (mine * size, 0), (size, width))
        value = keep + exchanged(send, bit).astype(f32)
    value = value.astype(bf16)
    for bit in reversed(bits):
        first = (place // bit) % 2 == 0
        other = exchanged(value, bit)
        value = jnp.concatenate([jnp.where(first, value, other), jnp.where(first, other, value)], axis=0)
    return value


def all_sum(value, bits):
    for bit in bits:
        value = value + exchanged(value, bit)
    return value


def band_rows(weight):
    size = weight.shape[1]
    found = []
    for offset in range(1 - size, size):
        pieces = [
            weight[:, o, o + offset] if 0 <= o + offset < size else jnp.zeros_like(weight[:, 0, 0])
            for o in range(size)
        ]
        found.append(jnp.stack(pieces, axis=1).reshape(-1))
    return jnp.stack(found + [jnp.zeros_like(found[0])])


def on_device(
    tokens, cotangent, ln_weight, up_inner, up_gate, conv_weight, conv_bias, query_weight, key_weight,
    value_weight, gate_weight, gate_bias, group_weight, skip_weight, down_weight,
):
    count = tokens.shape[0]
    chan = up_inner.shape[1]
    model = up_inner.shape[0]
    half = tokens.shape[1]
    band = query_weight.shape[1]
    span = SEQ_LEN // count
    devices = lax.axis_size("dp")
    stride = devices // span
    t_place = lax.axis_index("tensor")
    piece = lax.axis_index("dp") // stride
    low_half = t_place == 0

    def across(value):
        return lax.ppermute(value, "tensor", [(0, 1), (1, 0)])

    def side_by_side(own):
        other = across(own)
        return jnp.concatenate([jnp.where(low_half, own, other), jnp.where(low_half, other, own)], axis=1)

    def along(value, distance):
        route = [(i - distance, i) for i in range(devices) if 0 <= i - distance < devices]
        return lax.ppermute(value, "dp", route)

    def flag_of(value):
        return jnp.asarray(value).astype(jnp.int32)[None]

    halo = side_by_side(along(tokens[count - HALO :], stride))
    full = side_by_side(tokens)
    full_cot = side_by_side(cotangent)

    coefs = jnp.stack([band_rows(w) for w in (query_weight, key_weight, value_weight)])
    gw = jnp.pad(gate_weight, ((0, 0), (0, 0), (0, LANES - gate_weight.shape[2])))
    gwt = jnp.swapaxes(gw, 1, 2)

    normed, inner, conv, active, q, k, v, pre = first_stage(
        flag_of(piece == 0), full, halo, ln_weight[None], up_inner, conv_weight, conv_bias[None],
        coefs, gw,
    )
    row, col, total = gates_stage(flag_of(t_place), pre, across(pre), gate_bias[:, None])
    even = flag_of(piece % 2 == 0)
    own, send = ends_stage(even, k, v, col, total)
    mine, came = pass_states(own, send, piece, span, stride)
    gate_in = mm(normed, up_gate)
    dgated = mm_nt(full_cot, down_weight)
    inside, norms = inside_stage(q, k, v, col, row)
    (
        gated, gate_in_grad, sgrad, nlow, clow, start, nvec, stat, ggroup, gskip, own, send
    ) = middle_stage(
        even, mine, came, q, k, v, inside, norms, col, gate_in, dgated, active, group_weight[None],
        skip_weight[None], total,
    )
    mine, came = pass_states(own, send, span - 1 - piece, span, stride)

    bits = [1 << n for n in range(devices.bit_length() - 1)]
    early = summed(jnp.concatenate([mm_tn(gated, full_cot), mm_tn(normed, gate_in_grad)], axis=0), bits)
    branch = mm(gated, down_weight)
    keep_half = lax.dynamic_slice_in_dim(branch, t_place * half, half, axis=1)
    send_half = lax.dynamic_slice_in_dim(branch, (1 - t_place) * half, half, axis=1)
    result = tokens.astype(f32) + (keep_half + across(send_half))
    squares = jnp.sum(result * result)
    gate_part = mm_nt(gate_in_grad, up_gate)

    qg, kg, vg, pre_own = back_stage(even, mine, came, q, k, v, nlow, clow, start, nvec, col, row, stat)
    pre_other = across(pre_own)
    heads = gate_bias.shape[0] // 2
    local = heads // 2
    a = jnp.where(low_half, pre_own, pre_other)
    c = jnp.where(low_half, pre_other, pre_own)
    pre8 = jnp.concatenate(
        [a[:, 0:local], c[:, 0:local], a[:, local : 2 * local], c[:, local : 2 * local],
         jnp.zeros((count, LANES - 2 * heads), bf16)], axis=1,
    )
    skip = skip_weight[None]
    edge = along(edge_stage(qg, kg, pre8, sgrad, conv, skip, coefs, gwt), -stride)
    inner_low, small = maps_stage(
        flag_of(piece == span - 1), qg, kg, vg, pre8, sgrad, conv, inner, q, k, v, edge, skip, conv_weight,
        coefs, gwt,
    )
    grad_up_inner = mm_tn(normed, inner_low)
    other_bits = [bits[1], bits[0]] + bits[2:]
    late = jnp.concatenate(
        [summed(grad_up_inner[: model // 2], bits), summed(grad_up_inner[model // 2 :], other_bits)], axis=0
    )
    ones = jnp.pad((squares + across(squares))[None, None], ((0, 7), (0, chan - 1)))
    small = all_sum(jnp.concatenate([small, ggroup, gskip, ones], axis=0), bits)

    part = gate_part + mm_nt(inner_low, up_inner)
    wide = full.astype(f32)
    centered = wide - jnp.mean(wide, axis=1, keepdims=True)
    inverse = lax.rsqrt(jnp.mean(centered * centered, axis=1, keepdims=True) + NORM_EPS)
    xhat = centered * inverse
    scaled = part * ln_weight
    mean_h = jnp.mean(scaled, axis=1)
    mean_hx = jnp.mean(scaled * xhat, axis=1)
    means = jnp.stack([mean_h, mean_hx])
    means = means + across(means)
    own_part = lax.dynamic_slice_in_dim(part, t_place * half, half, axis=1)
    send_part = lax.dynamic_slice_in_dim(part, (1 - t_place) * half, half, axis=1)
    normed_grad = own_part + across(send_part)
    xhat_own = lax.dynamic_slice_in_dim(xhat, t_place * half, half, axis=1)
    ln_own = lax.dynamic_slice_in_dim(ln_weight, t_place * half, half, axis=0)
    token_grad = (
        inverse * (normed_grad * ln_own - means[0][:, None] - xhat_own * means[1][:, None])
        + cotangent.astype(f32)
    )
    grad_ln = jnp.sum(normed_grad * xhat_own, axis=0)

    grad_ln = all_sum(jnp.broadcast_to(grad_ln[None], (8, half)), bits)[0]
    taps = conv_weight.shape[0]
    folded = small[32:56].reshape(3, 8, chan)[:, :band].reshape(3, band, chan // band, band)
    folded = jnp.transpose(folded, (0, 2, 3, 1))
    gate_rows = jnp.swapaxes(small[8:32].reshape(3, 8, chan), 1, 2)
    rms = jnp.sqrt(small[72, 0:1] / (count * model * devices))
    return (
        result.astype(bf16), token_grad, grad_ln, late.astype(f32), early[model:].astype(f32), small[:taps],
        small[taps], folded[0], folded[1], folded[2], gate_rows, small[taps + 1, : 2 * heads], small[56],
        small[64], early[:model].astype(f32), rms,
    )


def solution(mesh):
    rows_spec = P("dp", "tensor")
    cols = P(None, "tensor")
    vec = P("tensor")
    blocks = P("tensor", None, None)
    gates = P(None, "tensor", None)
    in_specs = (
        rows_spec, rows_spec, P(), cols, cols, cols, vec, blocks, blocks, blocks, gates, P(), vec, vec,
        P("tensor", None),
    )
    out_specs = (
        rows_spec, rows_spec, vec, cols, cols, cols, vec, blocks, blocks, blocks, gates, P(), vec, vec,
        P("tensor", None), P(),
    )
    return jax.shard_map(on_device, mesh=mesh, in_specs=in_specs, out_specs=out_specs, check_vma=False)
```

```python
import jax
import jax.numpy as jnp
from jax import lax
from jax.experimental import pallas as pl
from jax.experimental.pallas import tpu as pltpu
from jax.sharding import PartitionSpec as P

DH = 512
BLOCK = 64
QB = 4
SEQ_LEN = 8192
TILE = 256
GROUP = 256
HALO = 16
LANES = 128
NORM_EPS = 1e-05
PACK = DH + 16
WIDE = DH + 8
SMALL = 48
LIMIT = 60
STRIP = 256
UNROLL = 4

f32 = jnp.float32
bf16 = jnp.bfloat16
highest = lax.Precision.HIGHEST


def mm(left, right):
    return lax.dot_general(left, right, (((1,), (0,)), ((), ())), preferred_element_type=f32)


def mm_tn(left, right):
    return lax.dot_general(left, right, (((0,), (0,)), ((), ())), preferred_element_type=f32)


def mm_nt(left, right):
    return lax.dot_general(left, right, (((1,), (1,)), ((), ())), preferred_element_type=f32)


def split2(value):
    high = value.astype(bf16)
    return high, (value - high.astype(f32)).astype(bf16)


def split3(value):
    high = value.astype(bf16)
    rest = value - high.astype(f32)
    mid = rest.astype(bf16)
    return high, mid, (rest - mid.astype(f32)).astype(bf16)


def sigmoid(value):
    return 1.0 / (1.0 + jnp.exp(-value))


def params(vmem_mib):
    return pltpu.CompilerParams(
        dimension_semantics=("arbitrary",), vmem_limit_bytes=vmem_mib * 1024 * 1024
    )


def cost(flops, moved):
    return pl.CostEstimate(flops=flops, bytes_accessed=moved, transcendentals=0)


def rows(width, tile=TILE, flip=0):
    if flip:
        return pl.BlockSpec((tile, width), lambda i: (flip - 1 - i, 0))
    return pl.BlockSpec((tile, width), lambda i: (i, 0))


def whole(*shape):
    return pl.BlockSpec(shape, lambda i: (0,) * len(shape))


smem = pl.BlockSpec(memory_space=pltpu.MemorySpace.SMEM)


def shape_of(*dims, dtype=f32):
    return jax.ShapeDtypeStruct(dims, dtype)


def normed_rows(x, ln):
    centered = x - jnp.mean(x, axis=1, keepdims=True)
    inverse = lax.rsqrt(jnp.mean(centered * centered, axis=1, keepdims=True) + NORM_EPS)
    return (centered * inverse * ln).astype(bf16)


def band_sum(value, coefs, reach):
    sums = [coef[reach : reach + 1] * value for coef in coefs]
    for offset in range(-reach, reach + 1):
        if offset != 0:
            moved = pltpu.roll(value, -offset % value.shape[1], 1)
            sums = [
                total + coef[reach + offset : reach + offset + 1] * moved for total, coef in zip(sums, coefs)
            ]
    return sums


def spread_coefs(maps_ref, coef_ref):
    count = maps_ref.shape[2]
    chan = count * QB
    column = lax.broadcasted_iota(jnp.int32, (count, chan), 1)
    block = lax.broadcasted_iota(jnp.int32, (count, chan), 0)
    apart = column - QB * block
    zero = jnp.zeros((1, count), f32)
    total = jnp.zeros((24, chan), f32)
    for out in range(QB):
        picked = []
        for m in range(3):
            for offset in range(1 - QB, QB + 1):
                inside = 0 <= out + offset < QB and offset < QB
                at = out * QB + out + offset
                picked.append(maps_ref[m, at : at + 1, :] if inside else zero)
        place = jnp.where(apart == out, 1.0, 0.0).astype(bf16)
        for term in split3(jnp.concatenate(picked, axis=0)):
            total = total + mm(term, place)
    for m in range(3):
        coef_ref[m] = total[8 * m : 8 * (m + 1)]


def both_halves(flag, own, other):
    is_low = flag[1] == 0
    return jnp.concatenate([jnp.where(is_low, own, other), jnp.where(is_low, other, own)], axis=1)


def first_kernel(
    flag, own_ref, other_ref, hown_ref, hother_ref, ln_ref, up_ref, cw_ref, cb_ref, maps_ref, gate_ref,
    normed_ref, inner_ref, conv_ref, active_ref, q_ref, k_ref, v_ref, pre_ref, coef_ref, pad_ref, gw_ref,
):
    step = pl.program_id(0)
    tile = own_ref.shape[0]

    @pl.when(step == 0)
    def _():
        halo = both_halves(flag, hown_ref[...].astype(f32), hother_ref[...].astype(f32))
        before = mm(normed_rows(halo, ln_ref[...]), up_ref[...])
        pad_ref[0:8, :] = jnp.where(flag[0] == 1, 0.0, before[HALO - 8 :, :])
        spread_coefs(maps_ref, coef_ref)
        gw_ref[...] = jnp.zeros_like(gw_ref)
        gw_ref[:, :, 0 : gate_ref.shape[2]] = gate_ref[...]

    x = both_halves(flag, own_ref[...].astype(f32), other_ref[...].astype(f32))
    normed = normed_rows(x, ln_ref[...])
    normed_ref[...] = normed
    inner = mm(normed, up_ref[...])
    inner_ref[...] = inner
    pad_ref[8:, :] = inner
    conv = cb_ref[...] + cw_ref[0:1, :] * inner
    for j in range(1, cw_ref.shape[0]):
        conv = conv + cw_ref[j : j + 1, :] * pad_ref[8 - j : 8 - j + tile, :]
    conv_ref[...] = conv
    pad_ref[0:8, :] = pad_ref[tile : tile + 8, :]
    active_ref[...] = conv * sigmoid(conv)
    reach = QB - 1
    for g in range(inner.shape[1] // LANES):
        part = slice(g * LANES, (g + 1) * LANES)
        query, key = band_sum(active_ref[:, part], (coef_ref[0, :, part], coef_ref[1, :, part]), reach)
        q_ref[:, part] = query.astype(bf16)
        k_ref[:, part] = key.astype(bf16)
        v_ref[:, part] = band_sum(inner_ref[:, part], (coef_ref[2, :, part],), reach)[0].astype(bf16)
    pre = mm(q_ref[...], gw_ref[0]) + mm(k_ref[...], gw_ref[1]) + mm(v_ref[...], gw_ref[2])
    pre_ref[...] = jnp.transpose(pre)[0:8, :]


def first_stage(flag, own, other, hown, hother, ln, up, cw, cb, maps, gate):
    count, half = own.shape
    model, chan = up.shape
    wide = (count, chan)
    return pl.pallas_call(
        first_kernel,
        grid=(count // TILE,),
        in_specs=[
            smem, rows(half), rows(half), whole(*hown.shape), whole(*hown.shape), whole(*ln.shape),
            whole(*up.shape), whole(*cw.shape), whole(*cb.shape), whole(*maps.shape), whole(*gate.shape),
        ],
        out_specs=[rows(model), rows(chan), rows(chan), rows(chan), rows(chan), rows(chan), rows(chan),
                   pl.BlockSpec((8, TILE), lambda i: (0, i)), whole(3, 8, chan)],
        out_shape=[shape_of(count, model, dtype=bf16), shape_of(*wide), shape_of(*wide), shape_of(*wide),
                   shape_of(*wide, dtype=bf16), shape_of(*wide, dtype=bf16), shape_of(*wide, dtype=bf16),
                   shape_of(8, count), shape_of(3, 8, chan)],
        scratch_shapes=[pltpu.VMEM((TILE + 8, chan), f32), pltpu.VMEM((3, chan, LANES), bf16)],
        compiler_params=params(LIMIT),
        cost_estimate=cost(2 * count * model * chan * 4, count * chan * 20),
        name="first",
    )(flag, own, other, hown, hother, ln, up, cw, cb, maps, gate)


def gates_kernel(place, own_ref, other_ref, bias_ref, row_ref, col_ref, total_ref):
    count = own_ref.shape[1]
    pre = own_ref[...] + other_ref[...] + bias_ref[...]
    low_half = place[0] == 0
    in_pre = jnp.where(low_half, pre[0:2], pre[2:4])
    forget = jnp.where(low_half, pre[4:6], pre[6:8])
    both = jnp.concatenate([in_pre, forget, in_pre, forget], axis=0)
    in8 = jnp.concatenate([in_pre] * 4, axis=0)
    f8 = jnp.concatenate([forget] * 4, axis=0)
    log_keep = jnp.minimum(f8, 0.0) - jnp.log1p(jnp.exp(-jnp.abs(f8)))
    lane = lax.broadcasted_iota(jnp.int32, f8.shape, 1)
    place_in = lane % BLOCK
    cum = log_keep
    dist = 1
    while dist < BLOCK:
        cum = cum + jnp.where(place_in >= dist, pltpu.roll(cum, dist, 1), 0.0)
        dist *= 2
    last = jnp.where(place_in == BLOCK - 1, cum, 0.0)
    dist = 1
    while dist < BLOCK:
        last = last + jnp.where(place_in < BLOCK - dist, pltpu.roll(last, count - dist, 1), 0.0)
        dist *= 2
    before = jnp.where(lane >= BLOCK, pltpu.roll(last, BLOCK, 1), 0.0)
    after = jnp.where(lane < count - BLOCK, pltpu.roll(last, count - BLOCK, 1), 0.0)
    dist = BLOCK
    while dist < count:
        before = before + jnp.where(lane >= dist, pltpu.roll(before, dist, 1), 0.0)
        after = after + jnp.where(lane < count - dist, pltpu.roll(after, count - dist, 1), 0.0)
        dist *= 2
    scale = DH ** (-0.5)
    keep = jnp.exp(last - cum + in8) * scale
    table = jnp.concatenate(
        [
            cum[0:2], jnp.exp(cum[0:2]), keep[0:2], jnp.exp(after[0:2]),
            jnp.exp(before[0:2]), jnp.exp(last[0:2]), in8[0:2], 1.0 / (1.0 + jnp.exp(f8[0:2])),
        ],
        axis=0,
    )
    tall = jnp.concatenate([table, jnp.zeros((LANES - 16, count), f32)], axis=0)
    col_ref[...] = jnp.transpose(tall)
    small = jnp.concatenate([cum[0:2], in8[0:2], cum[0:2], in8[0:2]], axis=0)
    for b in range(count // BLOCK):
        row_ref[b] = small[:, b * BLOCK : (b + 1) * BLOCK]
    total = (before + last)[:, count - 1 : count]
    total_ref[...] = jnp.broadcast_to(total, total_ref.shape)


def gates_stage(place, own, other, bias):
    count = own.shape[1]
    return pl.pallas_call(
        gates_kernel,
        grid=(1,),
        in_specs=[smem, whole(8, count), whole(8, count), whole(8, 1)],
        out_specs=[whole(count // BLOCK, 8, BLOCK), whole(count, LANES), whole(8, DH)],
        out_shape=[shape_of(count // BLOCK, 8, BLOCK), shape_of(count, LANES), shape_of(8, DH)],
        compiler_params=params(LIMIT),
        cost_estimate=cost(count * 1000, count * 600),
        name="gates",
    )(place, own, other, bias)


def write_pack(ref, state, vector, log_decay):
    ref[0:DH, :] = state.astype(bf16)
    terms = split3(vector) + split3(log_decay)
    tail = jnp.concatenate(
        [t.astype(f32) for t in terms] + [jnp.zeros((PACK - DH - 6, DH), f32)], axis=0
    )
    ref[DH:PACK, :] = tail.astype(bf16)


def write_wide(ref, state, vector, log_decay):
    ref[0:DH, :] = state
    ref[DH:WIDE, :] = jnp.concatenate([vector, log_decay, jnp.zeros((WIDE - DH - 2, DH), f32)], axis=0)


def read_pack(ref):
    tail = ref[DH:PACK, :].astype(f32)
    return (
        ref[0:DH, :].astype(f32), (tail[0:1] + tail[1:2]) + tail[2:3], (tail[3:4] + tail[4:5]) + tail[5:6]
    )


def read_wide(ref):
    return ref[0:DH, :], ref[DH : DH + 1, :], ref[DH + 1 : DH + 2, :]


def joined(first, second):
    decay = jnp.exp(second[2])
    return decay * first[0] + second[0], decay * first[1] + second[1], first[2] + second[2]


def chosen(which, yes, no):
    return tuple(jnp.where(which, a, b) for a, b in zip(yes, no))


def pair_kernel(flag, own_ref, got_ref, send_ref, total_ref, lead_ref):
    own, got = read_wide(own_ref), read_pack(got_ref)
    is_lead = flag[0] == 1
    lead = chosen(is_lead, own, got)
    total = joined(lead, chosen(is_lead, got, own))
    write_wide(lead_ref, *lead)
    write_wide(total_ref, *total)
    write_pack(send_ref, *total)


def step_kernel(flag, total_ref, got_ref, before_ref, send_ref, new_total_ref, new_before_ref):
    total, got, before = read_wide(total_ref), read_pack(got_ref), read_wide(before_ref)
    upper = flag[0] == 1
    both = joined(chosen(upper, got, total), chosen(upper, total, got))
    write_wide(new_total_ref, *both)
    write_pack(send_ref, *both)
    write_wide(new_before_ref, *chosen(upper, joined(got, before), before))


def last_kernel(flag, got_ref, before_ref, lead_ref, send_ref, mine_ref):
    before, got = read_wide(before_ref), read_pack(got_ref)
    upper = flag[0] == 1
    is_lead = flag[1] == 1
    found = chosen(upper, joined(got, before), before)
    after = joined(found, read_wide(lead_ref))
    write_pack(send_ref, *chosen(is_lead, after, found))
    write_wide(mine_ref, *chosen(is_lead, found, after))


def pack_spec(wide):
    return whole(WIDE if wide else PACK, DH)


def pack_shape(wide):
    return shape_of(WIDE if wide else PACK, DH, dtype=f32 if wide else bf16)


def small_call(kernel, name, ins, outs, flag, *packs):
    return pl.pallas_call(
        kernel,
        grid=(1,),
        in_specs=[smem] + [pack_spec(w) for w in ins],
        out_specs=[pack_spec(w) for w in outs],
        out_shape=[pack_shape(w) for w in outs],
        compiler_params=params(LIMIT),
        cost_estimate=cost(PACK * DH * 8, PACK * DH * 3 * (len(ins) + len(outs))),
        name=name,
    )(flag, *packs)


def pass_states(own, send, place, span, stride, fillers=((), (), ())):
    devices = lax.axis_size("dp")

    def swap(value, bit):
        route = [((i // stride ^ bit) * stride + i % stride, i) for i in range(devices)]
        return lax.ppermute(value, "dp", route)

    def as_flag(*values):
        return jnp.stack([jnp.asarray(v).astype(jnp.int32) for v in values])

    is_lead = place % 2 == 0
    got = swap(send, 1)
    done = []
    got, filler = lax.optimization_barrier((got, fillers[0]))
    done.append(filler)
    out, total, lead = small_call(pair_kernel, "pair", (1, 0), (0, 1, 1), as_flag(is_lead), own, got)
    before = jnp.zeros_like(own)
    bit = 2
    while bit < span:
        got = swap(out, bit)
        got, filler = lax.optimization_barrier((got, fillers[min(len(done), len(fillers) - 1)]))
        done.append(filler)
        upper = (place // bit) % 2 == 1
        if bit * 2 < span:
            out, total, before = small_call(
                step_kernel, "step", (1, 0, 1), (0, 1, 1), as_flag(upper), total, got, before
            )
        bit *= 2
    out, mine = small_call(last_kernel, "last", (0, 1, 1), (0, 1), as_flag(upper, is_lead), got, before, lead)
    return mine, swap(out, 1), done


def put_states(flag, mine_ref, came_ref, state_ref, vec_ref):
    mine, came = read_wide(mine_ref), read_pack(came_ref)
    for h in range(2):
        found = chosen((flag[0] == 1) == (h == 0), mine, came)
        state_ref[h] = found[0]
        vec_ref[h : h + 1, :] = found[1]


def ends_kernel(flag, k_ref, v_ref, col_ref, total_ref, own_ref, send_ref, state_ref, vec_ref):
    step = pl.program_id(0)

    @pl.when(step == 0)
    def _():
        state_ref[...] = jnp.zeros_like(state_ref)
        vec_ref[...] = jnp.zeros_like(vec_ref)

    col = col_ref[...]
    for h in range(2):
        part = slice(h * DH, (h + 1) * DH)
        wide = k_ref[:, part].astype(f32)
        keep = col[:, 4 + h : 5 + h]
        later = col[:, 6 + h : 7 + h]
        kept = wide * keep
        high, low = split2(kept.astype(bf16).astype(f32) * later)
        value = v_ref[:, part]
        state_ref[h] += mm_tn(high, value) + mm_tn(low, value)
        vec_ref[h : h + 1, :] += jnp.sum(kept * later, axis=0, keepdims=True)

    @pl.when(step == pl.num_programs(0) - 1)
    def _():
        write_two(flag, state_ref, vec_ref, total_ref, own_ref, send_ref)


def write_two(flag, state_ref, vec_ref, total_ref, own_ref, send_ref):
    for h in range(2):
        found = (state_ref[h], vec_ref[h : h + 1, :], total_ref[h : h + 1, :])

        @pl.when(flag[0] == 1 - h)
        def _():
            write_wide(own_ref, *found)

        @pl.when(flag[0] == h)
        def _():
            write_pack(send_ref, *found)


def ends_stage(flag, k, v, col, total):
    count, chan = k.shape
    return pl.pallas_call(
        ends_kernel,
        grid=(count // TILE,),
        in_specs=[smem, rows(chan), rows(chan), rows(LANES), whole(8, DH)],
        out_specs=[pack_spec(1), pack_spec(0)],
        out_shape=[pack_shape(1), pack_shape(0)],
        scratch_shapes=[pltpu.VMEM((2, DH, DH), f32), pltpu.VMEM((8, DH), f32)],
        compiler_params=params(LIMIT),
        cost_estimate=cost(4 * count * chan * DH, count * chan * 4),
        name="ends",
    )(flag, k, v, col, total)


def damping_of(col, row, h):
    t = lax.broadcasted_iota(jnp.int32, (BLOCK, BLOCK), 0)
    s = lax.broadcasted_iota(jnp.int32, (BLOCK, BLOCK), 1)
    expo = col[:, h : h + 1] - row[h : h + 1, :] + row[2 + h : 3 + h, :]
    return jnp.exp(jnp.where(t >= s, expo, -1e30))


def lanes_of(*columns, offset=0):
    lane = lax.broadcasted_iota(jnp.int32, (columns[0].shape[0], LANES), 1) - offset
    out = jnp.zeros(lane.shape, f32)
    for i, column in enumerate(columns):
        out = jnp.where(lane == i, column, out)
    return out


def inside_kernel(q_ref, k_ref, v_ref, col_ref, row_ref, inside_ref, norm_ref):
    scale = DH ** (-0.5)

    def body(b, carry):
        r0 = pl.multiple_of(b * BLOCK, BLOCK)
        here = pl.ds(r0, BLOCK)
        col = col_ref[here, :]
        row = row_ref[b]
        sums = []
        for h in range(2):
            part = slice(h * DH, (h + 1) * DH)
            scores = mm_nt(q_ref[here, part], k_ref[here, part])
            weights = scores * damping_of(col, row, h) * scale
            inside_ref[here, part] = mm(weights.astype(bf16), v_ref[here, part])
            sums.append(jnp.sum(weights, axis=1, keepdims=True))
        norm_ref[here, :] = lanes_of(*sums)
        return carry

    lax.fori_loop(0, q_ref.shape[0] // BLOCK, body, 0)


def inside_stage(q, k, v, col, row):
    count, chan = q.shape
    return pl.pallas_call(
        inside_kernel,
        grid=(count // TILE,),
        in_specs=[rows(chan), rows(chan), rows(chan), rows(LANES),
                  pl.BlockSpec((TILE // BLOCK, 8, BLOCK), lambda i: (i, 0, 0))],
        out_specs=[rows(chan), rows(LANES)],
        out_shape=[shape_of(count, chan), shape_of(count, LANES)],
        compiler_params=params(LIMIT),
        cost_estimate=cost(4 * count * chan * BLOCK, count * chan * 10),
        name="inside",
    )(q, k, v, col, row)


def middle_kernel(
    flag, mine_ref, came_ref, q_ref, k_ref, v_ref, inside_ref, norm_ref, col_ref, gate_ref, dgated_ref,
    active_ref, group_ref, skip_ref, total_ref,
    gated_ref, gig_ref, sgrad_ref, nlow_ref, clow_ref, start_ref, nvec_ref, stat_ref, ggroup_ref, gskip_ref,
    own_ref, send_ref,
    state_ref, vec_ref, back_ref, bvec_ref, cross_ref, ncross_ref,
):
    step = pl.program_id(0)

    @pl.when(step == 0)
    def _():
        put_states(flag, mine_ref, came_ref, state_ref, vec_ref)
        back_ref[...] = jnp.zeros_like(back_ref)
        bvec_ref[...] = jnp.zeros_like(bvec_ref)
        ggroup_ref[...] = jnp.zeros_like(ggroup_ref)
        gskip_ref[...] = jnp.zeros_like(gskip_ref)

    def body(b, carry):
        r0 = pl.multiple_of(b * BLOCK, BLOCK)
        here = pl.ds(r0, BLOCK)
        col = col_ref[here, :]
        nvec_ref[b] = vec_ref[...]
        crosses = []
        for h in range(2):
            part = slice(h * DH, (h + 1) * DH)
            query = q_ref[here, part]
            state = state_ref[h]
            state_low = state.astype(bf16)
            start_ref[h, b] = state_low
            cross_ref[here, part] = mm(query, state_low)
            vec = vec_ref[h : h + 1, :]
            crosses.append(jnp.sum(query.astype(f32) * vec, axis=1, keepdims=True))
            kept = k_ref[here, part].astype(f32) * col[:, 4 + h : 5 + h]
            decay = col[0:1, 10 + h : 11 + h]
            state_ref[h] = decay * state + mm_tn(kept.astype(bf16), v_ref[here, part])
            vec_ref[h : h + 1, :] = decay * vec + jnp.sum(kept, axis=0, keepdims=True)
        ncross_ref[here, :] = lanes_of(*crosses)
        return carry

    lax.fori_loop(0, q_ref.shape[0] // BLOCK, body, 0, unroll=UNROLL)

    def strip(i, carry):
        here = pl.ds(pl.multiple_of(i * STRIP, STRIP), STRIP)
        col = col_ref[here, :]
        norms = norm_ref[here, :]
        stats = []
        for h in range(2):
            part = slice(h * DH, (h + 1) * DH)
            growth = col[:, 2 + h : 3 + h]
            carried = growth * cross_ref[here, part]
            norm_cross = growth * ncross_ref[here, h : h + 1]
            numer = inside_ref[here, part] + carried
            normal = norms[:, h : h + 1] + norm_cross
            over = 1.0 / jnp.maximum(jnp.abs(normal), 1.0)
            mixed = numer * over
            centered = mixed - jnp.mean(mixed, axis=1, keepdims=True)
            inverse = lax.rsqrt(jnp.mean(centered * centered, axis=1, keepdims=True) + NORM_EPS)
            ghat = centered * inverse
            active = active_ref[here, part]
            gate = gate_ref[here, part]
            sig = sigmoid(gate)
            gact = gate * sig
            gweight = group_ref[0:1, part]
            gstate = ghat * gweight + skip_ref[0:1, part] * active
            gated_ref[here, part] = (gstate * gact).astype(bf16)
            dgated = dgated_ref[here, part]
            sgrad = dgated * gact
            sgrad_ref[here, part] = sgrad
            gig_ref[here, part] = (dgated * gstate * sig * (1.0 + gate * (1.0 - sig))).astype(bf16)
            gskip_ref[0:1, part] += jnp.sum(sgrad * active, axis=0, keepdims=True)
            ggroup_ref[0:1, part] += jnp.sum(sgrad * ghat, axis=0, keepdims=True)
            g = sgrad * gweight
            mgrad = inverse * (
                g - jnp.mean(g, axis=1, keepdims=True) - ghat * jnp.mean(g * ghat, axis=1, keepdims=True)
            )
            ngrad = mgrad * over
            down = -jnp.sum(mgrad * mixed, axis=1, keepdims=True) * over
            normal_grad = jnp.where(normal > 1.0, down, jnp.where(normal < -1.0, -down, 0.0))
            nlow_ref[here, part] = ngrad.astype(bf16)
            clow_ref[here, part] = (growth * ngrad).astype(bf16)
            moved = jnp.sum(ngrad * carried, axis=1, keepdims=True) + normal_grad * norm_cross
            stats.append((normal_grad, moved))
            scaled = col[:, 8 + h : 9 + h] * growth * normal_grad
            bvec_ref[h : h + 1, :] += jnp.sum(scaled * q_ref[here, part].astype(f32), axis=0, keepdims=True)
        stat_ref[here, :] = lanes_of(stats[0][0], stats[1][0], stats[0][1], stats[1][1])
        return carry

    lax.fori_loop(0, q_ref.shape[0] // STRIP, strip, 0)
    for h in range(2):
        part = slice(h * DH, (h + 1) * DH)
        high, low = split2(clow_ref[:, part].astype(f32) * col_ref[:, 8 + h : 9 + h])
        query = q_ref[:, part]
        back_ref[h] += mm_tn(query, high) + mm_tn(query, low)

    @pl.when(step == pl.num_programs(0) - 1)
    def _():
        write_two(flag, back_ref, bvec_ref, total_ref, own_ref, send_ref)


def middle_stage(flag, mine, came, q, k, v, inside, norms, col, gate, dgated, active, group, skip, total):
    count, chan = q.shape
    blocks = count // BLOCK
    per = TILE // BLOCK
    return pl.pallas_call(
        middle_kernel,
        grid=(count // TILE,),
        in_specs=[smem, pack_spec(1), pack_spec(0), rows(chan), rows(chan), rows(chan), rows(chan), rows(LANES), rows(LANES),
                  rows(chan), rows(chan), rows(chan), whole(1, chan), whole(1, chan), whole(8, DH)],
        out_specs=[rows(chan), rows(chan), rows(chan), rows(chan), rows(chan),
                   pl.BlockSpec((2, per, DH, DH), lambda i: (0, i, 0, 0)),
                   pl.BlockSpec((per, 8, DH), lambda i: (i, 0, 0)),
                   rows(LANES), whole(8, chan), whole(8, chan), pack_spec(1), pack_spec(0)],
        out_shape=[shape_of(count, chan, dtype=bf16), shape_of(count, chan, dtype=bf16), shape_of(count, chan),
                   shape_of(count, chan, dtype=bf16), shape_of(count, chan, dtype=bf16),
                   shape_of(2, blocks, DH, DH, dtype=bf16), shape_of(blocks, 8, DH), shape_of(count, LANES),
                   shape_of(8, chan), shape_of(8, chan),
                   pack_shape(1), pack_shape(0)],
        scratch_shapes=[pltpu.VMEM((2, DH, DH), f32), pltpu.VMEM((8, DH), f32),
                        pltpu.VMEM((2, DH, DH), f32), pltpu.VMEM((8, DH), f32),
                        pltpu.VMEM((TILE, chan), f32), pltpu.VMEM((TILE, LANES), f32)],
        compiler_params=params(LIMIT),
        cost_estimate=cost(10 * count * chan * DH, count * chan * 40),
        name="middle",
    )(flag, mine, came, q, k, v, inside, norms, col, gate, dgated, active, group, skip, total)


def back_kernel(
    flag, mine_ref, came_ref, q_ref, k_ref, v_ref, nlow_ref, clow_ref, start_ref, nvec_ref, col_ref, row_ref,
    stat_ref,
    qg_ref, kg_ref, vg_ref, pre_ref,
    state_ref, vec_ref,
):
    scale = DH ** (-0.5)

    @pl.when(pl.program_id(0) == 0)
    def _():
        put_states(flag, mine_ref, came_ref, state_ref, vec_ref)

    u = lax.broadcasted_iota(jnp.int32, (BLOCK, BLOCK), 0)
    t = lax.broadcasted_iota(jnp.int32, (BLOCK, BLOCK), 1)
    from_here = jnp.where(t >= u, 1.0, 0.0)
    at_end = lax.broadcasted_iota(jnp.int32, (BLOCK, 1), 0) == BLOCK - 1
    per = q_ref.shape[0] // BLOCK

    def body(i, carry):
        b = per - 1 - i
        r0 = pl.multiple_of(b * BLOCK, BLOCK)
        here = pl.ds(r0, BLOCK)
        col = col_ref[here, :]
        row = row_ref[b]
        stat = stat_ref[here, :]
        starts = nvec_ref[b]
        in_cols, cum_cols = [], []
        for h in range(2):
            part = slice(h * DH, (h + 1) * DH)
            query, key, value = q_ref[here, part], k_ref[here, part], v_ref[here, part]
            numer_low, cross_low = nlow_ref[here, part], clow_ref[here, part]
            growth = col[:, 2 + h : 3 + h]
            keep = col[:, 4 + h : 5 + h]
            decay = col[0:1, 10 + h : 11 + h]
            normal_grad = stat[:, h : h + 1]
            moved = stat[:, 2 + h : 3 + h]
            end = state_ref[h]
            end_low = end.astype(bf16)
            end_vec = vec_ref[h : h + 1, :]
            start_low = start_ref[h, b]
            start_vec = starts[h : h + 1, :]
            damping = damping_of(col, row, h)
            scores = mm_nt(query, key)
            weights_low = (scores * damping * scale).astype(bf16)
            weights_grad = mm_nt(numer_low, value) + normal_grad
            damped = weights_grad * scale * damping
            scores_low = damped.astype(bf16)
            expo = damped * scores
            pull = growth * normal_grad
            qg_ref[here, part] = mm(scores_low, key) + mm_nt(cross_low, start_low) + pull * start_vec
            wide = key.astype(f32)
            kept_low = (wide * keep).astype(bf16)
            key_total = mm_nt(value, end_low) + end_vec
            kg_ref[here, part] = mm_tn(scores_low, query) + keep * key_total
            vg_ref[here, part] = mm_tn(weights_low, numer_low) + mm(kept_low, end_low)
            keep_grad = keep * jnp.sum(wide * key_total, axis=1, keepdims=True)
            held = jnp.sum(end * start_low.astype(f32), axis=0, keepdims=True) + end_vec * start_vec
            last_grad = decay * jnp.sum(held, axis=1, keepdims=True) + jnp.sum(keep_grad, axis=0, keepdims=True)
            over_t = jnp.sum(jnp.transpose(expo), axis=1, keepdims=True)
            cum_grad = jnp.sum(expo, axis=1, keepdims=True) - over_t + moved - keep_grad
            cum_cols.append(cum_grad + jnp.where(at_end, last_grad, 0.0))
            in_cols.append(over_t + keep_grad)
            state_ref[h] = decay * end + mm_tn(query, cross_low)
            vec_ref[h : h + 1, :] = decay * end_vec + jnp.sum(pull * query.astype(f32), axis=0, keepdims=True)
        sums = lax.dot_general(
            from_here, lanes_of(*cum_cols), (((1,), (0,)), ((), ())), precision=highest, preferred_element_type=f32
        )
        forget = [sums[:, h : h + 1] * col[:, 14 + h : 15 + h] for h in range(2)]
        pre_ref[here, :] = lanes_of(*in_cols, *forget, offset=4 * flag[1]).astype(bf16)
        return carry

    lax.fori_loop(0, per, body, 0, unroll=2)


def back_stage(flag, mine, came, q, k, v, nlow, clow, start, nvec, col, row, stat):
    count, chan = q.shape
    tiles = count // TILE
    per = TILE // BLOCK
    flip = rows(chan, flip=tiles)
    thin = rows(LANES, flip=tiles)
    return pl.pallas_call(
        back_kernel,
        grid=(tiles,),
        in_specs=[smem, pack_spec(1), pack_spec(0), flip, flip, flip, flip, flip,
                  pl.BlockSpec((2, per, DH, DH), lambda i: (0, tiles - 1 - i, 0, 0)),
                  pl.BlockSpec((per, 8, DH), lambda i: (tiles - 1 - i, 0, 0)), thin,
                  pl.BlockSpec((per, 8, BLOCK), lambda i: (tiles - 1 - i, 0, 0)), thin],
        out_specs=[flip, flip, flip, thin],
        out_shape=[shape_of(count, chan)] * 3 + [shape_of(count, LANES, dtype=bf16)],
        scratch_shapes=[pltpu.VMEM((2, DH, DH), f32), pltpu.VMEM((8, DH), f32)],
        compiler_params=params(LIMIT),
        cost_estimate=cost(14 * count * chan * DH, count * chan * 30),
        name="back",
    )(flag, mine, came, q, k, v, nlow, clow, start, nvec, col, row, stat)


def band_back(value, map_hi, map_lo):
    high, low = value
    found = []
    for g in range(high.shape[1] // GROUP):
        part = slice(g * GROUP, (g + 1) * GROUP)
        found.append(
            mm_nt(high[:, part], map_hi[g])
            + (mm_nt(low[:, part], map_hi[g]) + mm_nt(high[:, part], map_lo[g]))
        )
    return jnp.concatenate(found, axis=1)


def conv_grad_of(active_grad, conv):
    sig = sigmoid(conv)
    return active_grad * sig * (1.0 + conv * (1.0 - sig))


def edge_kernel(qg_ref, kg_ref, pre_ref, other_ref, sgrad_ref, conv_ref, skip_ref, coef_ref, gwt_ref, out_ref):
    pre = pre_ref[...] + other_ref[...]
    query_all = qg_ref[...] + mm(pre, gwt_ref[0])
    key_all = kg_ref[...] + mm(pre, gwt_ref[1])
    reach = QB - 1
    for g in range(query_all.shape[1] // LANES):
        part = slice(g * LANES, (g + 1) * LANES)
        total = sgrad_ref[:, part] * skip_ref[:, part]
        for m, value in enumerate((query_all[:, part], key_all[:, part])):
            for offset in range(-reach, reach + 1):
                total = total + pltpu.roll(
                    coef_ref[m, reach - offset : reach - offset + 1, part] * value, -offset % LANES, 1
                )
        out_ref[:, part] = conv_grad_of(total, conv_ref[:, part])[0:8, :]


def edge_stage(qg, kg, pre, other, sgrad, conv, skip, coefs, gwt):
    chan = qg.shape[1]
    top = rows(chan, HALO)
    return pl.pallas_call(
        edge_kernel,
        grid=(1,),
        in_specs=[top, top, rows(LANES, HALO), rows(LANES, HALO), top, top, whole(*skip.shape), whole(*coefs.shape),
                  whole(*gwt.shape)],
        out_specs=whole(8, chan),
        out_shape=shape_of(8, chan),
        compiler_params=params(LIMIT),
        cost_estimate=cost(10**7, 10**6),
        name="edge",
    )(qg, kg, pre, other, sgrad, conv, skip, coefs, gwt)


def maps_kernel(
    flag, qg_ref, kg_ref, vg_ref, mine_ref, other_ref, sgrad_ref, conv_ref, inner_ref, q_ref, k_ref, v_ref, edge_ref,
    skip_ref, cw_ref, coef_ref, gwt_ref, ggroup_ref, gskip_ref,
    low_ref, small_ref,
    pad_ref, hi_ref, lo_ref, gmap_ref,
):
    tile, chan = qg_ref.shape
    groups = chan // GROUP
    reach = QB - 1

    @pl.when(pl.program_id(0) == 0)
    def _():
        pad_ref[tile : tile + 8, :] = jnp.where(flag[0] == 1, 0.0, edge_ref[...])
        gmap_ref[...] = jnp.zeros_like(gmap_ref)
        small_ref[...] = jnp.zeros_like(small_ref)
        apart = lax.broadcasted_iota(jnp.int32, (GROUP, GROUP), 0) - lax.broadcasted_iota(
            jnp.int32, (GROUP, GROUP), 1
        )
        for m in range(3):
            for g in range(groups):
                dense = jnp.zeros((GROUP, GROUP), f32)
                for offset in range(-reach, reach + 1):
                    coef = coef_ref[m, reach + offset : reach + offset + 1, g * GROUP : (g + 1) * GROUP]
                    dense = jnp.where(apart == offset, coef, dense)
                hi_ref[m, g], lo_ref[m, g] = split2(dense)

    pre = mine_ref[...] + other_ref[...]
    conv = conv_ref[...]
    inner = inner_ref[...]
    query_all = split2(qg_ref[...] + mm(pre, gwt_ref[0]))
    key_all = split2(kg_ref[...] + mm(pre, gwt_ref[1]))
    value_all = split2(vg_ref[...] + mm(pre, gwt_ref[2]))
    active = split2(conv * sigmoid(conv))
    inner2 = split2(inner)
    for m, (grads, acts) in enumerate(((query_all, active), (key_all, active), (value_all, inner2))):
        for g in range(groups):
            part = slice(g * GROUP, (g + 1) * GROUP)
            gmap_ref[m, g] += mm_tn(grads[0][:, part], acts[0][:, part]) + (
                mm_tn(grads[1][:, part], acts[0][:, part]) + mm_tn(grads[0][:, part], acts[1][:, part])
            )
    active_grad = (
        sgrad_ref[...] * skip_ref[...]
        + band_back(query_all, hi_ref[0], lo_ref[0])
        + band_back(key_all, hi_ref[1], lo_ref[1])
    )
    grad = conv_grad_of(active_grad, conv)
    pad_ref[0:tile, :] = grad
    taps = cw_ref.shape[0]
    small_ref[taps : taps + 1, :] += jnp.sum(grad, axis=0, keepdims=True)
    inner_grad = band_back(value_all, hi_ref[2], lo_ref[2])
    for j in range(cw_ref.shape[0]):
        moved = pad_ref[j : j + tile, :]
        inner_grad = inner_grad + cw_ref[j : j + 1, :] * moved
        small_ref[j : j + 1, :] += jnp.sum(moved * inner, axis=0, keepdims=True)
    low_ref[...] = inner_grad.astype(bf16)
    pad_ref[tile : tile + 8, :] = pad_ref[0:8, :]
    for m, ref in enumerate((q_ref, k_ref, v_ref)):
        small_ref[8 * (m + 1) : 8 * (m + 2), :] += mm_tn(pre, ref[...])[0:8, :]
    small_ref[taps + 1 : taps + 2, 0:LANES] += jnp.sum(pre.astype(f32), axis=0, keepdims=True)

    @pl.when(pl.program_id(0) == pl.num_programs(0) - 1)
    def _():
        r = lax.broadcasted_iota(jnp.int32, (GROUP, GROUP), 0)
        c = lax.broadcasted_iota(jnp.int32, (GROUP, GROUP), 1)
        pick = jnp.where(
            lax.broadcasted_iota(jnp.int32, (8, GROUP), 1) % QB == lax.broadcasted_iota(jnp.int32, (8, GROUP), 0),
            1.0, 0.0,
        )
        for m in range(3):
            for g in range(groups):
                held = jnp.where(r // QB == c // QB, gmap_ref[m, g], 0.0)
                found = lax.dot_general(
                    pick, held, (((1,), (1,)), ((), ())), precision=highest, preferred_element_type=f32
                )
                small_ref[32 + QB * m : 32 + QB * (m + 1), g * GROUP : (g + 1) * GROUP] = found[0:QB]
        small_ref[taps + 2 : taps + 3, :] = ggroup_ref[0:1, :]
        small_ref[taps + 3 : taps + 4, :] = gskip_ref[0:1, :]


def maps_stage(flag, qg, kg, vg, pre, other, sgrad, conv, inner, q, k, v, edge, skip, cw, coefs, gwt, ggroup, gskip):
    count, chan = qg.shape
    tiles = count // TILE
    flip = rows(chan, flip=tiles)
    groups = chan // GROUP
    return pl.pallas_call(
        maps_kernel,
        grid=(tiles,),
        in_specs=[smem, flip, flip, flip, rows(LANES, flip=tiles), rows(LANES, flip=tiles), flip, flip, flip, flip,
                  flip, flip,
                  whole(8, chan), whole(*skip.shape), whole(*cw.shape), whole(*coefs.shape), whole(*gwt.shape),
                  whole(8, chan), whole(8, chan)],
        out_specs=[flip, whole(SMALL, chan)],
        out_shape=[shape_of(count, chan, dtype=bf16), shape_of(SMALL, chan)],
        scratch_shapes=[pltpu.VMEM((TILE + 8, chan), f32), pltpu.VMEM((3, groups, GROUP, GROUP), bf16),
                        pltpu.VMEM((3, groups, GROUP, GROUP), bf16), pltpu.VMEM((3, groups, GROUP, GROUP), f32)],
        compiler_params=params(LIMIT),
        cost_estimate=cost(20 * count * chan * GROUP, count * chan * 32),
        name="maps",
    )(flag, qg, kg, vg, pre, other, sgrad, conv, inner, q, k, v, edge, skip, cw, coefs, gwt, ggroup, gskip)


def exchanged(value, bit):
    route = [(i ^ bit, i) for i in range(lax.axis_size("dp"))]
    return lax.ppermute(value, "dp", route)


def halved(value, bit):
    mine = (lax.axis_index("dp") // bit) % 2
    width = value.shape[1]
    size = value.shape[0] // 2
    send = lax.dynamic_slice(value, ((1 - mine) * size, 0), (size, width)).astype(bf16)
    keep = lax.dynamic_slice(value, (mine * size, 0), (size, width))
    return keep + exchanged(send, bit).astype(f32)


def joined_halves(value, bit):
    first = (lax.axis_index("dp") // bit) % 2 == 0
    other = exchanged(value, bit)
    return jnp.concatenate([jnp.where(first, value, other), jnp.where(first, other, value)], axis=0)


def finished(pair, bits):
    value = jnp.concatenate(pair, axis=0)
    for bit in bits[2:]:
        value = halved(value, bit)
    value = value.astype(bf16)
    for bit in reversed(bits[2:]):
        value = joined_halves(value, bit)
    size = value.shape[0] // 2
    one, two = joined_halves(value[:size], bits[1]), joined_halves(value[size:], bits[0])
    return jnp.concatenate([joined_halves(one, bits[0]), joined_halves(two, bits[1])], axis=0)


def half_products(pairs, side):
    found = []
    for left, right in pairs:
        size = left.shape[1] // 2
        found.append(mm_tn(lax.dynamic_slice_in_dim(left, side * size, size, axis=1), right))
    return found


def shares(value):
    devices = lax.axis_size("dp")
    groups = [[i for i in range(devices) if i & 5 == low] for low in (0, 1, 4, 5)]
    return lax.psum_scatter(value, "dp", scatter_dimension=0, axis_index_groups=groups, tiled=True)


def from_shares(every):
    devices = lax.axis_size("dp")
    size, width = every.shape[0] // devices, every.shape[1]
    every = every.reshape(devices // 8, 2, 2, 2, size, width)
    return [jnp.transpose(every[:, i], (2, 0, 1, 3, 4)).reshape(-1, width).astype(f32) for i in range(2)]


def all_sum(value, bits):
    for bit in bits:
        value = value + exchanged(value, bit)
    return value


def map_rows(weight):
    return weight.reshape(weight.shape[0], -1).T


def on_device(
    tokens, cotangent, ln_weight, up_inner, up_gate, conv_weight, conv_bias, query_weight, key_weight,
    value_weight, gate_weight, gate_bias, group_weight, skip_weight, down_weight,
):
    count = tokens.shape[0]
    chan = up_inner.shape[1]
    model = up_inner.shape[0]
    half = tokens.shape[1]
    band = query_weight.shape[1]
    span = SEQ_LEN // count
    devices = lax.axis_size("dp")
    stride = devices // span
    t_place = lax.axis_index("tensor")
    piece = lax.axis_index("dp") // stride
    low_half = t_place == 0

    def across(value):
        return lax.ppermute(value, "tensor", [(0, 1), (1, 0)])

    def side_by_side(own, other):
        return jnp.concatenate([jnp.where(low_half, own, other), jnp.where(low_half, other, own)], axis=1)

    def along(value, distance):
        route = [(i - distance, i) for i in range(devices) if 0 <= i - distance < devices]
        return lax.ppermute(value, "dp", route)

    def flags(*values):
        return jnp.stack([jnp.asarray(v).astype(jnp.int32) for v in values])

    halo = along(tokens[count - HALO :], stride)
    other_tokens = across(tokens)
    full = side_by_side(tokens, other_tokens)
    full_cot = side_by_side(cotangent, across(cotangent))

    maps = jnp.stack([map_rows(w) for w in (query_weight, key_weight, value_weight)])
    heads = gate_bias.shape[0] // 2
    local = heads // 2
    order = [kind * heads + t * local + j for t in range(2) for kind in range(2) for j in range(local)]
    gwt = jnp.pad(
        jnp.swapaxes(gate_weight, 1, 2)[:, jnp.array(order)], ((0, 0), (0, LANES - 2 * heads), (0, 0))
    )

    normed, inner, conv, active, q, k, v, pre, coefs = first_stage(
        flags(piece == 0, t_place), tokens, other_tokens, halo, across(halo), ln_weight[None], up_inner,
        conv_weight, conv_bias[None], maps, gate_weight,
    )
    row, col, total = gates_stage(flags(t_place), pre, across(pre), gate_bias[:, None])
    even = flags(piece % 2 == 0)
    own, send = ends_stage(even, k, v, col, total)
    gate_in = mm(normed, up_gate)
    dgated = mm_nt(full_cot, down_weight)
    inside, norms = inside_stage(q, k, v, col, row)
    mine, came, done = pass_states(
        own, send, piece, span, stride, ((inside, norms), (dgated,), (gate_in,))
    )
    (inside, norms), (dgated,), (gate_in,) = done
    (
        gated, gate_in_grad, sgrad, nlow, clow, start, nvec, stat, ggroup, gskip, own, send
    ) = middle_stage(
        even, mine, came, q, k, v, inside, norms, col, gate_in, dgated, active, group_weight[None],
        skip_weight[None], total,
    )
    pairs = ((gated, full_cot), (normed, gate_in_grad))
    lowest = lax.axis_index("dp") % 2
    sends = [value.astype(bf16) for value in half_products(pairs, 1 - lowest)]
    keeps = [
        value + exchanged(sent, 1).astype(f32) for value, sent in zip(half_products(pairs, lowest), sends)
    ]
    both = jnp.concatenate(keeps, axis=0)
    branch = mm(gated, down_weight)
    second = (lax.axis_index("dp") // 4) % 2
    away = lax.dynamic_slice_in_dim(both, (1 - second) * (model // 2), model // 2, axis=0).astype(bf16)
    mine, came, done = pass_states(own, send, span - 1 - piece, span, stride, (sends, (branch,), (both, away)))
    _, (branch,), (both, away) = done
    both = lax.dynamic_slice_in_dim(both, second * (model // 2), model // 2, axis=0)
    both = both + exchanged(away, 4).astype(f32)
    mine, came, both = lax.optimization_barrier((mine, came, both))
    share = shares(both)

    bits = [1 << n for n in range(devices.bit_length() - 1)]
    keep_half = lax.dynamic_slice_in_dim(branch, t_place * half, half, axis=1)
    send_half = lax.dynamic_slice_in_dim(branch, (1 - t_place) * half, half, axis=1)
    result = tokens.astype(f32) + (keep_half + across(send_half))
    squares = jnp.sum(result * result)
    gate_part = mm_nt(gate_in_grad, up_gate)

    qg, kg, vg, pre_own = back_stage(flags(piece % 2 == 0, t_place), mine, came, q, k, v, nlow, clow, start, nvec, col, row, stat)
    pre_other = across(pre_own)
    skip = skip_weight[None]
    edge = along(edge_stage(qg, kg, pre_own, pre_other, sgrad, conv, skip, coefs, gwt), -stride)
    edge, share = lax.optimization_barrier((edge, share.astype(bf16)))
    every = lax.all_gather(share, "dp", axis=0, tiled=True)
    inner_low, small = maps_stage(
        flags(piece == span - 1), qg, kg, vg, pre_own, pre_other, sgrad, conv, inner, q, k, v, edge, skip, conv_weight,
        coefs, gwt, ggroup, gskip,
    )
    grad_up_inner, inner_low = lax.optimization_barrier((mm_tn(normed, inner_low), inner_low))
    late = [halved(grad_up_inner[: model // 2], bits[0]), halved(grad_up_inner[model // 2 :], bits[1])]
    part = gate_part + mm_nt(inner_low, up_inner)
    wide = full.astype(f32)
    centered = wide - jnp.mean(wide, axis=1, keepdims=True)
    inverse = lax.rsqrt(jnp.mean(centered * centered, axis=1, keepdims=True) + NORM_EPS)
    xhat = centered * inverse
    scaled = part * ln_weight
    mean_h = jnp.mean(scaled, axis=1)
    mean_hx = jnp.mean(scaled * xhat, axis=1)
    means = jnp.stack([mean_h, mean_hx])
    late, part, means = lax.optimization_barrier((late, part, means))
    late = [halved(late[0], bits[1]), halved(late[1], bits[0])]
    means = means + across(means)
    own_part = lax.dynamic_slice_in_dim(part, t_place * half, half, axis=1)
    send_part = lax.dynamic_slice_in_dim(part, (1 - t_place) * half, half, axis=1)
    normed_grad = own_part + across(send_part)
    xhat_own = lax.dynamic_slice_in_dim(xhat, t_place * half, half, axis=1)
    ln_own = lax.dynamic_slice_in_dim(ln_weight, t_place * half, half, axis=0)
    token_grad = (
        inverse * (normed_grad * ln_own - means[0][:, None] - xhat_own * means[1][:, None])
        + cotangent.astype(f32)
    )
    grad_ln = jnp.sum(normed_grad * xhat_own, axis=0)

    late, grad_ln, token_grad, every = lax.optimization_barrier((late, grad_ln, token_grad, every))
    last = jnp.concatenate([grad_ln, jnp.broadcast_to(squares + across(squares), (LANES,))])
    small = all_sum(small + jnp.pad(last[None], ((SMALL - 1, 0), (0, chan - half - LANES))), bits)
    grad_ln = small[SMALL - 1, :half]
    late = finished(late, bits)
    early = from_shares(every)
    taps = conv_weight.shape[0]
    folded = small[32 : 32 + 3 * band].reshape(3, band, chan // band, band)
    folded = jnp.transpose(folded, (0, 2, 3, 1))
    back_order = jnp.array([order.index(c) for c in range(2 * heads)])
    gate_rows = jnp.swapaxes(small[8:32].reshape(3, 8, chan)[:, back_order], 1, 2)
    rms = jnp.sqrt(small[SMALL - 1, half : half + 1] / (count * model * devices))
    return (
        result.astype(bf16), token_grad, grad_ln, late.astype(f32), early[1], small[:taps],
        small[taps], folded[0], folded[1], folded[2], gate_rows, small[taps + 1, : 2 * heads][back_order], small[taps + 2],
        small[taps + 3], early[0], rms,
    )


def solution(mesh):
    rows_spec = P("dp", "tensor")
    cols = P(None, "tensor")
    vec = P("tensor")
    blocks = P("tensor", None, None)
    gates = P(None, "tensor", None)
    in_specs = (
        rows_spec, rows_spec, P(), cols, cols, cols, vec, blocks, blocks, blocks, gates, P(), vec, vec,
        P("tensor", None),
    )
    out_specs = (
        rows_spec, rows_spec, vec, cols, cols, cols, vec, blocks, blocks, blocks, gates, P(), vec, vec,
        P("tensor", None), P(),
    )
    return jax.shard_map(on_device, mesh=mesh, in_specs=in_specs, out_specs=out_specs, check_vma=False)
```

```python
import jax
import jax.numpy as jnp
from jax import lax
from jax.experimental import pallas as pl
from jax.experimental.pallas import tpu as pltpu
from jax.sharding import PartitionSpec as P

DH = 512
BLOCK = 64
QB = 4
SEQ_LEN = 8192
TILE = 256
GROUP = 256
HALO = 16
LANES = 128
NORM_EPS = 1e-05
PACK = DH + 16
WIDE = DH + 8
SMALL = 48
LIMIT = 60
FORTH = 2
BACK = 1
STRIP = 256
UNROLL = 4

f32 = jnp.float32
bf16 = jnp.bfloat16
highest = lax.Precision.HIGHEST


def mm(left, right):
    return lax.dot_general(left, right, (((1,), (0,)), ((), ())), preferred_element_type=f32)


def mm_tn(left, right):
    return lax.dot_general(left, right, (((0,), (0,)), ((), ())), preferred_element_type=f32)


def mm_nt(left, right):
    return lax.dot_general(left, right, (((1,), (1,)), ((), ())), preferred_element_type=f32)


def split2(value):
    high = value.astype(bf16)
    return high, (value - high.astype(f32)).astype(bf16)


def split3(value):
    high = value.astype(bf16)
    rest = value - high.astype(f32)
    mid = rest.astype(bf16)
    return high, mid, (rest - mid.astype(f32)).astype(bf16)


def sigmoid(value):
    return 1.0 / (1.0 + jnp.exp(-value))


def params(vmem_mib):
    return pltpu.CompilerParams(
        dimension_semantics=("arbitrary",), vmem_limit_bytes=vmem_mib * 1024 * 1024
    )


def cost(flops, moved):
    return pl.CostEstimate(flops=flops, bytes_accessed=moved, transcendentals=0)


def rows(width, tile=TILE, flip=0):
    if flip:
        return pl.BlockSpec((tile, width), lambda i: (flip - 1 - i, 0))
    return pl.BlockSpec((tile, width), lambda i: (i, 0))


def whole(*shape):
    return pl.BlockSpec(shape, lambda i: (0,) * len(shape))


smem = pl.BlockSpec(memory_space=pltpu.MemorySpace.SMEM)


def shape_of(*dims, dtype=f32):
    return jax.ShapeDtypeStruct(dims, dtype)


def normed_rows(x, ln):
    centered = x - jnp.mean(x, axis=1, keepdims=True)
    inverse = lax.rsqrt(jnp.mean(centered * centered, axis=1, keepdims=True) + NORM_EPS)
    return (centered * inverse * ln).astype(bf16)


def band_sum(value, coefs, reach):
    sums = [coef[reach : reach + 1] * value for coef in coefs]
    for offset in range(-reach, reach + 1):
        if offset != 0:
            moved = pltpu.roll(value, -offset % value.shape[1], 1)
            sums = [
                total + coef[reach + offset : reach + offset + 1] * moved for total, coef in zip(sums, coefs)
            ]
    return sums


def spread_coefs(maps_ref, coef_ref):
    count = maps_ref.shape[2]
    chan = count * QB
    column = lax.broadcasted_iota(jnp.int32, (count, chan), 1)
    block = lax.broadcasted_iota(jnp.int32, (count, chan), 0)
    apart = column - QB * block
    zero = jnp.zeros((1, count), f32)
    total = jnp.zeros((24, chan), f32)
    for out in range(QB):
        picked = []
        for m in range(3):
            for offset in range(1 - QB, QB + 1):
                inside = 0 <= out + offset < QB and offset < QB
                at = out * QB + out + offset
                picked.append(maps_ref[m, at : at + 1, :] if inside else zero)
        place = jnp.where(apart == out, 1.0, 0.0).astype(bf16)
        for term in split3(jnp.concatenate(picked, axis=0)):
            total = total + mm(term, place)
    for m in range(3):
        coef_ref[m] = total[8 * m : 8 * (m + 1)]


def both_halves(flag, own, other):
    is_low = flag[1] == 0
    return jnp.concatenate([jnp.where(is_low, own, other), jnp.where(is_low, other, own)], axis=1)


def first_kernel(
    flag, own_ref, other_ref, hown_ref, hother_ref, ln_ref, up_ref, cw_ref, cb_ref, maps_ref, gate_ref,
    normed_ref, inner_ref, conv_ref, active_ref, q_ref, k_ref, v_ref, pre_ref, coef_ref, pad_ref, gw_ref,
):
    step = pl.program_id(0)
    tile = own_ref.shape[0]

    @pl.when(step == 0)
    def _():
        halo = both_halves(flag, hown_ref[...].astype(f32), hother_ref[...].astype(f32))
        before = mm(normed_rows(halo, ln_ref[...]), up_ref[...])
        pad_ref[0:8, :] = jnp.where(flag[0] == 1, 0.0, before[HALO - 8 :, :])
        spread_coefs(maps_ref, coef_ref)
        gw_ref[...] = jnp.zeros_like(gw_ref)
        gw_ref[:, :, 0 : gate_ref.shape[2]] = gate_ref[...]

    x = both_halves(flag, own_ref[...].astype(f32), other_ref[...].astype(f32))
    normed = normed_rows(x, ln_ref[...])
    normed_ref[...] = normed
    inner = mm(normed, up_ref[...])
    inner_ref[...] = inner
    pad_ref[8:, :] = inner
    conv = cb_ref[...] + cw_ref[0:1, :] * inner
    for j in range(1, cw_ref.shape[0]):
        conv = conv + cw_ref[j : j + 1, :] * pad_ref[8 - j : 8 - j + tile, :]
    conv_ref[...] = conv
    pad_ref[0:8, :] = pad_ref[tile : tile + 8, :]
    active_ref[...] = conv * sigmoid(conv)
    reach = QB - 1
    for g in range(inner.shape[1] // LANES):
        part = slice(g * LANES, (g + 1) * LANES)
        query, key = band_sum(active_ref[:, part], (coef_ref[0, :, part], coef_ref[1, :, part]), reach)
        q_ref[:, part] = query.astype(bf16)
        k_ref[:, part] = key.astype(bf16)
        v_ref[:, part] = band_sum(inner_ref[:, part], (coef_ref[2, :, part],), reach)[0].astype(bf16)
    pre = mm(q_ref[...], gw_ref[0]) + mm(k_ref[...], gw_ref[1]) + mm(v_ref[...], gw_ref[2])
    pre_ref[...] = jnp.transpose(pre)[0:8, :]


def first_stage(flag, own, other, hown, hother, ln, up, cw, cb, maps, gate):
    count, half = own.shape
    model, chan = up.shape
    wide = (count, chan)
    return pl.pallas_call(
        first_kernel,
        grid=(count // TILE,),
        in_specs=[
            smem, rows(half), rows(half), whole(*hown.shape), whole(*hown.shape), whole(*ln.shape),
            whole(*up.shape), whole(*cw.shape), whole(*cb.shape), whole(*maps.shape), whole(*gate.shape),
        ],
        out_specs=[rows(model), rows(chan), rows(chan), rows(chan), rows(chan), rows(chan), rows(chan),
                   pl.BlockSpec((8, TILE), lambda i: (0, i)), whole(3, 8, chan)],
        out_shape=[shape_of(count, model, dtype=bf16), shape_of(*wide), shape_of(*wide), shape_of(*wide),
                   shape_of(*wide, dtype=bf16), shape_of(*wide, dtype=bf16), shape_of(*wide, dtype=bf16),
                   shape_of(8, count), shape_of(3, 8, chan)],
        scratch_shapes=[pltpu.VMEM((TILE + 8, chan), f32), pltpu.VMEM((3, chan, LANES), bf16)],
        compiler_params=params(LIMIT),
        cost_estimate=cost(2 * count * model * chan * 4, count * chan * 20),
        name="first",
    )(flag, own, other, hown, hother, ln, up, cw, cb, maps, gate)


def gates_kernel(place, own_ref, other_ref, bias_ref, row_ref, col_ref, total_ref):
    count = own_ref.shape[1]
    pre = own_ref[...] + other_ref[...] + bias_ref[...]
    low_half = place[0] == 0
    in_pre = jnp.where(low_half, pre[0:2], pre[2:4])
    forget = jnp.where(low_half, pre[4:6], pre[6:8])
    both = jnp.concatenate([in_pre, forget, in_pre, forget], axis=0)
    in8 = jnp.concatenate([in_pre] * 4, axis=0)
    f8 = jnp.concatenate([forget] * 4, axis=0)
    log_keep = jnp.minimum(f8, 0.0) - jnp.log1p(jnp.exp(-jnp.abs(f8)))
    lane = lax.broadcasted_iota(jnp.int32, f8.shape, 1)
    place_in = lane % BLOCK
    cum = log_keep
    dist = 1
    while dist < BLOCK:
        cum = cum + jnp.where(place_in >= dist, pltpu.roll(cum, dist, 1), 0.0)
        dist *= 2
    last = jnp.where(place_in == BLOCK - 1, cum, 0.0)
    dist = 1
    while dist < BLOCK:
        last = last + jnp.where(place_in < BLOCK - dist, pltpu.roll(last, count - dist, 1), 0.0)
        dist *= 2
    before = jnp.where(lane >= BLOCK, pltpu.roll(last, BLOCK, 1), 0.0)
    after = jnp.where(lane < count - BLOCK, pltpu.roll(last, count - BLOCK, 1), 0.0)
    dist = BLOCK
    while dist < count:
        before = before + jnp.where(lane >= dist, pltpu.roll(before, dist, 1), 0.0)
        after = after + jnp.where(lane < count - dist, pltpu.roll(after, count - dist, 1), 0.0)
        dist *= 2
    scale = DH ** (-0.5)
    keep = jnp.exp(last - cum + in8) * scale
    table = jnp.concatenate(
        [
            cum[0:2], jnp.exp(cum[0:2]), keep[0:2], jnp.exp(after[0:2]),
            jnp.exp(before[0:2]), jnp.exp(last[0:2]), in8[0:2], 1.0 / (1.0 + jnp.exp(f8[0:2])),
        ],
        axis=0,
    )
    tall = jnp.concatenate([table, jnp.zeros((LANES - 16, count), f32)], axis=0)
    col_ref[...] = jnp.transpose(tall)
    small = jnp.concatenate([cum[0:2], in8[0:2], cum[0:2], in8[0:2]], axis=0)
    for b in range(count // BLOCK):
        row_ref[b] = small[:, b * BLOCK : (b + 1) * BLOCK]
    total = (before + last)[:, count - 1 : count]
    total_ref[...] = jnp.broadcast_to(total, total_ref.shape)


def gates_stage(place, own, other, bias):
    count = own.shape[1]
    return pl.pallas_call(
        gates_kernel,
        grid=(1,),
        in_specs=[smem, whole(8, count), whole(8, count), whole(8, 1)],
        out_specs=[whole(count // BLOCK, 8, BLOCK), whole(count, LANES), whole(8, DH)],
        out_shape=[shape_of(count // BLOCK, 8, BLOCK), shape_of(count, LANES), shape_of(8, DH)],
        compiler_params=params(24),
        cost_estimate=cost(count * 1000, count * 600),
        name="gates",
    )(place, own, other, bias)


def write_pack(ref, state, vector, log_decay):
    ref[0:DH, :] = state.astype(bf16)
    terms = split3(vector) + split3(log_decay)
    tail = jnp.concatenate(
        [t.astype(f32) for t in terms] + [jnp.zeros((PACK - DH - 6, vector.shape[1]), f32)], axis=0
    )
    ref[DH:PACK, :] = tail.astype(bf16)


def write_wide(ref, state, vector, log_decay):
    ref[0:DH, :] = state
    ref[DH:WIDE, :] = jnp.concatenate(
        [vector, log_decay, jnp.zeros((WIDE - DH - 2, vector.shape[1]), f32)], axis=0
    )


def read_pack(ref):
    tail = ref[DH:PACK, :].astype(f32)
    return (
        ref[0:DH, :].astype(f32), (tail[0:1] + tail[1:2]) + tail[2:3], (tail[3:4] + tail[4:5]) + tail[5:6]
    )


def read_wide(ref):
    return ref[0:DH, :], ref[DH : DH + 1, :], ref[DH + 1 : DH + 2, :]


def joined(first, second):
    decay = jnp.exp(second[2])
    return decay * first[0] + second[0], decay * first[1] + second[1], first[2] + second[2]


def chosen(which, yes, no):
    return tuple(jnp.where(which, a, b) for a, b in zip(yes, no))


def pair_kernel(flag, own_ref, got_ref, send_ref, total_ref, lead_ref):
    own, got = read_wide(own_ref), read_pack(got_ref)
    is_lead = flag[0] == 1
    lead = chosen(is_lead, own, got)
    total = joined(lead, chosen(is_lead, got, own))
    write_wide(lead_ref, *lead)
    write_wide(total_ref, *total)
    write_pack(send_ref, *total)


def step_kernel(flag, total_ref, got_ref, before_ref, send_ref, new_total_ref, new_before_ref):
    total, got, before = read_wide(total_ref), read_pack(got_ref), read_wide(before_ref)
    upper = flag[0] == 1
    both = joined(chosen(upper, got, total), chosen(upper, total, got))
    write_wide(new_total_ref, *both)
    write_pack(send_ref, *both)
    write_wide(new_before_ref, *chosen(upper, joined(got, before), before))


def last_kernel(flag, got_ref, before_ref, lead_ref, send_ref, mine_ref):
    before, got = read_wide(before_ref), read_pack(got_ref)
    upper = flag[0] == 1
    is_lead = flag[1] == 1
    found = chosen(upper, joined(got, before), before)
    after = joined(found, read_wide(lead_ref))
    write_pack(send_ref, *chosen(is_lead, after, found))
    write_wide(mine_ref, *chosen(is_lead, found, after))


def pack_spec(wide, streams):
    return whole(WIDE if wide else PACK, DH // streams)


def pack_shape(wide, streams):
    return shape_of(WIDE if wide else PACK, DH // streams, dtype=f32 if wide else bf16)


def pack_specs(streams):
    return [pack_spec(1, streams)] * streams + [pack_spec(0, streams)] * streams


def pack_shapes(streams):
    return [pack_shape(1, streams)] * streams + [pack_shape(0, streams)] * streams


def small_call(kernel, name, ins, outs, flag, *packs):
    streams = DH // packs[0].shape[1]
    return pl.pallas_call(
        kernel,
        grid=(1,),
        in_specs=[smem] + [pack_spec(w, streams) for w in ins],
        out_specs=[pack_spec(w, streams) for w in outs],
        out_shape=[pack_shape(w, streams) for w in outs],
        compiler_params=params(24),
        cost_estimate=cost(PACK * DH * 8, PACK * DH * 3 * (len(ins) + len(outs))),
        name=name,
    )(flag, *packs)


def pass_states(own, send, place, span, stride, fillers=((), (), ())):
    devices = lax.axis_size("dp")

    def swap(value, bit):
        route = [((i // stride ^ bit) * stride + i % stride, i) for i in range(devices)]
        return lax.ppermute(value, "dp", route)

    def as_flag(*values):
        return jnp.stack([jnp.asarray(v).astype(jnp.int32) for v in values])

    is_lead = place % 2 == 0
    streams = range(len(own))
    done = []

    def exchange(packs, bit):
        got = [swap(pack, bit) for pack in packs]
        if bit < span and len(done) < len(fillers):
            got[-1], filler = lax.optimization_barrier((got[-1], fillers[len(done)]))
            done.append(filler)
        return got

    got = exchange(send, 1)
    found = [
        small_call(pair_kernel, "pair", (1, 0), (0, 1, 1), as_flag(is_lead), own[n], got[n]) for n in streams
    ]
    out, total, lead = zip(*found)
    before = [jnp.zeros_like(pack) for pack in own]
    bit = 2
    while bit < span:
        got = exchange(out, bit)
        upper = (place // bit) % 2 == 1
        if bit * 2 < span:
            found = [
                small_call(
                    step_kernel, "step", (1, 0, 1), (0, 1, 1), as_flag(upper), total[n], got[n], before[n]
                )
                for n in streams
            ]
            out, total, before = zip(*found)
        bit *= 2
    found = [
        small_call(
            last_kernel, "last", (0, 1, 1), (0, 1), as_flag(upper, is_lead), got[n], before[n], lead[n]
        )
        for n in streams
    ]
    out, mine = zip(*found)
    return mine + tuple(swap(pack, 1) for pack in out), done


def put_states(flag, packs, state_ref, vec_ref):
    streams = len(packs) // 2
    size = DH // streams
    for n in range(streams):
        mine, came = read_wide(packs[n]), read_pack(packs[streams + n])
        part = slice(n * size, (n + 1) * size)
        for h in range(2):
            found = chosen((flag[0] == 1) == (h == 0), mine, came)
            state_ref[h, :, part] = found[0]
            vec_ref[h : h + 1, part] = found[1]


def ends_kernel(flag, k_ref, v_ref, col_ref, total_ref, *refs):
    packs, (state_ref, vec_ref) = refs[: 2 * FORTH], refs[2 * FORTH :]
    step = pl.program_id(0)

    @pl.when(step == 0)
    def _():
        state_ref[...] = jnp.zeros_like(state_ref)
        vec_ref[...] = jnp.zeros_like(vec_ref)

    col = col_ref[...]
    for h in range(2):
        part = slice(h * DH, (h + 1) * DH)
        wide = k_ref[:, part].astype(f32)
        keep = col[:, 4 + h : 5 + h]
        later = col[:, 6 + h : 7 + h]
        kept = wide * keep
        high, low = split2(kept.astype(bf16).astype(f32) * later)
        value = v_ref[:, part]
        state_ref[h] += mm_tn(high, value) + mm_tn(low, value)
        vec_ref[h : h + 1, :] += jnp.sum(kept * later, axis=0, keepdims=True)

    @pl.when(step == pl.num_programs(0) - 1)
    def _():
        write_two(flag, state_ref, vec_ref, total_ref, packs)


def write_two(flag, state_ref, vec_ref, total_ref, packs):
    streams = len(packs) // 2
    size = DH // streams
    for n in range(streams):
        part = slice(n * size, (n + 1) * size)
        for h in range(2):
            found = (state_ref[h, :, part], vec_ref[h : h + 1, part], total_ref[h : h + 1, part])

            @pl.when(flag[0] == 1 - h)
            def _():
                write_wide(packs[n], *found)

            @pl.when(flag[0] == h)
            def _():
                write_pack(packs[streams + n], *found)


def ends_stage(flag, k, v, col, total):
    count, chan = k.shape
    return pl.pallas_call(
        ends_kernel,
        grid=(count // TILE,),
        in_specs=[smem, rows(chan), rows(chan), rows(LANES), whole(8, DH)],
        out_specs=pack_specs(FORTH),
        out_shape=pack_shapes(FORTH),
        scratch_shapes=[pltpu.VMEM((2, DH, DH), f32), pltpu.VMEM((8, DH), f32)],
        compiler_params=params(LIMIT),
        cost_estimate=cost(4 * count * chan * DH, count * chan * 4),
        name="ends",
    )(flag, k, v, col, total)


def damping_of(col, row, h):
    t = lax.broadcasted_iota(jnp.int32, (BLOCK, BLOCK), 0)
    s = lax.broadcasted_iota(jnp.int32, (BLOCK, BLOCK), 1)
    expo = col[:, h : h + 1] - row[h : h + 1, :] + row[2 + h : 3 + h, :]
    return jnp.exp(jnp.where(t >= s, expo, -1e30))


def lanes_of(*columns, offset=0):
    lane = lax.broadcasted_iota(jnp.int32, (columns[0].shape[0], LANES), 1) - offset
    out = jnp.zeros(lane.shape, f32)
    for i, column in enumerate(columns):
        out = jnp.where(lane == i, column, out)
    return out


def inside_kernel(q_ref, k_ref, v_ref, col_ref, row_ref, inside_ref, norm_ref):
    scale = DH ** (-0.5)

    def body(b, carry):
        r0 = pl.multiple_of(b * BLOCK, BLOCK)
        here = pl.ds(r0, BLOCK)
        col = col_ref[here, :]
        row = row_ref[b]
        sums = []
        for h in range(2):
            part = slice(h * DH, (h + 1) * DH)
            scores = mm_nt(q_ref[here, part], k_ref[here, part])
            weights = scores * damping_of(col, row, h) * scale
            inside_ref[here, part] = mm(weights.astype(bf16), v_ref[here, part])
            sums.append(jnp.sum(weights, axis=1, keepdims=True))
        norm_ref[here, :] = lanes_of(*sums)
        return carry

    lax.fori_loop(0, q_ref.shape[0] // BLOCK, body, 0)


def inside_stage(q, k, v, col, row):
    count, chan = q.shape
    return pl.pallas_call(
        inside_kernel,
        grid=(count // TILE,),
        in_specs=[rows(chan), rows(chan), rows(chan), rows(LANES),
                  pl.BlockSpec((TILE // BLOCK, 8, BLOCK), lambda i: (i, 0, 0))],
        out_specs=[rows(chan), rows(LANES)],
        out_shape=[shape_of(count, chan), shape_of(count, LANES)],
        compiler_params=params(32),
        cost_estimate=cost(4 * count * chan * BLOCK, count * chan * 10),
        name="inside",
    )(q, k, v, col, row)


def middle_kernel(flag, *refs):
    states, refs = refs[: 2 * FORTH], refs[2 * FORTH :]
    (
        q_ref, k_ref, v_ref, inside_ref, norm_ref, col_ref, gate_ref, dgated_ref, active_ref, group_ref,
        skip_ref, total_ref,
        gated_ref, gig_ref, sgrad_ref, nlow_ref, clow_ref, start_ref, nvec_ref, stat_ref, ggroup_ref, gskip_ref,
    ) = refs[:22]
    packs = refs[22 : 22 + 2 * BACK]
    state_ref, vec_ref, back_ref, bvec_ref, cross_ref, ncross_ref = refs[22 + 2 * BACK :]
    step = pl.program_id(0)

    @pl.when(step == 0)
    def _():
        put_states(flag, states, state_ref, vec_ref)
        back_ref[...] = jnp.zeros_like(back_ref)
        bvec_ref[...] = jnp.zeros_like(bvec_ref)
        ggroup_ref[...] = jnp.zeros_like(ggroup_ref)
        gskip_ref[...] = jnp.zeros_like(gskip_ref)

    def body(b, carry):
        r0 = pl.multiple_of(b * BLOCK, BLOCK)
        here = pl.ds(r0, BLOCK)
        col = col_ref[here, :]
        nvec_ref[b] = vec_ref[...]
        crosses = []
        for h in range(2):
            part = slice(h * DH, (h + 1) * DH)
            query = q_ref[here, part]
            state = state_ref[h]
            state_low = state.astype(bf16)
            start_ref[h, b] = state_low
            cross_ref[here, part] = mm(query, state_low)
            vec = vec_ref[h : h + 1, :]
            crosses.append(jnp.sum(query.astype(f32) * vec, axis=1, keepdims=True))
            kept = k_ref[here, part].astype(f32) * col[:, 4 + h : 5 + h]
            decay = col[0:1, 10 + h : 11 + h]
            state_ref[h] = decay * state + mm_tn(kept.astype(bf16), v_ref[here, part])
            vec_ref[h : h + 1, :] = decay * vec + jnp.sum(kept, axis=0, keepdims=True)
        ncross_ref[here, :] = lanes_of(*crosses)
        return carry

    lax.fori_loop(0, q_ref.shape[0] // BLOCK, body, 0, unroll=UNROLL)

    def strip(i, carry):
        here = pl.ds(pl.multiple_of(i * STRIP, STRIP), STRIP)
        col = col_ref[here, :]
        norms = norm_ref[here, :]
        stats = []
        for h in range(2):
            part = slice(h * DH, (h + 1) * DH)
            growth = col[:, 2 + h : 3 + h]
            carried = growth * cross_ref[here, part]
            norm_cross = growth * ncross_ref[here, h : h + 1]
            numer = inside_ref[here, part] + carried
            normal = norms[:, h : h + 1] + norm_cross
            over = 1.0 / jnp.maximum(jnp.abs(normal), 1.0)
            mixed = numer * over
            centered = mixed - jnp.mean(mixed, axis=1, keepdims=True)
            inverse = lax.rsqrt(jnp.mean(centered * centered, axis=1, keepdims=True) + NORM_EPS)
            ghat = centered * inverse
            active = active_ref[here, part]
            gate = gate_ref[here, part]
            sig = sigmoid(gate)
            gact = gate * sig
            gweight = group_ref[0:1, part]
            gstate = ghat * gweight + skip_ref[0:1, part] * active
            gated_ref[here, part] = (gstate * gact).astype(bf16)
            dgated = dgated_ref[here, part]
            sgrad = dgated * gact
            sgrad_ref[here, part] = sgrad
            gig_ref[here, part] = (dgated * gstate * sig * (1.0 + gate * (1.0 - sig))).astype(bf16)
            gskip_ref[0:1, part] += jnp.sum(sgrad * active, axis=0, keepdims=True)
            ggroup_ref[0:1, part] += jnp.sum(sgrad * ghat, axis=0, keepdims=True)
            g = sgrad * gweight
            mgrad = inverse * (
                g - jnp.mean(g, axis=1, keepdims=True) - ghat * jnp.mean(g * ghat, axis=1, keepdims=True)
            )
            ngrad = mgrad * over
            down = -jnp.sum(mgrad * mixed, axis=1, keepdims=True) * over
            normal_grad = jnp.where(normal > 1.0, down, jnp.where(normal < -1.0, -down, 0.0))
            nlow_ref[here, part] = ngrad.astype(bf16)
            clow_ref[here, part] = (growth * ngrad).astype(bf16)
            moved = jnp.sum(ngrad * carried, axis=1, keepdims=True) + normal_grad * norm_cross
            stats.append((normal_grad, moved))
            scaled = col[:, 8 + h : 9 + h] * growth * normal_grad
            bvec_ref[h : h + 1, :] += jnp.sum(scaled * q_ref[here, part].astype(f32), axis=0, keepdims=True)
        stat_ref[here, :] = lanes_of(stats[0][0], stats[1][0], stats[0][1], stats[1][1])
        return carry

    lax.fori_loop(0, q_ref.shape[0] // STRIP, strip, 0)
    for h in range(2):
        part = slice(h * DH, (h + 1) * DH)
        high, low = split2(clow_ref[:, part].astype(f32) * col_ref[:, 8 + h : 9 + h])
        query = q_ref[:, part]
        back_ref[h] += mm_tn(query, high) + mm_tn(query, low)

    @pl.when(step == pl.num_programs(0) - 1)
    def _():
        write_two(flag, back_ref, bvec_ref, total_ref, packs)


def middle_stage(flag, states, q, k, v, inside, norms, col, gate, dgated, active, group, skip, total):
    count, chan = q.shape
    blocks = count // BLOCK
    per = TILE // BLOCK
    return pl.pallas_call(
        middle_kernel,
        grid=(count // TILE,),
        in_specs=[smem, *pack_specs(FORTH), rows(chan), rows(chan), rows(chan),
                  rows(chan), rows(LANES), rows(LANES), rows(chan), rows(chan), rows(chan), whole(1, chan), whole(1, chan), whole(8, DH)],
        out_specs=[rows(chan), rows(chan), rows(chan), rows(chan), rows(chan),
                   pl.BlockSpec((2, per, DH, DH), lambda i: (0, i, 0, 0)),
                   pl.BlockSpec((per, 8, DH), lambda i: (i, 0, 0)),
                   rows(LANES), whole(8, chan), whole(8, chan), *pack_specs(BACK)],
        out_shape=[shape_of(count, chan, dtype=bf16), shape_of(count, chan, dtype=bf16), shape_of(count, chan),
                   shape_of(count, chan, dtype=bf16), shape_of(count, chan, dtype=bf16),
                   shape_of(2, blocks, DH, DH, dtype=bf16), shape_of(blocks, 8, DH), shape_of(count, LANES),
                   shape_of(8, chan), shape_of(8, chan),
                   *pack_shapes(BACK)],
        scratch_shapes=[pltpu.VMEM((2, DH, DH), f32), pltpu.VMEM((8, DH), f32),
                        pltpu.VMEM((2, DH, DH), f32), pltpu.VMEM((8, DH), f32),
                        pltpu.VMEM((TILE, chan), f32), pltpu.VMEM((TILE, LANES), f32)],
        compiler_params=params(LIMIT),
        cost_estimate=cost(10 * count * chan * DH, count * chan * 40),
        name="middle",
    )(flag, *states, q, k, v, inside, norms, col, gate, dgated, active, group, skip, total)


def back_kernel(flag, *refs):
    states, refs = refs[: 2 * BACK], refs[2 * BACK :]
    (
        q_ref, k_ref, v_ref, nlow_ref, clow_ref, start_ref, nvec_ref, col_ref, row_ref, stat_ref,
        qg_ref, kg_ref, vg_ref, pre_ref,
        state_ref, vec_ref,
    ) = refs
    scale = DH ** (-0.5)

    @pl.when(pl.program_id(0) == 0)
    def _():
        put_states(flag, states, state_ref, vec_ref)

    u = lax.broadcasted_iota(jnp.int32, (BLOCK, BLOCK), 0)
    t = lax.broadcasted_iota(jnp.int32, (BLOCK, BLOCK), 1)
    from_here = jnp.where(t >= u, 1.0, 0.0)
    at_end = lax.broadcasted_iota(jnp.int32, (BLOCK, 1), 0) == BLOCK - 1
    per = q_ref.shape[0] // BLOCK

    def body(i, carry):
        b = per - 1 - i
        r0 = pl.multiple_of(b * BLOCK, BLOCK)
        here = pl.ds(r0, BLOCK)
        col = col_ref[here, :]
        row = row_ref[b]
        stat = stat_ref[here, :]
        starts = nvec_ref[b]
        in_cols, cum_cols = [], []
        for h in range(2):
            part = slice(h * DH, (h + 1) * DH)
            query, key, value = q_ref[here, part], k_ref[here, part], v_ref[here, part]
            numer_low, cross_low = nlow_ref[here, part], clow_ref[here, part]
            growth = col[:, 2 + h : 3 + h]
            keep = col[:, 4 + h : 5 + h]
            decay = col[0:1, 10 + h : 11 + h]
            normal_grad = stat[:, h : h + 1]
            moved = stat[:, 2 + h : 3 + h]
            end = state_ref[h]
            end_low = end.astype(bf16)
            end_vec = vec_ref[h : h + 1, :]
            start_low = start_ref[h, b]
            start_vec = starts[h : h + 1, :]
            damping = damping_of(col, row, h)
            scores = mm_nt(query, key)
            weights_low = (scores * damping * scale).astype(bf16)
            weights_grad = mm_nt(numer_low, value) + normal_grad
            damped = weights_grad * scale * damping
            scores_low = damped.astype(bf16)
            expo = damped * scores
            pull = growth * normal_grad
            qg_ref[here, part] = mm(scores_low, key) + mm_nt(cross_low, start_low) + pull * start_vec
            wide = key.astype(f32)
            kept_low = (wide * keep).astype(bf16)
            key_total = mm_nt(value, end_low) + end_vec
            kg_ref[here, part] = mm_tn(scores_low, query) + keep * key_total
            vg_ref[here, part] = mm_tn(weights_low, numer_low) + mm(kept_low, end_low)
            keep_grad = keep * jnp.sum(wide * key_total, axis=1, keepdims=True)
            held = jnp.sum(end * start_low.astype(f32), axis=0, keepdims=True) + end_vec * start_vec
            last_grad = decay * jnp.sum(held, axis=1, keepdims=True) + jnp.sum(keep_grad, axis=0, keepdims=True)
            over_t = jnp.sum(jnp.transpose(expo), axis=1, keepdims=True)
            cum_grad = jnp.sum(expo, axis=1, keepdims=True) - over_t + moved - keep_grad
            cum_cols.append(cum_grad + jnp.where(at_end, last_grad, 0.0))
            in_cols.append(over_t + keep_grad)
            state_ref[h] = decay * end + mm_tn(query, cross_low)
            vec_ref[h : h + 1, :] = decay * end_vec + jnp.sum(pull * query.astype(f32), axis=0, keepdims=True)
        sums = lax.dot_general(
            from_here, lanes_of(*cum_cols), (((1,), (0,)), ((), ())), precision=highest, preferred_element_type=f32
        )
        forget = [sums[:, h : h + 1] * col[:, 14 + h : 15 + h] for h in range(2)]
        pre_ref[here, :] = lanes_of(*in_cols, *forget, offset=4 * flag[1]).astype(bf16)
        return carry

    lax.fori_loop(0, per, body, 0, unroll=2)


def back_stage(flag, states, q, k, v, nlow, clow, start, nvec, col, row, stat):
    count, chan = q.shape
    tiles = count // TILE
    per = TILE // BLOCK
    flip = rows(chan, flip=tiles)
    thin = rows(LANES, flip=tiles)
    return pl.pallas_call(
        back_kernel,
        grid=(tiles,),
        in_specs=[smem, *pack_specs(BACK), flip, flip, flip, flip, flip,
                  pl.BlockSpec((2, per, DH, DH), lambda i: (0, tiles - 1 - i, 0, 0)),
                  pl.BlockSpec((per, 8, DH), lambda i: (tiles - 1 - i, 0, 0)), thin,
                  pl.BlockSpec((per, 8, BLOCK), lambda i: (tiles - 1 - i, 0, 0)), thin],
        out_specs=[flip, flip, flip, thin],
        out_shape=[shape_of(count, chan)] * 3 + [shape_of(count, LANES, dtype=bf16)],
        scratch_shapes=[pltpu.VMEM((2, DH, DH), f32), pltpu.VMEM((8, DH), f32)],
        compiler_params=params(LIMIT),
        cost_estimate=cost(14 * count * chan * DH, count * chan * 30),
        name="back",
    )(flag, *states, q, k, v, nlow, clow, start, nvec, col, row, stat)


def band_back(value, map_hi, map_lo):
    high, low = value
    found = []
    for g in range(high.shape[1] // GROUP):
        part = slice(g * GROUP, (g + 1) * GROUP)
        found.append(
            mm_nt(high[:, part], map_hi[g])
            + (mm_nt(low[:, part], map_hi[g]) + mm_nt(high[:, part], map_lo[g]))
        )
    return jnp.concatenate(found, axis=1)


def conv_grad_of(active_grad, conv):
    sig = sigmoid(conv)
    return active_grad * sig * (1.0 + conv * (1.0 - sig))


def edge_kernel(qg_ref, kg_ref, pre_ref, other_ref, sgrad_ref, conv_ref, skip_ref, coef_ref, gwt_ref, out_ref):
    pre = pre_ref[...] + other_ref[...]
    query_all = qg_ref[...] + mm(pre, gwt_ref[0])
    key_all = kg_ref[...] + mm(pre, gwt_ref[1])
    reach = QB - 1
    for g in range(query_all.shape[1] // LANES):
        part = slice(g * LANES, (g + 1) * LANES)
        total = sgrad_ref[:, part] * skip_ref[:, part]
        for m, value in enumerate((query_all[:, part], key_all[:, part])):
            for offset in range(-reach, reach + 1):
                total = total + pltpu.roll(
                    coef_ref[m, reach - offset : reach - offset + 1, part] * value, -offset % LANES, 1
                )
        out_ref[:, part] = conv_grad_of(total, conv_ref[:, part])[0:8, :]


def edge_stage(qg, kg, pre, other, sgrad, conv, skip, coefs, gwt):
    chan = qg.shape[1]
    top = rows(chan, HALO)
    return pl.pallas_call(
        edge_kernel,
        grid=(1,),
        in_specs=[top, top, rows(LANES, HALO), rows(LANES, HALO), top, top, whole(*skip.shape), whole(*coefs.shape),
                  whole(*gwt.shape)],
        out_specs=whole(8, chan),
        out_shape=shape_of(8, chan),
        compiler_params=params(LIMIT),
        cost_estimate=cost(10**7, 10**6),
        name="edge",
    )(qg, kg, pre, other, sgrad, conv, skip, coefs, gwt)


def maps_kernel(
    flag, qg_ref, kg_ref, vg_ref, mine_ref, other_ref, sgrad_ref, conv_ref, inner_ref, q_ref, k_ref, v_ref, edge_ref,
    skip_ref, cw_ref, coef_ref, gwt_ref, ggroup_ref, gskip_ref,
    low_ref, small_ref,
    pad_ref, hi_ref, lo_ref, gmap_ref,
):
    tile, chan = qg_ref.shape
    groups = chan // GROUP
    reach = QB - 1

    @pl.when(pl.program_id(0) == 0)
    def _():
        pad_ref[tile : tile + 8, :] = jnp.where(flag[0] == 1, 0.0, edge_ref[...])
        gmap_ref[...] = jnp.zeros_like(gmap_ref)
        small_ref[...] = jnp.zeros_like(small_ref)
        apart = lax.broadcasted_iota(jnp.int32, (GROUP, GROUP), 0) - lax.broadcasted_iota(
            jnp.int32, (GROUP, GROUP), 1
        )
        for m in range(3):
            for g in range(groups):
                dense = jnp.zeros((GROUP, GROUP), f32)
                for offset in range(-reach, reach + 1):
                    coef = coef_ref[m, reach + offset : reach + offset + 1, g * GROUP : (g + 1) * GROUP]
                    dense = jnp.where(apart == offset, coef, dense)
                hi_ref[m, g], lo_ref[m, g] = split2(dense)

    pre = mine_ref[...] + other_ref[...]
    conv = conv_ref[...]
    inner = inner_ref[...]
    query_all = split2(qg_ref[...] + mm(pre, gwt_ref[0]))
    key_all = split2(kg_ref[...] + mm(pre, gwt_ref[1]))
    value_all = split2(vg_ref[...] + mm(pre, gwt_ref[2]))
    active = split2(conv * sigmoid(conv))
    inner2 = split2(inner)
    for m, (grads, acts) in enumerate(((query_all, active), (key_all, active), (value_all, inner2))):
        for g in range(groups):
            part = slice(g * GROUP, (g + 1) * GROUP)
            gmap_ref[m, g] += mm_tn(grads[0][:, part], acts[0][:, part]) + (
                mm_tn(grads[1][:, part], acts[0][:, part]) + mm_tn(grads[0][:, part], acts[1][:, part])
            )
    active_grad = (
        sgrad_ref[...] * skip_ref[...]
        + band_back(query_all, hi_ref[0], lo_ref[0])
        + band_back(key_all, hi_ref[1], lo_ref[1])
    )
    grad = conv_grad_of(active_grad, conv)
    pad_ref[0:tile, :] = grad
    taps = cw_ref.shape[0]
    small_ref[taps : taps + 1, :] += jnp.sum(grad, axis=0, keepdims=True)
    inner_grad = band_back(value_all, hi_ref[2], lo_ref[2])
    for j in range(cw_ref.shape[0]):
        moved = pad_ref[j : j + tile, :]
        inner_grad = inner_grad + cw_ref[j : j + 1, :] * moved
        small_ref[j : j + 1, :] += jnp.sum(moved * inner, axis=0, keepdims=True)
    low_ref[...] = inner_grad.astype(bf16)
    pad_ref[tile : tile + 8, :] = pad_ref[0:8, :]
    for m, ref in enumerate((q_ref, k_ref, v_ref)):
        small_ref[8 * (m + 1) : 8 * (m + 2), :] += mm_tn(pre, ref[...])[0:8, :]
    small_ref[taps + 1 : taps + 2, 0:LANES] += jnp.sum(pre.astype(f32), axis=0, keepdims=True)

    @pl.when(pl.program_id(0) == pl.num_programs(0) - 1)
    def _():
        r = lax.broadcasted_iota(jnp.int32, (GROUP, GROUP), 0)
        c = lax.broadcasted_iota(jnp.int32, (GROUP, GROUP), 1)
        pick = jnp.where(
            lax.broadcasted_iota(jnp.int32, (8, GROUP), 1) % QB == lax.broadcasted_iota(jnp.int32, (8, GROUP), 0),
            1.0, 0.0,
        )
        for m in range(3):
            for g in range(groups):
                held = jnp.where(r // QB == c // QB, gmap_ref[m, g], 0.0)
                found = lax.dot_general(
                    pick, held, (((1,), (1,)), ((), ())), precision=highest, preferred_element_type=f32
                )
                small_ref[32 + QB * m : 32 + QB * (m + 1), g * GROUP : (g + 1) * GROUP] = found[0:QB]
        small_ref[taps + 2 : taps + 3, :] = ggroup_ref[0:1, :]
        small_ref[taps + 3 : taps + 4, :] = gskip_ref[0:1, :]


def maps_stage(flag, qg, kg, vg, pre, other, sgrad, conv, inner, q, k, v, edge, skip, cw, coefs, gwt, ggroup, gskip):
    count, chan = qg.shape
    tiles = count // TILE
    flip = rows(chan, flip=tiles)
    groups = chan // GROUP
    return pl.pallas_call(
        maps_kernel,
        grid=(tiles,),
        in_specs=[smem, flip, flip, flip, rows(LANES, flip=tiles), rows(LANES, flip=tiles), flip, flip, flip, flip,
                  flip, flip,
                  whole(8, chan), whole(*skip.shape), whole(*cw.shape), whole(*coefs.shape), whole(*gwt.shape),
                  whole(8, chan), whole(8, chan)],
        out_specs=[flip, whole(SMALL, chan)],
        out_shape=[shape_of(count, chan, dtype=bf16), shape_of(SMALL, chan)],
        scratch_shapes=[pltpu.VMEM((TILE + 8, chan), f32), pltpu.VMEM((3, groups, GROUP, GROUP), bf16),
                        pltpu.VMEM((3, groups, GROUP, GROUP), bf16), pltpu.VMEM((3, groups, GROUP, GROUP), f32)],
        compiler_params=params(LIMIT),
        cost_estimate=cost(20 * count * chan * GROUP, count * chan * 32),
        name="maps",
    )(flag, qg, kg, vg, pre, other, sgrad, conv, inner, q, k, v, edge, skip, cw, coefs, gwt, ggroup, gskip)


def exchanged(value, bit):
    route = [(i ^ bit, i) for i in range(lax.axis_size("dp"))]
    return lax.ppermute(value, "dp", route)


def halved(value, bit):
    mine = (lax.axis_index("dp") // bit) % 2
    width = value.shape[1]
    size = value.shape[0] // 2
    send = lax.dynamic_slice(value, ((1 - mine) * size, 0), (size, width)).astype(bf16)
    keep = lax.dynamic_slice(value, (mine * size, 0), (size, width))
    return keep + exchanged(send, bit).astype(f32)


def joined_halves(value, bit):
    first = (lax.axis_index("dp") // bit) % 2 == 0
    other = exchanged(value, bit)
    return jnp.concatenate([jnp.where(first, value, other), jnp.where(first, other, value)], axis=0)


def finished(pair, bits):
    value = jnp.concatenate(pair, axis=0)
    for bit in bits[2:]:
        value = halved(value, bit)
    value = value.astype(bf16)
    for bit in reversed(bits[2:]):
        value = joined_halves(value, bit)
    size = value.shape[0] // 2
    one, two = joined_halves(value[:size], bits[1]), joined_halves(value[size:], bits[0])
    return jnp.concatenate([joined_halves(one, bits[0]), joined_halves(two, bits[1])], axis=0)


def half_products(pairs, side):
    found = []
    for left, right in pairs:
        size = left.shape[1] // 2
        found.append(mm_tn(lax.dynamic_slice_in_dim(left, side * size, size, axis=1), right))
    return found


def shares(value):
    devices = lax.axis_size("dp")
    groups = [[i for i in range(devices) if i & 5 == low] for low in (0, 1, 4, 5)]
    return lax.psum_scatter(value, "dp", scatter_dimension=0, axis_index_groups=groups, tiled=True)


def from_shares(every):
    devices = lax.axis_size("dp")
    size, width = every.shape[0] // devices, every.shape[1]
    every = every.reshape(devices // 8, 2, 2, 2, size, width)
    return [jnp.transpose(every[:, i], (2, 0, 1, 3, 4)).reshape(-1, width).astype(f32) for i in range(2)]


def all_sum(value, bits):
    for bit in bits:
        value = value + exchanged(value, bit)
    return value


def map_rows(weight):
    return weight.reshape(weight.shape[0], -1).T


def on_device(
    tokens, cotangent, ln_weight, up_inner, up_gate, conv_weight, conv_bias, query_weight, key_weight,
    value_weight, gate_weight, gate_bias, group_weight, skip_weight, down_weight,
):
    count = tokens.shape[0]
    chan = up_inner.shape[1]
    model = up_inner.shape[0]
    half = tokens.shape[1]
    band = query_weight.shape[1]
    span = SEQ_LEN // count
    devices = lax.axis_size("dp")
    stride = devices // span
    t_place = lax.axis_index("tensor")
    piece = lax.axis_index("dp") // stride
    low_half = t_place == 0

    def across(value):
        return lax.ppermute(value, "tensor", [(0, 1), (1, 0)])

    def side_by_side(own, other):
        return jnp.concatenate([jnp.where(low_half, own, other), jnp.where(low_half, other, own)], axis=1)

    def along(value, distance):
        route = [(i - distance, i) for i in range(devices) if 0 <= i - distance < devices]
        return lax.ppermute(value, "dp", route)

    def flags(*values):
        return jnp.stack([jnp.asarray(v).astype(jnp.int32) for v in values])

    halo = along(tokens[count - HALO :], stride)
    other_tokens = across(tokens)
    full = side_by_side(tokens, other_tokens)
    full_cot = side_by_side(cotangent, across(cotangent))

    maps = jnp.stack([map_rows(w) for w in (query_weight, key_weight, value_weight)])
    heads = gate_bias.shape[0] // 2
    local = heads // 2
    order = [kind * heads + t * local + j for t in range(2) for kind in range(2) for j in range(local)]
    gwt = jnp.pad(
        jnp.swapaxes(gate_weight, 1, 2)[:, jnp.array(order)], ((0, 0), (0, LANES - 2 * heads), (0, 0))
    )

    normed, inner, conv, active, q, k, v, pre, coefs = first_stage(
        flags(piece == 0, t_place), tokens, other_tokens, halo, across(halo), ln_weight[None], up_inner,
        conv_weight, conv_bias[None], maps, gate_weight,
    )
    row, col, total = gates_stage(flags(t_place), pre, across(pre), gate_bias[:, None])
    even = flags(piece % 2 == 0)
    packs = ends_stage(even, k, v, col, total)
    gate_in = mm(normed, up_gate)
    dgated = mm_nt(full_cot, down_weight)
    inside, norms = inside_stage(q, k, v, col, row)
    states, done = pass_states(
        packs[:FORTH], packs[FORTH:], piece, span, stride, ((inside, norms), (dgated,), (gate_in,))
    )
    (inside, norms), (dgated,), (gate_in,) = done
    (
        gated, gate_in_grad, sgrad, nlow, clow, start, nvec, stat, ggroup, gskip, *packs
    ) = middle_stage(
        even, states, q, k, v, inside, norms, col, gate_in, dgated, active, group_weight[None],
        skip_weight[None], total,
    )
    pairs = ((gated, full_cot), (normed, gate_in_grad))
    lowest = lax.axis_index("dp") % 2
    sends = [value.astype(bf16) for value in half_products(pairs, 1 - lowest)]
    keeps = [
        value + exchanged(sent, 1).astype(f32) for value, sent in zip(half_products(pairs, lowest), sends)
    ]
    both = jnp.concatenate(keeps, axis=0)
    branch = mm(gated, down_weight)
    second = (lax.axis_index("dp") // 4) % 2
    away = lax.dynamic_slice_in_dim(both, (1 - second) * (model // 2), model // 2, axis=0).astype(bf16)
    states, done = pass_states(
        packs[:BACK], packs[BACK:], span - 1 - piece, span, stride, (sends, (branch,), (both, away)))
    _, (branch,), (both, away) = done
    both = lax.dynamic_slice_in_dim(both, second * (model // 2), model // 2, axis=0)
    both = both + exchanged(away, 4).astype(f32)
    states, both = lax.optimization_barrier((states, both))
    share = shares(both)

    bits = [1 << n for n in range(devices.bit_length() - 1)]
    keep_half = lax.dynamic_slice_in_dim(branch, t_place * half, half, axis=1)
    send_half = lax.dynamic_slice_in_dim(branch, (1 - t_place) * half, half, axis=1)
    result = tokens.astype(f32) + (keep_half + across(send_half))
    squares = jnp.sum(result * result)
    gate_part = mm_nt(gate_in_grad, up_gate)

    qg, kg, vg, pre_own = back_stage(flags(piece % 2 == 0, t_place), states, q, k, v, nlow, clow, start, nvec, col, row, stat)
    pre_other = across(pre_own)
    skip = skip_weight[None]
    edge = along(edge_stage(qg, kg, pre_own, pre_other, sgrad, conv, skip, coefs, gwt), -stride)
    edge, share = lax.optimization_barrier((edge, share.astype(bf16)))
    every = lax.all_gather(share, "dp", axis=0, tiled=True)
    inner_low, small = maps_stage(
        flags(piece == span - 1), qg, kg, vg, pre_own, pre_other, sgrad, conv, inner, q, k, v, edge, skip, conv_weight,
        coefs, gwt, ggroup, gskip,
    )
    grad_up_inner, inner_low = lax.optimization_barrier((mm_tn(normed, inner_low), inner_low))
    late = [halved(grad_up_inner[: model // 2], bits[0]), halved(grad_up_inner[model // 2 :], bits[1])]
    part = gate_part + mm_nt(inner_low, up_inner)
    wide = full.astype(f32)
    centered = wide - jnp.mean(wide, axis=1, keepdims=True)
    inverse = lax.rsqrt(jnp.mean(centered * centered, axis=1, keepdims=True) + NORM_EPS)
    xhat = centered * inverse
    scaled = part * ln_weight
    mean_h = jnp.mean(scaled, axis=1)
    mean_hx = jnp.mean(scaled * xhat, axis=1)
    means = jnp.stack([mean_h, mean_hx])
    late, part, means = lax.optimization_barrier((late, part, means))
    late = [halved(late[0], bits[1]), halved(late[1], bits[0])]
    means = means + across(means)
    own_part = lax.dynamic_slice_in_dim(part, t_place * half, half, axis=1)
    send_part = lax.dynamic_slice_in_dim(part, (1 - t_place) * half, half, axis=1)
    normed_grad = own_part + across(send_part)
    xhat_own = lax.dynamic_slice_in_dim(xhat, t_place * half, half, axis=1)
    ln_own = lax.dynamic_slice_in_dim(ln_weight, t_place * half, half, axis=0)
    token_grad = (
        inverse * (normed_grad * ln_own - means[0][:, None] - xhat_own * means[1][:, None])
        + cotangent.astype(f32)
    )
    grad_ln = jnp.sum(normed_grad * xhat_own, axis=0)

    late, grad_ln, token_grad, every = lax.optimization_barrier((late, grad_ln, token_grad, every))
    last = jnp.concatenate([grad_ln, jnp.broadcast_to(squares + across(squares), (LANES,))])
    small = all_sum(small + jnp.pad(last[None], ((SMALL - 1, 0), (0, chan - half - LANES))), bits)
    grad_ln = small[SMALL - 1, :half]
    late = finished(late, bits)
    early = from_shares(every)
    taps = conv_weight.shape[0]
    folded = small[32 : 32 + 3 * band].reshape(3, band, chan // band, band)
    folded = jnp.transpose(folded, (0, 2, 3, 1))
    back_order = jnp.array([order.index(c) for c in range(2 * heads)])
    gate_rows = jnp.swapaxes(small[8:32].reshape(3, 8, chan)[:, back_order], 1, 2)
    rms = jnp.sqrt(small[SMALL - 1, half : half + 1] / (count * model * devices))
    return (
        result.astype(bf16), token_grad, grad_ln, late.astype(f32), early[1], small[:taps],
        small[taps], folded[0], folded[1], folded[2], gate_rows, small[taps + 1, : 2 * heads][back_order], small[taps + 2],
        small[taps + 3], early[0], rms,
    )


def solution(mesh):
    rows_spec = P("dp", "tensor")
    cols = P(None, "tensor")
    vec = P("tensor")
    blocks = P("tensor", None, None)
    gates = P(None, "tensor", None)
    in_specs = (
        rows_spec, rows_spec, P(), cols, cols, cols, vec, blocks, blocks, blocks, gates, P(), vec, vec,
        P("tensor", None),
    )
    out_specs = (
        rows_spec, rows_spec, vec, cols, cols, cols, vec, blocks, blocks, blocks, gates, P(), vec, vec,
        P("tensor", None), P(),
    )
    return jax.shard_map(on_device, mesh=mesh, in_specs=in_specs, out_specs=out_specs, check_vma=False)
```

```python
import jax
import jax.numpy as jnp
from jax import lax
from jax.experimental import pallas as pl
from jax.experimental.pallas import tpu as pltpu
from jax.sharding import PartitionSpec as P

DH = 512
BLOCK = 64
QB = 4
SEQ_LEN = 8192
TILE = 256
GROUP = 256
HALO = 16
LANES = 128
NORM_EPS = 1e-05
PACK = DH + 16
WIDE = DH + 8
SMALL = 48
LIMIT = 60
FORTH = 2
BACK = 1
STRIP = 256
UNROLL = 4

f32 = jnp.float32
bf16 = jnp.bfloat16
highest = lax.Precision.HIGHEST


def mm(left, right):
    return lax.dot_general(left, right, (((1,), (0,)), ((), ())), preferred_element_type=f32)


def mm_tn(left, right):
    return lax.dot_general(left, right, (((0,), (0,)), ((), ())), preferred_element_type=f32)


def mm_nt(left, right):
    return lax.dot_general(left, right, (((1,), (1,)), ((), ())), preferred_element_type=f32)


def split2(value):
    high = value.astype(bf16)
    return high, (value - high.astype(f32)).astype(bf16)


def split3(value):
    high = value.astype(bf16)
    rest = value - high.astype(f32)
    mid = rest.astype(bf16)
    return high, mid, (rest - mid.astype(f32)).astype(bf16)


def sigmoid(value):
    return 1.0 / (1.0 + jnp.exp(-value))


def params(vmem_mib):
    return pltpu.CompilerParams(
        dimension_semantics=("arbitrary",), vmem_limit_bytes=vmem_mib * 1024 * 1024
    )


def cost(flops, moved):
    return pl.CostEstimate(flops=flops, bytes_accessed=moved, transcendentals=0)


def rows(width, tile=TILE, flip=0):
    if flip:
        return pl.BlockSpec((tile, width), lambda i: (flip - 1 - i, 0))
    return pl.BlockSpec((tile, width), lambda i: (i, 0))


def whole(*shape):
    return pl.BlockSpec(shape, lambda i: (0,) * len(shape))


smem = pl.BlockSpec(memory_space=pltpu.MemorySpace.SMEM)


def shape_of(*dims, dtype=f32):
    return jax.ShapeDtypeStruct(dims, dtype)


def normed_rows(x, ln):
    centered = x - jnp.mean(x, axis=1, keepdims=True)
    inverse = lax.rsqrt(jnp.mean(centered * centered, axis=1, keepdims=True) + NORM_EPS)
    return (centered * inverse * ln).astype(bf16)


def band_sum(value, coefs, reach):
    sums = [coef[reach : reach + 1] * value for coef in coefs]
    for offset in range(-reach, reach + 1):
        if offset != 0:
            moved = pltpu.roll(value, -offset % value.shape[1], 1)
            sums = [
                total + coef[reach + offset : reach + offset + 1] * moved for total, coef in zip(sums, coefs)
            ]
    return sums


def spread_coefs(maps_ref, coef_ref):
    count = maps_ref.shape[2]
    chan = count * QB
    column = lax.broadcasted_iota(jnp.int32, (count, chan), 1)
    block = lax.broadcasted_iota(jnp.int32, (count, chan), 0)
    apart = column - QB * block
    zero = jnp.zeros((1, count), f32)
    total = jnp.zeros((24, chan), f32)
    for out in range(QB):
        picked = []
        for m in range(3):
            for offset in range(1 - QB, QB + 1):
                inside = 0 <= out + offset < QB and offset < QB
                at = out * QB + out + offset
                picked.append(maps_ref[m, at : at + 1, :] if inside else zero)
        place = jnp.where(apart == out, 1.0, 0.0).astype(bf16)
        for term in split3(jnp.concatenate(picked, axis=0)):
            total = total + mm(term, place)
    for m in range(3):
        coef_ref[m] = total[8 * m : 8 * (m + 1)]


def both_halves(flag, own, other):
    is_low = flag[1] == 0
    return jnp.concatenate([jnp.where(is_low, own, other), jnp.where(is_low, other, own)], axis=1)


def first_kernel(
    flag, own_ref, other_ref, hown_ref, hother_ref, ln_ref, up_ref, cw_ref, cb_ref, maps_ref, gate_ref,
    normed_ref, inner_ref, conv_ref, active_ref, q_ref, k_ref, v_ref, pre_ref, coef_ref, pad_ref, gw_ref,
):
    step = pl.program_id(0)
    tile = own_ref.shape[0]

    @pl.when(step == 0)
    def _():
        halo = both_halves(flag, hown_ref[...].astype(f32), hother_ref[...].astype(f32))
        before = mm(normed_rows(halo, ln_ref[...]), up_ref[...])
        pad_ref[0:8, :] = jnp.where(flag[0] == 1, 0.0, before[HALO - 8 :, :])
        spread_coefs(maps_ref, coef_ref)
        gw_ref[...] = jnp.zeros_like(gw_ref)
        gw_ref[:, :, 0 : gate_ref.shape[2]] = gate_ref[...]

    x = both_halves(flag, own_ref[...].astype(f32), other_ref[...].astype(f32))
    normed = normed_rows(x, ln_ref[...])
    normed_ref[...] = normed
    inner = mm(normed, up_ref[...])
    inner_ref[...] = inner
    pad_ref[8:, :] = inner
    conv = cb_ref[...] + cw_ref[0:1, :] * inner
    for j in range(1, cw_ref.shape[0]):
        conv = conv + cw_ref[j : j + 1, :] * pad_ref[8 - j : 8 - j + tile, :]
    conv_ref[...] = conv
    pad_ref[0:8, :] = pad_ref[tile : tile + 8, :]
    active_ref[...] = conv * sigmoid(conv)
    reach = QB - 1
    for g in range(inner.shape[1] // LANES):
        part = slice(g * LANES, (g + 1) * LANES)
        query, key = band_sum(active_ref[:, part], (coef_ref[0, :, part], coef_ref[1, :, part]), reach)
        q_ref[:, part] = query.astype(bf16)
        k_ref[:, part] = key.astype(bf16)
        v_ref[:, part] = band_sum(inner_ref[:, part], (coef_ref[2, :, part],), reach)[0].astype(bf16)
    pre = mm(q_ref[...], gw_ref[0]) + mm(k_ref[...], gw_ref[1]) + mm(v_ref[...], gw_ref[2])
    pre_ref[...] = jnp.transpose(pre)[0:8, :]


def first_stage(flag, own, other, hown, hother, ln, up, cw, cb, maps, gate):
    count, half = own.shape
    model, chan = up.shape
    wide = (count, chan)
    return pl.pallas_call(
        first_kernel,
        grid=(count // TILE,),
        in_specs=[
            smem, rows(half), rows(half), whole(*hown.shape), whole(*hown.shape), whole(*ln.shape),
            whole(*up.shape), whole(*cw.shape), whole(*cb.shape), whole(*maps.shape), whole(*gate.shape),
        ],
        out_specs=[rows(model), rows(chan), rows(chan), rows(chan), rows(chan), rows(chan), rows(chan),
                   pl.BlockSpec((8, TILE), lambda i: (0, i)), whole(3, 8, chan)],
        out_shape=[shape_of(count, model, dtype=bf16), shape_of(*wide), shape_of(*wide), shape_of(*wide),
                   shape_of(*wide, dtype=bf16), shape_of(*wide, dtype=bf16), shape_of(*wide, dtype=bf16),
                   shape_of(8, count), shape_of(3, 8, chan)],
        scratch_shapes=[pltpu.VMEM((TILE + 8, chan), f32), pltpu.VMEM((3, chan, LANES), bf16)],
        compiler_params=params(LIMIT),
        cost_estimate=cost(2 * count * model * chan * 4, count * chan * 20),
        name="first",
    )(flag, own, other, hown, hother, ln, up, cw, cb, maps, gate)


def gates_kernel(place, own_ref, other_ref, bias_ref, row_ref, col_ref, total_ref):
    count = own_ref.shape[1]
    pre = own_ref[...] + other_ref[...] + bias_ref[...]
    low_half = place[0] == 0
    in_pre = jnp.where(low_half, pre[0:2], pre[2:4])
    forget = jnp.where(low_half, pre[4:6], pre[6:8])
    both = jnp.concatenate([in_pre, forget, in_pre, forget], axis=0)
    in8 = jnp.concatenate([in_pre] * 4, axis=0)
    f8 = jnp.concatenate([forget] * 4, axis=0)
    log_keep = jnp.minimum(f8, 0.0) - jnp.log1p(jnp.exp(-jnp.abs(f8)))
    lane = lax.broadcasted_iota(jnp.int32, f8.shape, 1)
    place_in = lane % BLOCK
    cum = log_keep
    dist = 1
    while dist < BLOCK:
        cum = cum + jnp.where(place_in >= dist, pltpu.roll(cum, dist, 1), 0.0)
        dist *= 2
    last = jnp.where(place_in == BLOCK - 1, cum, 0.0)
    dist = 1
    while dist < BLOCK:
        last = last + jnp.where(place_in < BLOCK - dist, pltpu.roll(last, count - dist, 1), 0.0)
        dist *= 2
    before = jnp.where(lane >= BLOCK, pltpu.roll(last, BLOCK, 1), 0.0)
    after = jnp.where(lane < count - BLOCK, pltpu.roll(last, count - BLOCK, 1), 0.0)
    dist = BLOCK
    while dist < count:
        before = before + jnp.where(lane >= dist, pltpu.roll(before, dist, 1), 0.0)
        after = after + jnp.where(lane < count - dist, pltpu.roll(after, count - dist, 1), 0.0)
        dist *= 2
    scale = DH ** (-0.5)
    keep = jnp.exp(last - cum + in8) * scale
    table = jnp.concatenate(
        [
            cum[0:2], jnp.exp(cum[0:2]), keep[0:2], jnp.exp(after[0:2]),
            jnp.exp(before[0:2]), jnp.exp(last[0:2]), in8[0:2], 1.0 / (1.0 + jnp.exp(f8[0:2])),
        ],
        axis=0,
    )
    tall = jnp.concatenate([table, jnp.zeros((LANES - 16, count), f32)], axis=0)
    col_ref[...] = jnp.transpose(tall)
    small = jnp.concatenate([cum[0:2], in8[0:2], cum[0:2], in8[0:2]], axis=0)
    for b in range(count // BLOCK):
        row_ref[b] = small[:, b * BLOCK : (b + 1) * BLOCK]
    total = (before + last)[:, count - 1 : count]
    total_ref[...] = jnp.broadcast_to(total, total_ref.shape)


def gates_stage(place, own, other, bias):
    count = own.shape[1]
    return pl.pallas_call(
        gates_kernel,
        grid=(1,),
        in_specs=[smem, whole(8, count), whole(8, count), whole(8, 1)],
        out_specs=[whole(count // BLOCK, 8, BLOCK), whole(count, LANES), whole(8, DH)],
        out_shape=[shape_of(count // BLOCK, 8, BLOCK), shape_of(count, LANES), shape_of(8, DH)],
        compiler_params=params(24),
        cost_estimate=cost(count * 1000, count * 600),
        name="gates",
    )(place, own, other, bias)


def write_pack(ref, state, vector, log_decay):
    ref[0:DH, :] = state.astype(bf16)
    terms = split3(vector) + split3(log_decay)
    tail = jnp.concatenate(
        [t.astype(f32) for t in terms] + [jnp.zeros((PACK - DH - 6, vector.shape[1]), f32)], axis=0
    )
    ref[DH:PACK, :] = tail.astype(bf16)


def write_wide(ref, state, vector, log_decay):
    ref[0:DH, :] = state
    ref[DH:WIDE, :] = jnp.concatenate(
        [vector, log_decay, jnp.zeros((WIDE - DH - 2, vector.shape[1]), f32)], axis=0
    )


def read_pack(ref):
    tail = ref[DH:PACK, :].astype(f32)
    return (
        ref[0:DH, :].astype(f32), (tail[0:1] + tail[1:2]) + tail[2:3], (tail[3:4] + tail[4:5]) + tail[5:6]
    )


def read_wide(ref):
    return ref[0:DH, :], ref[DH : DH + 1, :], ref[DH + 1 : DH + 2, :]


def joined(first, second):
    decay = jnp.exp(second[2])
    return decay * first[0] + second[0], decay * first[1] + second[1], first[2] + second[2]


def chosen(which, yes, no):
    return tuple(jnp.where(which, a, b) for a, b in zip(yes, no))


def pair_kernel(flag, own_ref, got_ref, send_ref, total_ref, lead_ref):
    own, got = read_wide(own_ref), read_pack(got_ref)
    is_lead = flag[0] == 1
    lead = chosen(is_lead, own, got)
    total = joined(lead, chosen(is_lead, got, own))
    write_wide(lead_ref, *lead)
    write_wide(total_ref, *total)
    write_pack(send_ref, *total)


def step_kernel(flag, total_ref, got_ref, before_ref, send_ref, new_total_ref, new_before_ref):
    total, got, before = read_wide(total_ref), read_pack(got_ref), read_wide(before_ref)
    upper = flag[0] == 1
    both = joined(chosen(upper, got, total), chosen(upper, total, got))
    write_wide(new_total_ref, *both)
    write_pack(send_ref, *both)
    write_wide(new_before_ref, *chosen(upper, joined(got, before), before))


def last_kernel(flag, got_ref, before_ref, lead_ref, send_ref, mine_ref):
    before, got = read_wide(before_ref), read_pack(got_ref)
    upper = flag[0] == 1
    is_lead = flag[1] == 1
    found = chosen(upper, joined(got, before), before)
    after = joined(found, read_wide(lead_ref))
    write_pack(send_ref, *chosen(is_lead, after, found))
    write_wide(mine_ref, *chosen(is_lead, found, after))


def pack_spec(wide, streams):
    return whole(WIDE if wide else PACK, DH // streams)


def pack_shape(wide, streams):
    return shape_of(WIDE if wide else PACK, DH // streams, dtype=f32 if wide else bf16)


def pack_specs(streams):
    return [pack_spec(1, streams)] * streams + [pack_spec(0, streams)] * streams


def pack_shapes(streams):
    return [pack_shape(1, streams)] * streams + [pack_shape(0, streams)] * streams


def small_call(kernel, name, ins, outs, flag, *packs):
    streams = DH // packs[0].shape[1]
    return pl.pallas_call(
        kernel,
        grid=(1,),
        in_specs=[smem] + [pack_spec(w, streams) for w in ins],
        out_specs=[pack_spec(w, streams) for w in outs],
        out_shape=[pack_shape(w, streams) for w in outs],
        compiler_params=params(24),
        cost_estimate=cost(PACK * DH * 8, PACK * DH * 3 * (len(ins) + len(outs))),
        name=name,
    )(flag, *packs)


def pass_states(own, send, place, span, stride, fillers=((), (), ())):
    devices = lax.axis_size("dp")

    def swap(value, bit):
        route = [((i // stride ^ bit) * stride + i % stride, i) for i in range(devices)]
        return lax.ppermute(value, "dp", route)

    def as_flag(*values):
        return jnp.stack([jnp.asarray(v).astype(jnp.int32) for v in values])

    is_lead = place % 2 == 0
    streams = range(len(own))
    done = []

    def exchange(packs, bit):
        got = [swap(pack, bit) for pack in packs]
        if bit < span and len(done) < len(fillers):
            got[-1], filler = lax.optimization_barrier((got[-1], fillers[len(done)]))
            done.append(filler)
        return got

    got = exchange(send, 1)
    found = [
        small_call(pair_kernel, "pair", (1, 0), (0, 1, 1), as_flag(is_lead), own[n], got[n]) for n in streams
    ]
    out, total, lead = zip(*found)
    before = [jnp.zeros_like(pack) for pack in own]
    bit = 2
    while bit < span:
        got = exchange(out, bit)
        upper = (place // bit) % 2 == 1
        if bit * 2 < span:
            found = [
                small_call(
                    step_kernel, "step", (1, 0, 1), (0, 1, 1), as_flag(upper), total[n], got[n], before[n]
                )
                for n in streams
            ]
            out, total, before = zip(*found)
        bit *= 2
    found = [
        small_call(
            last_kernel, "last", (0, 1, 1), (0, 1), as_flag(upper, is_lead), got[n], before[n], lead[n]
        )
        for n in streams
    ]
    out, mine = zip(*found)
    return mine + tuple(swap(pack, 1) for pack in out), done


def put_states(flag, packs, state_ref, vec_ref):
    streams = len(packs) // 2
    size = DH // streams
    for n in range(streams):
        mine, came = read_wide(packs[n]), read_pack(packs[streams + n])
        part = slice(n * size, (n + 1) * size)
        for h in range(2):
            found = chosen((flag[0] == 1) == (h == 0), mine, came)
            state_ref[h, :, part] = found[0]
            vec_ref[h : h + 1, part] = found[1]


def ends_kernel(flag, k_ref, v_ref, col_ref, total_ref, *refs):
    packs, (state_ref, vec_ref) = refs[: 2 * FORTH], refs[2 * FORTH :]
    step = pl.program_id(0)

    @pl.when(step == 0)
    def _():
        state_ref[...] = jnp.zeros_like(state_ref)
        vec_ref[...] = jnp.zeros_like(vec_ref)

    col = col_ref[...]
    for h in range(2):
        part = slice(h * DH, (h + 1) * DH)
        wide = k_ref[:, part].astype(f32)
        keep = col[:, 4 + h : 5 + h]
        later = col[:, 6 + h : 7 + h]
        kept = wide * keep
        high, low = split2(kept.astype(bf16).astype(f32) * later)
        value = v_ref[:, part]
        state_ref[h] += mm_tn(high, value) + mm_tn(low, value)
        vec_ref[h : h + 1, :] += jnp.sum(kept * later, axis=0, keepdims=True)

    @pl.when(step == pl.num_programs(0) - 1)
    def _():
        write_two(flag, state_ref, vec_ref, total_ref, packs)


def write_two(flag, state_ref, vec_ref, total_ref, packs):
    streams = len(packs) // 2
    size = DH // streams
    for n in range(streams):
        part = slice(n * size, (n + 1) * size)
        for h in range(2):
            found = (state_ref[h, :, part], vec_ref[h : h + 1, part], total_ref[h : h + 1, part])

            @pl.when(flag[0] == 1 - h)
            def _():
                write_wide(packs[n], *found)

            @pl.when(flag[0] == h)
            def _():
                write_pack(packs[streams + n], *found)


def ends_stage(flag, k, v, col, total):
    count, chan = k.shape
    return pl.pallas_call(
        ends_kernel,
        grid=(count // TILE,),
        in_specs=[smem, rows(chan), rows(chan), rows(LANES), whole(8, DH)],
        out_specs=pack_specs(FORTH),
        out_shape=pack_shapes(FORTH),
        scratch_shapes=[pltpu.VMEM((2, DH, DH), f32), pltpu.VMEM((8, DH), f32)],
        compiler_params=params(LIMIT),
        cost_estimate=cost(4 * count * chan * DH, count * chan * 4),
        name="ends",
    )(flag, k, v, col, total)


def damping_of(col, row, h):
    t = lax.broadcasted_iota(jnp.int32, (BLOCK, BLOCK), 0)
    s = lax.broadcasted_iota(jnp.int32, (BLOCK, BLOCK), 1)
    expo = col[:, h : h + 1] - row[h : h + 1, :] + row[2 + h : 3 + h, :]
    return jnp.exp(jnp.where(t >= s, expo, -1e30))


def lanes_of(*columns, offset=0):
    lane = lax.broadcasted_iota(jnp.int32, (columns[0].shape[0], LANES), 1) - offset
    out = jnp.zeros(lane.shape, f32)
    for i, column in enumerate(columns):
        out = jnp.where(lane == i, column, out)
    return out


def inside_kernel(q_ref, k_ref, v_ref, col_ref, row_ref, inside_ref, norm_ref):
    scale = DH ** (-0.5)

    def body(b, carry):
        r0 = pl.multiple_of(b * BLOCK, BLOCK)
        here = pl.ds(r0, BLOCK)
        col = col_ref[here, :]
        row = row_ref[b]
        sums = []
        for h in range(2):
            part = slice(h * DH, (h + 1) * DH)
            scores = mm_nt(q_ref[here, part], k_ref[here, part])
            weights = scores * damping_of(col, row, h) * scale
            inside_ref[here, part] = mm(weights.astype(bf16), v_ref[here, part])
            sums.append(jnp.sum(weights, axis=1, keepdims=True))
        norm_ref[here, :] = lanes_of(*sums)
        return carry

    lax.fori_loop(0, q_ref.shape[0] // BLOCK, body, 0)


def inside_stage(q, k, v, col, row):
    count, chan = q.shape
    return pl.pallas_call(
        inside_kernel,
        grid=(count // TILE,),
        in_specs=[rows(chan), rows(chan), rows(chan), rows(LANES),
                  pl.BlockSpec((TILE // BLOCK, 8, BLOCK), lambda i: (i, 0, 0))],
        out_specs=[rows(chan), rows(LANES)],
        out_shape=[shape_of(count, chan), shape_of(count, LANES)],
        compiler_params=params(32),
        cost_estimate=cost(4 * count * chan * BLOCK, count * chan * 10),
        name="inside",
    )(q, k, v, col, row)


def middle_kernel(flag, *refs):
    states, refs = refs[: 2 * FORTH], refs[2 * FORTH :]
    (
        q_ref, k_ref, v_ref, inside_ref, norm_ref, col_ref, gate_ref, dgated_ref, active_ref, group_ref,
        skip_ref, total_ref,
        gated_ref, gig_ref, sgrad_ref, nlow_ref, clow_ref, start_ref, nvec_ref, stat_ref, ggroup_ref, gskip_ref,
    ) = refs[:22]
    packs = refs[22 : 22 + 2 * BACK]
    state_ref, vec_ref, back_ref, bvec_ref, cross_ref, ncross_ref = refs[22 + 2 * BACK :]
    step = pl.program_id(0)

    @pl.when(step == 0)
    def _():
        put_states(flag, states, state_ref, vec_ref)
        back_ref[...] = jnp.zeros_like(back_ref)
        bvec_ref[...] = jnp.zeros_like(bvec_ref)
        ggroup_ref[...] = jnp.zeros_like(ggroup_ref)
        gskip_ref[...] = jnp.zeros_like(gskip_ref)

    def body(b, carry):
        r0 = pl.multiple_of(b * BLOCK, BLOCK)
        here = pl.ds(r0, BLOCK)
        col = col_ref[here, :]
        nvec_ref[b] = vec_ref[...]
        crosses = []
        for h in range(2):
            part = slice(h * DH, (h + 1) * DH)
            query = q_ref[here, part]
            state = state_ref[h]
            state_low = state.astype(bf16)
            start_ref[h, b] = state_low
            cross_ref[here, part] = mm(query, state_low)
            vec = vec_ref[h : h + 1, :]
            crosses.append(jnp.sum(query.astype(f32) * vec, axis=1, keepdims=True))
            kept = k_ref[here, part].astype(f32) * col[:, 4 + h : 5 + h]
            decay = col[0:1, 10 + h : 11 + h]
            state_ref[h] = decay * state + mm_tn(kept.astype(bf16), v_ref[here, part])
            vec_ref[h : h + 1, :] = decay * vec + jnp.sum(kept, axis=0, keepdims=True)
        ncross_ref[here, :] = lanes_of(*crosses)
        return carry

    lax.fori_loop(0, q_ref.shape[0] // BLOCK, body, 0, unroll=UNROLL)

    def strip(i, carry):
        here = pl.ds(pl.multiple_of(i * STRIP, STRIP), STRIP)
        col = col_ref[here, :]
        norms = norm_ref[here, :]
        stats = []
        for h in range(2):
            part = slice(h * DH, (h + 1) * DH)
            growth = col[:, 2 + h : 3 + h]
            carried = growth * cross_ref[here, part]
            norm_cross = growth * ncross_ref[here, h : h + 1]
            numer = inside_ref[here, part] + carried
            normal = norms[:, h : h + 1] + norm_cross
            over = 1.0 / jnp.maximum(jnp.abs(normal), 1.0)
            mixed = numer * over
            centered = mixed - jnp.mean(mixed, axis=1, keepdims=True)
            inverse = lax.rsqrt(jnp.mean(centered * centered, axis=1, keepdims=True) + NORM_EPS)
            ghat = centered * inverse
            active = active_ref[here, part]
            gate = gate_ref[here, part]
            sig = sigmoid(gate)
            gact = gate * sig
            gweight = group_ref[0:1, part]
            gstate = ghat * gweight + skip_ref[0:1, part] * active
            gated_ref[here, part] = (gstate * gact).astype(bf16)
            dgated = dgated_ref[here, part]
            sgrad = dgated * gact
            sgrad_ref[here, part] = sgrad
            gig_ref[here, part] = (dgated * gstate * sig * (1.0 + gate * (1.0 - sig))).astype(bf16)
            gskip_ref[0:1, part] += jnp.sum(sgrad * active, axis=0, keepdims=True)
            ggroup_ref[0:1, part] += jnp.sum(sgrad * ghat, axis=0, keepdims=True)
            g = sgrad * gweight
            mgrad = inverse * (
                g - jnp.mean(g, axis=1, keepdims=True) - ghat * jnp.mean(g * ghat, axis=1, keepdims=True)
            )
            ngrad = mgrad * over
            down = -jnp.sum(mgrad * mixed, axis=1, keepdims=True) * over
            normal_grad = jnp.where(normal > 1.0, down, jnp.where(normal < -1.0, -down, 0.0))
            nlow_ref[here, part] = ngrad.astype(bf16)
            clow_ref[here, part] = (growth * ngrad).astype(bf16)
            moved = jnp.sum(ngrad * carried, axis=1, keepdims=True) + normal_grad * norm_cross
            stats.append((normal_grad, moved))
            scaled = col[:, 8 + h : 9 + h] * growth * normal_grad
            bvec_ref[h : h + 1, :] += jnp.sum(scaled * q_ref[here, part].astype(f32), axis=0, keepdims=True)
        stat_ref[here, :] = lanes_of(stats[0][0], stats[1][0], stats[0][1], stats[1][1])
        return carry

    lax.fori_loop(0, q_ref.shape[0] // STRIP, strip, 0)
    for h in range(2):
        part = slice(h * DH, (h + 1) * DH)
        high, low = split2(clow_ref[:, part].astype(f32) * col_ref[:, 8 + h : 9 + h])
        query = q_ref[:, part]
        back_ref[h] += mm_tn(query, high) + mm_tn(query, low)

    @pl.when(step == pl.num_programs(0) - 1)
    def _():
        write_two(flag, back_ref, bvec_ref, total_ref, packs)


def middle_stage(flag, states, q, k, v, inside, norms, col, gate, dgated, active, group, skip, total):
    count, chan = q.shape
    blocks = count // BLOCK
    per = TILE // BLOCK
    return pl.pallas_call(
        middle_kernel,
        grid=(count // TILE,),
        in_specs=[smem, *pack_specs(FORTH), rows(chan), rows(chan), rows(chan),
                  rows(chan), rows(LANES), rows(LANES), rows(chan), rows(chan), rows(chan), whole(1, chan), whole(1, chan), whole(8, DH)],
        out_specs=[rows(chan), rows(chan), rows(chan), rows(chan), rows(chan),
                   pl.BlockSpec((2, per, DH, DH), lambda i: (0, i, 0, 0)),
                   pl.BlockSpec((per, 8, DH), lambda i: (i, 0, 0)),
                   rows(LANES), whole(8, chan), whole(8, chan), *pack_specs(BACK)],
        out_shape=[shape_of(count, chan, dtype=bf16), shape_of(count, chan, dtype=bf16), shape_of(count, chan),
                   shape_of(count, chan, dtype=bf16), shape_of(count, chan, dtype=bf16),
                   shape_of(2, blocks, DH, DH, dtype=bf16), shape_of(blocks, 8, DH), shape_of(count, LANES),
                   shape_of(8, chan), shape_of(8, chan),
                   *pack_shapes(BACK)],
        scratch_shapes=[pltpu.VMEM((2, DH, DH), f32), pltpu.VMEM((8, DH), f32),
                        pltpu.VMEM((2, DH, DH), f32), pltpu.VMEM((8, DH), f32),
                        pltpu.VMEM((TILE, chan), f32), pltpu.VMEM((TILE, LANES), f32)],
        compiler_params=params(LIMIT),
        cost_estimate=cost(10 * count * chan * DH, count * chan * 107),
        name="middle",
    )(flag, *states, q, k, v, inside, norms, col, gate, dgated, active, group, skip, total)


def back_kernel(flag, *refs):
    states, refs = refs[: 2 * BACK], refs[2 * BACK :]
    (
        q_ref, k_ref, v_ref, nlow_ref, clow_ref, start_ref, nvec_ref, col_ref, row_ref, stat_ref,
        qg_ref, kg_ref, vg_ref, pre_ref,
        state_ref, vec_ref,
    ) = refs
    scale = DH ** (-0.5)

    @pl.when(pl.program_id(0) == 0)
    def _():
        put_states(flag, states, state_ref, vec_ref)

    u = lax.broadcasted_iota(jnp.int32, (BLOCK, BLOCK), 0)
    t = lax.broadcasted_iota(jnp.int32, (BLOCK, BLOCK), 1)
    from_here = jnp.where(t >= u, 1.0, 0.0)
    at_end = lax.broadcasted_iota(jnp.int32, (BLOCK, 1), 0) == BLOCK - 1
    per = q_ref.shape[0] // BLOCK

    def body(i, carry):
        b = per - 1 - i
        r0 = pl.multiple_of(b * BLOCK, BLOCK)
        here = pl.ds(r0, BLOCK)
        col = col_ref[here, :]
        row = row_ref[b]
        stat = stat_ref[here, :]
        starts = nvec_ref[b]
        in_cols, cum_cols = [], []
        for h in range(2):
            part = slice(h * DH, (h + 1) * DH)
            query, key, value = q_ref[here, part], k_ref[here, part], v_ref[here, part]
            numer_low, cross_low = nlow_ref[here, part], clow_ref[here, part]
            growth = col[:, 2 + h : 3 + h]
            keep = col[:, 4 + h : 5 + h]
            decay = col[0:1, 10 + h : 11 + h]
            normal_grad = stat[:, h : h + 1]
            moved = stat[:, 2 + h : 3 + h]
            end = state_ref[h]
            end_low = end.astype(bf16)
            end_vec = vec_ref[h : h + 1, :]
            start_low = start_ref[h, b]
            start_vec = starts[h : h + 1, :]
            damping = damping_of(col, row, h)
            scores = mm_nt(query, key)
            weights_low = (scores * damping * scale).astype(bf16)
            weights_grad = mm_nt(numer_low, value) + normal_grad
            damped = weights_grad * scale * damping
            scores_low = damped.astype(bf16)
            expo = damped * scores
            pull = growth * normal_grad
            qg_ref[here, part] = mm(scores_low, key) + mm_nt(cross_low, start_low) + pull * start_vec
            wide = key.astype(f32)
            kept_low = (wide * keep).astype(bf16)
            key_total = mm_nt(value, end_low) + end_vec
            kg_ref[here, part] = mm_tn(scores_low, query) + keep * key_total
            vg_ref[here, part] = mm_tn(weights_low, numer_low) + mm(kept_low, end_low)
            keep_grad = keep * jnp.sum(wide * key_total, axis=1, keepdims=True)
            held = jnp.sum(end * start_low.astype(f32), axis=0, keepdims=True) + end_vec * start_vec
            last_grad = decay * jnp.sum(held, axis=1, keepdims=True) + jnp.sum(keep_grad, axis=0, keepdims=True)
            over_t = jnp.sum(jnp.transpose(expo), axis=1, keepdims=True)
            cum_grad = jnp.sum(expo, axis=1, keepdims=True) - over_t + moved - keep_grad
            cum_cols.append(cum_grad + jnp.where(at_end, last_grad, 0.0))
            in_cols.append(over_t + keep_grad)
            state_ref[h] = decay * end + mm_tn(query, cross_low)
            vec_ref[h : h + 1, :] = decay * end_vec + jnp.sum(pull * query.astype(f32), axis=0, keepdims=True)
        sums = lax.dot_general(
            from_here, lanes_of(*cum_cols), (((1,), (0,)), ((), ())), precision=highest, preferred_element_type=f32
        )
        forget = [sums[:, h : h + 1] * col[:, 14 + h : 15 + h] for h in range(2)]
        pre_ref[here, :] = lanes_of(*in_cols, *forget, offset=4 * flag[1]).astype(bf16)
        return carry

    lax.fori_loop(0, per, body, 0, unroll=4)


def back_stage(flag, states, q, k, v, nlow, clow, start, nvec, col, row, stat):
    count, chan = q.shape
    tiles = count // TILE
    per = TILE // BLOCK
    flip = rows(chan, flip=tiles)
    thin = rows(LANES, flip=tiles)
    return pl.pallas_call(
        back_kernel,
        grid=(tiles,),
        in_specs=[smem, *pack_specs(BACK), flip, flip, flip, flip, flip,
                  pl.BlockSpec((2, per, DH, DH), lambda i: (0, tiles - 1 - i, 0, 0)),
                  pl.BlockSpec((per, 8, DH), lambda i: (tiles - 1 - i, 0, 0)), thin,
                  pl.BlockSpec((per, 8, BLOCK), lambda i: (tiles - 1 - i, 0, 0)), thin],
        out_specs=[flip, flip, flip, thin],
        out_shape=[shape_of(count, chan)] * 3 + [shape_of(count, LANES, dtype=bf16)],
        scratch_shapes=[pltpu.VMEM((2, DH, DH), f32), pltpu.VMEM((8, DH), f32)],
        compiler_params=params(LIMIT),
        cost_estimate=cost(14 * count * chan * DH, count * chan * 133),
        name="back",
    )(flag, *states, q, k, v, nlow, clow, start, nvec, col, row, stat)


def band_back(value, map_hi, map_lo):
    high, low = value
    found = []
    for g in range(high.shape[1] // GROUP):
        part = slice(g * GROUP, (g + 1) * GROUP)
        found.append(
            mm_nt(high[:, part], map_hi[g])
            + (mm_nt(low[:, part], map_hi[g]) + mm_nt(high[:, part], map_lo[g]))
        )
    return jnp.concatenate(found, axis=1)


def conv_grad_of(active_grad, conv):
    sig = sigmoid(conv)
    return active_grad * sig * (1.0 + conv * (1.0 - sig))


def edge_kernel(qg_ref, kg_ref, pre_ref, other_ref, sgrad_ref, conv_ref, skip_ref, coef_ref, gwt_ref, out_ref):
    pre = pre_ref[...] + other_ref[...]
    query_all = qg_ref[...] + mm(pre, gwt_ref[0])
    key_all = kg_ref[...] + mm(pre, gwt_ref[1])
    reach = QB - 1
    for g in range(query_all.shape[1] // LANES):
        part = slice(g * LANES, (g + 1) * LANES)
        total = sgrad_ref[:, part] * skip_ref[:, part]
        for m, value in enumerate((query_all[:, part], key_all[:, part])):
            for offset in range(-reach, reach + 1):
                total = total + pltpu.roll(
                    coef_ref[m, reach - offset : reach - offset + 1, part] * value, -offset % LANES, 1
                )
        out_ref[:, part] = conv_grad_of(total, conv_ref[:, part])[0:8, :]


def edge_stage(qg, kg, pre, other, sgrad, conv, skip, coefs, gwt):
    chan = qg.shape[1]
    top = rows(chan, HALO)
    return pl.pallas_call(
        edge_kernel,
        grid=(1,),
        in_specs=[top, top, rows(LANES, HALO), rows(LANES, HALO), top, top, whole(*skip.shape), whole(*coefs.shape),
                  whole(*gwt.shape)],
        out_specs=whole(8, chan),
        out_shape=shape_of(8, chan),
        compiler_params=params(LIMIT),
        cost_estimate=cost(10**7, 10**6),
        name="edge",
    )(qg, kg, pre, other, sgrad, conv, skip, coefs, gwt)


def maps_kernel(
    flag, qg_ref, kg_ref, vg_ref, mine_ref, other_ref, sgrad_ref, conv_ref, inner_ref, q_ref, k_ref, v_ref, edge_ref,
    skip_ref, cw_ref, coef_ref, gwt_ref, ggroup_ref, gskip_ref,
    low_ref, small_ref,
    pad_ref, hi_ref, lo_ref, gmap_ref,
):
    tile, chan = qg_ref.shape
    groups = chan // GROUP
    reach = QB - 1

    @pl.when(pl.program_id(0) == 0)
    def _():
        pad_ref[tile : tile + 8, :] = jnp.where(flag[0] == 1, 0.0, edge_ref[...])
        gmap_ref[...] = jnp.zeros_like(gmap_ref)
        small_ref[...] = jnp.zeros_like(small_ref)
        apart = lax.broadcasted_iota(jnp.int32, (GROUP, GROUP), 0) - lax.broadcasted_iota(
            jnp.int32, (GROUP, GROUP), 1
        )
        for m in range(3):
            for g in range(groups):
                dense = jnp.zeros((GROUP, GROUP), f32)
                for offset in range(-reach, reach + 1):
                    coef = coef_ref[m, reach + offset : reach + offset + 1, g * GROUP : (g + 1) * GROUP]
                    dense = jnp.where(apart == offset, coef, dense)
                hi_ref[m, g], lo_ref[m, g] = split2(dense)

    pre = mine_ref[...] + other_ref[...]
    conv = conv_ref[...]
    inner = inner_ref[...]
    query_all = split2(qg_ref[...] + mm(pre, gwt_ref[0]))
    key_all = split2(kg_ref[...] + mm(pre, gwt_ref[1]))
    value_all = split2(vg_ref[...] + mm(pre, gwt_ref[2]))
    active = split2(conv * sigmoid(conv))
    inner2 = split2(inner)
    for m, (grads, acts) in enumerate(((query_all, active), (key_all, active), (value_all, inner2))):
        for g in range(groups):
            part = slice(g * GROUP, (g + 1) * GROUP)
            gmap_ref[m, g] += mm_tn(grads[0][:, part], acts[0][:, part]) + (
                mm_tn(grads[1][:, part], acts[0][:, part]) + mm_tn(grads[0][:, part], acts[1][:, part])
            )
    active_grad = (
        sgrad_ref[...] * skip_ref[...]
        + band_back(query_all, hi_ref[0], lo_ref[0])
        + band_back(key_all, hi_ref[1], lo_ref[1])
    )
    grad = conv_grad_of(active_grad, conv)
    pad_ref[0:tile, :] = grad
    taps = cw_ref.shape[0]
    small_ref[taps : taps + 1, :] += jnp.sum(grad, axis=0, keepdims=True)
    inner_grad = band_back(value_all, hi_ref[2], lo_ref[2])
    for j in range(cw_ref.shape[0]):
        moved = pad_ref[j : j + tile, :]
        inner_grad = inner_grad + cw_ref[j : j + 1, :] * moved
        small_ref[j : j + 1, :] += jnp.sum(moved * inner, axis=0, keepdims=True)
    low_ref[...] = inner_grad.astype(bf16)
    pad_ref[tile : tile + 8, :] = pad_ref[0:8, :]
    for m, ref in enumerate((q_ref, k_ref, v_ref)):
        small_ref[8 * (m + 1) : 8 * (m + 2), :] += mm_tn(pre, ref[...])[0:8, :]
    small_ref[taps + 1 : taps + 2, 0:LANES] += jnp.sum(pre.astype(f32), axis=0, keepdims=True)

    @pl.when(pl.program_id(0) == pl.num_programs(0) - 1)
    def _():
        r = lax.broadcasted_iota(jnp.int32, (GROUP, GROUP), 0)
        c = lax.broadcasted_iota(jnp.int32, (GROUP, GROUP), 1)
        pick = jnp.where(
            lax.broadcasted_iota(jnp.int32, (8, GROUP), 1) % QB == lax.broadcasted_iota(jnp.int32, (8, GROUP), 0),
            1.0, 0.0,
        )
        for m in range(3):
            for g in range(groups):
                held = jnp.where(r // QB == c // QB, gmap_ref[m, g], 0.0)
                found = lax.dot_general(
                    pick, held, (((1,), (1,)), ((), ())), precision=highest, preferred_element_type=f32
                )
                small_ref[32 + QB * m : 32 + QB * (m + 1), g * GROUP : (g + 1) * GROUP] = found[0:QB]
        small_ref[taps + 2 : taps + 3, :] = ggroup_ref[0:1, :]
        small_ref[taps + 3 : taps + 4, :] = gskip_ref[0:1, :]


def maps_stage(flag, qg, kg, vg, pre, other, sgrad, conv, inner, q, k, v, edge, skip, cw, coefs, gwt, ggroup, gskip):
    count, chan = qg.shape
    tiles = count // TILE
    flip = rows(chan, flip=tiles)
    groups = chan // GROUP
    return pl.pallas_call(
        maps_kernel,
        grid=(tiles,),
        in_specs=[smem, flip, flip, flip, rows(LANES, flip=tiles), rows(LANES, flip=tiles), flip, flip, flip, flip,
                  flip, flip,
                  whole(8, chan), whole(*skip.shape), whole(*cw.shape), whole(*coefs.shape), whole(*gwt.shape),
                  whole(8, chan), whole(8, chan)],
        out_specs=[flip, whole(SMALL, chan)],
        out_shape=[shape_of(count, chan, dtype=bf16), shape_of(SMALL, chan)],
        scratch_shapes=[pltpu.VMEM((TILE + 8, chan), f32), pltpu.VMEM((3, groups, GROUP, GROUP), bf16),
                        pltpu.VMEM((3, groups, GROUP, GROUP), bf16), pltpu.VMEM((3, groups, GROUP, GROUP), f32)],
        compiler_params=params(LIMIT),
        cost_estimate=cost(20 * count * chan * GROUP, count * chan * 110),
        name="maps",
    )(flag, qg, kg, vg, pre, other, sgrad, conv, inner, q, k, v, edge, skip, cw, coefs, gwt, ggroup, gskip)


def exchanged(value, bit):
    route = [(i ^ bit, i) for i in range(lax.axis_size("dp"))]
    return lax.ppermute(value, "dp", route)


def halved(value, bit):
    mine = (lax.axis_index("dp") // bit) % 2
    width = value.shape[1]
    size = value.shape[0] // 2
    send = lax.dynamic_slice(value, ((1 - mine) * size, 0), (size, width)).astype(bf16)
    keep = lax.dynamic_slice(value, (mine * size, 0), (size, width))
    return keep + exchanged(send, bit).astype(f32)


def joined_halves(value, bit):
    first = (lax.axis_index("dp") // bit) % 2 == 0
    other = exchanged(value, bit)
    return jnp.concatenate([jnp.where(first, value, other), jnp.where(first, other, value)], axis=0)


def finished(pair, bits):
    value = jnp.concatenate(pair, axis=0)
    for bit in bits[2:]:
        value = halved(value, bit)
    value = value.astype(bf16)
    for bit in reversed(bits[2:]):
        value = joined_halves(value, bit)
    size = value.shape[0] // 2
    one, two = joined_halves(value[:size], bits[1]), joined_halves(value[size:], bits[0])
    return jnp.concatenate([joined_halves(one, bits[0]), joined_halves(two, bits[1])], axis=0)


def half_products(pairs, side):
    found = []
    for left, right in pairs:
        size = left.shape[1] // 2
        found.append(mm_tn(lax.dynamic_slice_in_dim(left, side * size, size, axis=1), right))
    return found


def shares(value):
    devices = lax.axis_size("dp")
    groups = [[i for i in range(devices) if i & 5 == low] for low in (0, 1, 4, 5)]
    return lax.psum_scatter(value, "dp", scatter_dimension=0, axis_index_groups=groups, tiled=True)


def from_shares(every):
    devices = lax.axis_size("dp")
    size, width = every.shape[0] // devices, every.shape[1]
    every = every.reshape(devices // 8, 2, 2, 2, size, width)
    return [jnp.transpose(every[:, i], (2, 0, 1, 3, 4)).reshape(-1, width).astype(f32) for i in range(2)]


def all_sum(value, bits):
    for bit in bits:
        value = value + exchanged(value, bit)
    return value


def map_rows(weight):
    return weight.reshape(weight.shape[0], -1).T


def on_device(
    tokens, cotangent, ln_weight, up_inner, up_gate, conv_weight, conv_bias, query_weight, key_weight,
    value_weight, gate_weight, gate_bias, group_weight, skip_weight, down_weight,
):
    count = tokens.shape[0]
    chan = up_inner.shape[1]
    model = up_inner.shape[0]
    half = tokens.shape[1]
    band = query_weight.shape[1]
    span = SEQ_LEN // count
    devices = lax.axis_size("dp")
    stride = devices // span
    t_place = lax.axis_index("tensor")
    piece = lax.axis_index("dp") // stride
    low_half = t_place == 0

    def across(value):
        return lax.ppermute(value, "tensor", [(0, 1), (1, 0)])

    def side_by_side(own, other):
        return jnp.concatenate([jnp.where(low_half, own, other), jnp.where(low_half, other, own)], axis=1)

    def along(value, distance):
        route = [(i - distance, i) for i in range(devices) if 0 <= i - distance < devices]
        return lax.ppermute(value, "dp", route)

    def flags(*values):
        return jnp.stack([jnp.asarray(v).astype(jnp.int32) for v in values])

    halo = along(tokens[count - HALO :], stride)
    other_tokens = across(tokens)
    full = side_by_side(tokens, other_tokens)
    full_cot = side_by_side(cotangent, across(cotangent))

    maps = jnp.stack([map_rows(w) for w in (query_weight, key_weight, value_weight)])
    heads = gate_bias.shape[0] // 2
    local = heads // 2
    order = [kind * heads + t * local + j for t in range(2) for kind in range(2) for j in range(local)]
    gwt = jnp.pad(
        jnp.swapaxes(gate_weight, 1, 2)[:, jnp.array(order)], ((0, 0), (0, LANES - 2 * heads), (0, 0))
    )

    normed, inner, conv, active, q, k, v, pre, coefs = first_stage(
        flags(piece == 0, t_place), tokens, other_tokens, halo, across(halo), ln_weight[None], up_inner,
        conv_weight, conv_bias[None], maps, gate_weight,
    )
    row, col, total = gates_stage(flags(t_place), pre, across(pre), gate_bias[:, None])
    even = flags(piece % 2 == 0)
    packs = ends_stage(even, k, v, col, total)
    gate_in = mm(normed, up_gate)
    dgated = mm_nt(full_cot, down_weight)
    inside, norms = inside_stage(q, k, v, col, row)
    states, done = pass_states(
        packs[:FORTH], packs[FORTH:], piece, span, stride, ((inside, norms), (dgated,), (gate_in,))
    )
    (inside, norms), (dgated,), (gate_in,) = done
    (
        gated, gate_in_grad, sgrad, nlow, clow, start, nvec, stat, ggroup, gskip, *packs
    ) = middle_stage(
        even, states, q, k, v, inside, norms, col, gate_in, dgated, active, group_weight[None],
        skip_weight[None], total,
    )
    pairs = ((gated, full_cot), (normed, gate_in_grad))
    lowest = lax.axis_index("dp") % 2
    sends = [value.astype(bf16) for value in half_products(pairs, 1 - lowest)]
    keeps = [
        value + exchanged(sent, 1).astype(f32) for value, sent in zip(half_products(pairs, lowest), sends)
    ]
    both = jnp.concatenate(keeps, axis=0)
    branch = mm(gated, down_weight)
    second = (lax.axis_index("dp") // 4) % 2
    away = lax.dynamic_slice_in_dim(both, (1 - second) * (model // 2), model // 2, axis=0).astype(bf16)
    states, done = pass_states(
        packs[:BACK], packs[BACK:], span - 1 - piece, span, stride, (sends, (branch,), (both, away)))
    _, (branch,), (both, away) = done
    both = lax.dynamic_slice_in_dim(both, second * (model // 2), model // 2, axis=0)
    both = both + exchanged(away, 4).astype(f32)
    states, both = lax.optimization_barrier((states, both))
    share = shares(both)

    bits = [1 << n for n in range(devices.bit_length() - 1)]
    keep_half = lax.dynamic_slice_in_dim(branch, t_place * half, half, axis=1)
    send_half = lax.dynamic_slice_in_dim(branch, (1 - t_place) * half, half, axis=1)
    result = tokens.astype(f32) + (keep_half + across(send_half))
    squares = jnp.sum(result * result)
    gate_part = mm_nt(gate_in_grad, up_gate)

    qg, kg, vg, pre_own = back_stage(flags(piece % 2 == 0, t_place), states, q, k, v, nlow, clow, start, nvec, col, row, stat)
    pre_other = across(pre_own)
    skip = skip_weight[None]
    edge = along(edge_stage(qg, kg, pre_own, pre_other, sgrad, conv, skip, coefs, gwt), -stride)
    edge, share = lax.optimization_barrier((edge, share.astype(bf16)))
    every = lax.all_gather(share, "dp", axis=0, tiled=True)
    inner_low, small = maps_stage(
        flags(piece == span - 1), qg, kg, vg, pre_own, pre_other, sgrad, conv, inner, q, k, v, edge, skip, conv_weight,
        coefs, gwt, ggroup, gskip,
    )
    grad_up_inner, inner_low = lax.optimization_barrier((mm_tn(normed, inner_low), inner_low))
    late = [halved(grad_up_inner[: model // 2], bits[0]), halved(grad_up_inner[model // 2 :], bits[1])]
    part = gate_part + mm_nt(inner_low, up_inner)
    wide = full.astype(f32)
    centered = wide - jnp.mean(wide, axis=1, keepdims=True)
    inverse = lax.rsqrt(jnp.mean(centered * centered, axis=1, keepdims=True) + NORM_EPS)
    xhat = centered * inverse
    scaled = part * ln_weight
    mean_h = jnp.mean(scaled, axis=1)
    mean_hx = jnp.mean(scaled * xhat, axis=1)
    means = jnp.stack([mean_h, mean_hx])
    late, part, means = lax.optimization_barrier((late, part, means))
    late = [halved(late[0], bits[1]), halved(late[1], bits[0])]
    means = means + across(means)
    own_part = lax.dynamic_slice_in_dim(part, t_place * half, half, axis=1)
    send_part = lax.dynamic_slice_in_dim(part, (1 - t_place) * half, half, axis=1)
    normed_grad = own_part + across(send_part)
    xhat_own = lax.dynamic_slice_in_dim(xhat, t_place * half, half, axis=1)
    ln_own = lax.dynamic_slice_in_dim(ln_weight, t_place * half, half, axis=0)
    token_grad = (
        inverse * (normed_grad * ln_own - means[0][:, None] - xhat_own * means[1][:, None])
        + cotangent.astype(f32)
    )
    grad_ln = jnp.sum(normed_grad * xhat_own, axis=0)

    late, grad_ln, token_grad, every = lax.optimization_barrier((late, grad_ln, token_grad, every))
    last = jnp.concatenate([grad_ln, jnp.broadcast_to(squares + across(squares), (LANES,))])
    small = all_sum(small + jnp.pad(last[None], ((SMALL - 1, 0), (0, chan - half - LANES))), bits)
    grad_ln = small[SMALL - 1, :half]
    late = finished(late, bits)
    early = from_shares(every)
    taps = conv_weight.shape[0]
    folded = small[32 : 32 + 3 * band].reshape(3, band, chan // band, band)
    folded = jnp.transpose(folded, (0, 2, 3, 1))
    back_order = jnp.array([order.index(c) for c in range(2 * heads)])
    gate_rows = jnp.swapaxes(small[8:32].reshape(3, 8, chan)[:, back_order], 1, 2)
    rms = jnp.sqrt(small[SMALL - 1, half : half + 1] / (count * model * devices))
    return (
        result.astype(bf16), token_grad, grad_ln, late.astype(f32), early[1], small[:taps],
        small[taps], folded[0], folded[1], folded[2], gate_rows, small[taps + 1, : 2 * heads][back_order], small[taps + 2],
        small[taps + 3], early[0], rms,
    )


def solution(mesh):
    rows_spec = P("dp", "tensor")
    cols = P(None, "tensor")
    vec = P("tensor")
    blocks = P("tensor", None, None)
    gates = P(None, "tensor", None)
    in_specs = (
        rows_spec, rows_spec, P(), cols, cols, cols, vec, blocks, blocks, blocks, gates, P(), vec, vec,
        P("tensor", None),
    )
    out_specs = (
        rows_spec, rows_spec, vec, cols, cols, cols, vec, blocks, blocks, blocks, gates, P(), vec, vec,
        P("tensor", None), P(),
    )
    return jax.shard_map(on_device, mesh=mesh, in_specs=in_specs, out_specs=out_specs, check_vma=False)
```
